32 devices in a mesh: row: 8 (over z, x), col: 4 (over y, core).
Axes of the slice: x: 2, y: 2, z: 4, core: 2. Of those that a mesh axis runs over, the one named last changes fastest.
Arguments:
- layer_input: bfloat16 [16384, 768], P(('row', 'col')), may hold values from -6 to 6
- attn_gain: float32 [768], replicated, may hold values from 0.5 to 1.5
- attn_shift: float32 [768], replicated, may hold values from -2 to 2
- qkv_weight: bfloat16 [768, 3, 768], P('row', None, 'col'), may hold values from -0.21875 to 0.21875
- qkv_bias: float32 [2, 768], P(None, 'col'), may hold values from -2 to 2
- output_weight: bfloat16 [768, 768], P('row', 'col'), may hold values from -4 to 4
- output_bias: float32 [768], replicated, may hold values from -2 to 2
- mlp_gain: float32 [768], replicated, may hold values from 0.5 to 1.5
- mlp_shift: float32 [768], replicated, may hold values from -2 to 2
- up_weight: bfloat16 [768, 3072], P('row', 'col'), may hold values from -0.21875 to 0.21875
- up_bias: float32 [3072], P('col'), may hold values from -3 to 3
- down_weight: bfloat16 [768, 3072], P('row', 'col'), may hold values from -0.109375 to 0.109375
- down_bias: float32 [768], replicated, may hold values from -2 to 2
- cotangent: bfloat16 [16384, 768], P(('row', 'col')), may hold values from -6 to 6
Outputs:
- layer_output: bfloat16 [16384, 768], P(('row', 'col'))
- input_grad: float32 [16384, 768], P(('row', 'col'))
- attn_gain_grad: float32 [768], replicated
- attn_shift_grad: float32 [768], replicated
- qkv_weight_grad: float32 [768, 3, 768], P('row', None, 'col')
- qkv_bias_grad: float32 [2, 768], P(None, 'col')
- output_weight_grad: float32 [768, 768], P('row', 'col')
- output_bias_grad: float32 [768], replicated
- mlp_gain_grad: float32 [768], replicated
- mlp_shift_grad: float32 [768], replicated
- up_weight_grad: float32 [768, 3072], P('row', 'col')
- up_bias_grad: float32 [3072], P('col')
- down_weight_grad: float32 [768, 3072], P('row', 'col')
- down_bias_grad: float32 [768], replicated
- rms_values: float32 [3], replicated
The draws below stay inside these ranges and needn't reach their ends.
All inputs are finite; a program needn't handle non-finite values.
Results may differ from the reference program's by a relative error of at most 0.013.
Values may be sent and summed in bfloat16 or wider, within the bound.
No kernel may reach another device: no remote copies, remote signals or barrier semaphores. Data moves between devices by JAX's collectives and lax.ppermute only.
A program may use at most 128 MiB of HBM per device.

```python
import jax
import jax.numpy as jnp
from jax import lax

D = 768
HEADS = 12
HEAD_DIM = 64
FF = 3072
SEQ_LEN = 1024
SEQ_DEV = 2
TOKENS = 16384


def steps_of(rng, dims, cuts, smallest, top_value):
    level = 1.0
    for axis_at, blocks in cuts:
        heights = jax.random.uniform(jax.random.fold_in(jax.random.fold_in(rng, 6), axis_at), (blocks,), jnp.float32, smallest / len(cuts), top_value / len(cuts))
        level = level * jnp.repeat(jnp.exp(heights), dims[axis_at] // blocks).reshape((-1,) + (1,) * (len(dims) - 1 - axis_at))
    return level


def noise(stream_key, dims, spread, limit, shards=(), kind=jnp.bfloat16):
    level = steps_of(stream_key, dims, shards, -0.22, 0.18) if shards else 1.0
    values = jax.random.normal(stream_key, dims, jnp.float32) * spread * level
    return jnp.minimum(jnp.maximum(values, -limit), limit).astype(kind)


def setup_inputs(seed: int = 0) -> dict:
    streams_of = jax.random.split(jax.random.key(seed), 15)
    return {
        "layer_input": noise(streams_of[0], (TOKENS, D), 1.0, 6.0, ((0, 32),)),
        "attn_gain": jnp.clip(1.0 + 0.1 * jax.random.normal(streams_of[1], (D,), jnp.float32), 0.5, 1.5),
        "attn_shift": noise(streams_of[2], (D,), 0.3, 2.0, (), jnp.float32),
        "qkv_weight": noise(streams_of[3], (D, 3, D), D ** -0.5, 0.21875, ((0, 8), (2, 4))),
        "qkv_bias": noise(streams_of[4], (2, D), 0.3, 2.0, ((1, 4),), jnp.float32),
        "output_weight": noise(streams_of[5], (D, D), (max(3 * D // SEQ_LEN, 1)) ** -0.5, 4.0, ((0, 8), (1, 4))),
        "output_bias": noise(streams_of[6], (D,), 0.3, 2.0, (), jnp.float32),
        "mlp_gain": jnp.clip(1.0 + 0.1 * jax.random.normal(streams_of[7], (D,), jnp.float32), 0.5, 1.5),
        "mlp_shift": noise(streams_of[8], (D,), 0.3, 2.0, (), jnp.float32),
        "up_weight": noise(streams_of[9], (D, FF), D ** -0.5, 0.21875, ((0, 8), (1, 4))),
        "up_bias": noise(streams_of[10], (FF,), 0.5, 3.0, ((0, 4),), jnp.float32),
        "down_weight": noise(streams_of[11], (D, FF), FF ** -0.5, 0.109375, ((0, 8), (1, 4))),
        "down_bias": noise(streams_of[12], (D,), 0.3, 2.0, (), jnp.float32),
        "cotangent": noise(streams_of[13], (TOKENS, D), 1.0, 6.0, ((0, 32),)),
    }


@jax.custom_vjp
def low(v):
    return lax.optimization_barrier(v.astype(jnp.bfloat16)).astype(jnp.float32)

@jax.custom_vjp
def low_back(v):
    return v

def low_keep(v):
    return (low(v), None)

def low_pass(kept, grad):
    return (grad,)

def back_keep(v):
    return (v, None)

def back_low(kept, grad):
    return (low(grad),)
low.defvjp(low_keep, low_pass)
low_back.defvjp(back_keep, back_low)
EPSILON = 1e-06
HIGH = lax.Precision.HIGHEST

def layer_norm(values, gain, shift):
    row_mean = lax.optimization_barrier(jnp.mean(values, axis=-1, keepdims=True))
    variance = lax.optimization_barrier(jnp.mean(jnp.square(values - row_mean), axis=-1, keepdims=True))
    return (values - row_mean) * lax.rsqrt(variance + EPSILON) * gain + shift

def attend(triple):
    query_rows, key_rows, value_rows = triple
    scores = jnp.einsum('qhd,khd->hqk', query_rows, key_rows, precision=HIGH) * HEAD_DIM ** (-0.5)
    scores = low_back(scores)
    probabilities = jax.nn.softmax(scores, axis=-1)
    return jnp.einsum('hqk,khd->qhd', low(probabilities), value_rows, precision=HIGH)

def layer(params, inputs):
    attn_gain, attn_shift, qkv_weight, qkv_bias, output_weight, output_bias, mlp_gain, mlp_shift, up_weight, up_bias, down_weight, down_bias = params
    rows = inputs.shape[0]
    attn_in = low(layer_norm(inputs, attn_gain, attn_shift))
    projected = jnp.einsum('td,dcf->tcf', attn_in, qkv_weight, precision=HIGH)
    query_rows = low_back(low(projected[:, 0] + qkv_bias[0]))
    key_rows = low_back(low(projected[:, 1]))
    value_rows = low_back(low(projected[:, 2] + qkv_bias[1]))
    shape_heads = (rows // SEQ_LEN, SEQ_LEN, HEADS, HEAD_DIM)
    mixed = lax.map(jax.checkpoint(attend), (query_rows.reshape(shape_heads), key_rows.reshape(shape_heads), value_rows.reshape(shape_heads)))
    mixed = low_back(low(mixed.reshape(rows, D)))
    attn_branch = low_back(jnp.dot(mixed, output_weight.T, precision=HIGH) + output_bias)
    hidden_resid = inputs + attn_branch
    mlp_in = low(layer_norm(hidden_resid, mlp_gain, mlp_shift))
    pre_act = low_back(jnp.dot(mlp_in, up_weight, precision=HIGH) + up_bias)
    activated = low(jax.nn.gelu(pre_act, approximate=True))
    mlp_branch = low_back(jnp.dot(activated, down_weight.T, precision=HIGH) + down_bias)
    result = hidden_resid + mlp_branch
    return (result, (jnp.sum(attn_branch * attn_branch), jnp.sum(mlp_branch * mlp_branch)))

def reference(layer_input, attn_gain, attn_shift, qkv_weight, qkv_bias, output_weight, output_bias, mlp_gain, mlp_shift, up_weight, up_bias, down_weight, down_bias, cotangent):
    params = tuple((item.astype(jnp.float32) for item in (attn_gain, attn_shift, qkv_weight, qkv_bias, output_weight, output_bias, mlp_gain, mlp_shift, up_weight, up_bias, down_weight, down_bias)))
    group_rows = SEQ_DEV * SEQ_LEN
    inputs_grouped = layer_input.astype(jnp.float32).reshape(-1, group_rows, D)
    grads_grouped = cotangent.astype(jnp.float32).reshape(-1, group_rows, D)
    zeros_init = jax.tree.map(jnp.zeros_like, params)

    def scan_step(running, group_pair):
        group_in, group_grad = group_pair
        result, pullback, extras = jax.vjp(layer, params, group_in, has_aux=True)
        param_grads, input_grad = pullback(group_grad)
        running = jax.tree.map(lambda left, right: left + right, running, param_grads)
        sums = jnp.stack([jnp.sum(result * result), extras[0], extras[1]])
        return (running, (result, input_grad, sums))
    totals, (results, input_grads, sums) = lax.scan(scan_step, zeros_init, (inputs_grouped, grads_grouped))
    rms_values = jnp.sqrt(lax.optimization_barrier(jnp.sum(sums, axis=0)) / (TOKENS * D))
    return (results.reshape(TOKENS, D).astype(jnp.bfloat16), input_grads.reshape(TOKENS, D), totals[0], totals[1], totals[2], totals[3], totals[4], totals[5], totals[6], totals[7], totals[8], totals[9], totals[10], totals[11], rms_values)
```

```python
import math

import jax
import jax.numpy as jnp
from jax import lax
from jax.experimental import pallas as pl
from jax.experimental.pallas import tpu as pltpu
from jax.sharding import Mesh, PartitionSpec as P

HEAD_DIM = 64
EPSILON = 1e-06
SWAP = [(0, 1), (1, 0)]
LOG2E = math.log2(math.e)
BF16 = jnp.bfloat16
F32 = jnp.float32


def swap(array, axis):
    return lax.ppermute(array, axis, SWAP)


def dot_nn(left, right):
    return lax.dot_general(left, right, (((1,), (0,)), ((), ())), preferred_element_type=F32)


def dot_nt(left, right):
    return lax.dot_general(left, right, (((1,), (1,)), ((), ())), preferred_element_type=F32)


def dot_tn(left, right):
    return lax.dot_general(left, right, (((0,), (0,)), ((), ())), preferred_element_type=F32)


def xor_exchange(blocks_of, axes):
    got = {}
    count = len(axes)
    sizes = [2] * count
    for bits in range(1, 2**count):
        perm = [(i, i ^ bits) for i in range(math.prod(sizes))]
        got[bits] = lax.ppermute(blocks_of(bits), axes, perm)
    return got


def in_order(own, got, axes):
    parts = [own] + [got[bits] for bits in range(1, 2 ** len(axes))]
    for depth, axis in enumerate(reversed(axes)):
        bit = 2**depth
        flip = lax.axis_index(axis) == 1
        parts = [jnp.where(flip, parts[i ^ bit], parts[i]) for i in range(len(parts))]
    return jnp.stack(parts)


def pair_in_order(own, other, axis, dim):
    flip = lax.axis_index(axis) == 1
    return jnp.stack([jnp.where(flip, other, own), jnp.where(flip, own, other)], axis=dim)


def gather_rows(shard, rows):
    low, high = rows[-1], rows[:-1]
    n, c = shard.shape
    near = high[-2:]
    stack = in_order(shard, xor_exchange(lambda bits: shard, near), near)
    for axis in reversed(high[:-2]):
        other = swap(stack, axis)
        stack = pair_in_order(stack, other, axis, 0).reshape(-1, n, c)
    half = c // 2
    first, second = stack[:, :, :half], stack[:, :, half:]
    first_low, second_y = swap(first, low), swap(second, "y")
    first = pair_in_order(first, first_low, low, 1).reshape(-1, half)
    first_y = swap(first, "y")
    second_low = swap(jnp.stack([second, second_y]), low)
    second_own = pair_in_order(second, second_low[0], low, 1).reshape(-1, half)
    second_other = pair_in_order(second_y, second_low[1], low, 1).reshape(-1, half)
    return (
        jnp.concatenate([first, second_own], axis=1),
        jnp.concatenate([first_y, second_other], axis=1),
    )


def pick(array, axis, dim, other):
    zero = lax.index_in_dim(array, 0, dim, keepdims=False)
    one = lax.index_in_dim(array, 1, dim, keepdims=False)
    flip = lax.axis_index(axis) == (0 if other else 1)
    return jnp.where(flip, one, zero)


def scatter_rows(own, other, rows):
    low, high = rows[-1], rows[:-1]
    near = high[-2:]
    total = 2 ** len(rows)
    n, c = own.shape[0] // total, own.shape[1]
    half = c // 2
    own = own.reshape(total // 2, 2, n, c)
    other = other.reshape(total // 2, 2, n, c)
    a_own, a_other = own[..., :half], other[..., :half]
    b_own, b_other = own[..., half:], other[..., half:]
    a_got = swap(a_other, "y")
    b_send = jnp.stack([pick(b_own, low, 1, True), pick(b_other, low, 1, True)])
    b_got = swap(b_send, low)
    a_sum = a_own.astype(F32) + a_got.astype(F32)
    a_send = pick(a_sum, low, 1, True).astype(BF16)
    b_own = pick(b_own, low, 1, False).astype(F32) + b_got[0].astype(F32)
    b_other = (pick(b_other, low, 1, False).astype(F32) + b_got[1].astype(F32)).astype(BF16)
    a_got = swap(a_send, low)
    b_got = swap(b_other, "y")
    a_sum = pick(a_sum, low, 1, False) + a_got.astype(F32)
    b_sum = b_own + b_got.astype(F32)
    both = jnp.concatenate([a_sum, b_sum], axis=2)
    for axis in high[:-2]:
        both = both.reshape(2, -1, n, c)
        got = swap(pick(both, axis, 0, True).astype(BF16), axis)
        both = pick(both, axis, 0, False) + got.astype(F32)
    low_both = both.astype(BF16)
    place = lax.axis_index(near)
    take = lambda bits: lax.dynamic_index_in_dim(low_both, place ^ bits, 0, keepdims=False)
    got = xor_exchange(take, near)
    out = lax.dynamic_index_in_dim(both, place, 0, keepdims=False)
    for piece in got.values():
        out = out + piece.astype(F32)
    return out


def attend_forward_kernel(
    xa_ref, xb_ref, wa_ref, wb_ref, bias_ref, q_ref, k_ref, v_ref, mixed_ref, lse_ref, vt_ref
):
    step = pl.program_id(0)
    block = mixed_ref.shape[0]
    d = HEAD_DIM

    @pl.when(step == 0)
    def _():
        parts = []
        for kind in range(3):
            parts += [wa_ref[:, kind * d : (kind + 1) * d], wb_ref[:, kind * d : (kind + 1) * d]]
        weight = jnp.concatenate(parts, axis=1)
        rows = xa_ref.shape[0]
        for side, ref in enumerate((xa_ref, xb_ref)):
            proj = (dot_nn(ref[...], weight) + bias_ref[0:1, :]).astype(BF16)
            q_ref[side * rows : (side + 1) * rows, :] = proj[:, : 2 * d]
            k_ref[side * rows : (side + 1) * rows, :] = proj[:, 2 * d : 4 * d]
            v_ref[side * rows : (side + 1) * rows, :] = proj[:, 4 * d :]
        vt = v_ref[...].T
        for head in range(2):
            vt_ref[head, :d, :] = vt[head * d : (head + 1) * d, :]
            vt_ref[head, d:, :] = jnp.ones((vt_ref.shape[1] - d, vt.shape[1]), BF16)

    query = q_ref[pl.ds(pl.multiple_of(step * block, block), block), :]
    lane = lax.broadcasted_iota(jnp.int32, query.shape, 1)
    outs = []
    for head in range(2):
        masked = jnp.where(lane // d == head, query, jnp.zeros_like(query)) * BF16(d**-0.5)
        scores = dot_nt(k_ref[...], masked)
        top = jnp.max(scores, axis=0, keepdims=True)
        weights = jnp.exp2((scores - top) * LOG2E).astype(BF16)
        out = dot_nn(vt_ref[head], weights)
        total = out[d : d + 1, :]
        outs.append(out[:d, :] / total)
        lse_ref[head : head + 1, :] = top + jnp.log(total)
    mixed_ref[...] = jnp.concatenate(outs, axis=0).T.astype(BF16)


def attend_forward(xa, xb, wa, wb, bias):
    seq = xa.shape[0] * 2
    width = xa.shape[1]
    block = 256
    two = 2 * HEAD_DIM
    whole = lambda shape: pl.BlockSpec(shape, lambda i: (0,) * len(shape))
    out = jax.ShapeDtypeStruct((seq, two), BF16)
    return pl.pallas_call(
        attend_forward_kernel,
        grid=(seq // block,),
        in_specs=[
            whole(xa.shape),
            whole(xb.shape),
            whole(wa.shape),
            whole(wb.shape),
            whole(bias.shape),
        ],
        out_specs=[
            whole((seq, two)),
            whole((seq, two)),
            whole((seq, two)),
            pl.BlockSpec((block, two), lambda i: (i, 0)),
            pl.BlockSpec((8, block), lambda i: (0, i)),
        ],
        out_shape=[out, out, out, out, jax.ShapeDtypeStruct((8, seq), F32)],
        scratch_shapes=[pltpu.VMEM((2, HEAD_DIM + 16, seq), BF16)],
        cost_estimate=pl.CostEstimate(
            flops=2 * seq * width * 3 * two + 4 * seq * seq * two * 2,
            bytes_accessed=8 * seq * two * 4,
            transcendentals=2 * seq * seq,
        ),
        name="attend_forward",
    )(xa, xb, wa, wb, bias)


def attend_backward_kernel(
    q_ref, k_ref, v_ref, grad_ref, mixed_ref, lse_ref, dq_ref, dk_ref, dv_ref, kt_ref, dk_acc, dv_acc
):
    step = pl.program_id(0)
    d = HEAD_DIM
    scale = d**-0.5

    @pl.when(step == 0)
    def _():
        kt_ref[...] = k_ref[...].T
        dk_acc[...] = jnp.zeros_like(dk_acc)
        dv_acc[...] = jnp.zeros_like(dv_acc)

    query = q_ref[...]
    grad = grad_ref[...]
    lane = lax.broadcasted_iota(jnp.int32, query.shape, 1)
    dots = (grad.astype(F32) * mixed_ref[...].astype(F32)).T
    dqs = []
    for head in range(2):
        mine = lane // d == head
        query_h = jnp.where(mine, query, jnp.zeros_like(query))
        grad_h = jnp.where(mine, grad, jnp.zeros_like(grad))
        row_dots = jnp.sum(dots[head * d : (head + 1) * d, :], axis=0, keepdims=True)
        log_total = lse_ref[head : head + 1, :] * LOG2E
        scores = dot_nt(k_ref[...], query_h * BF16(scale))
        probs = jnp.exp2(scores * LOG2E - log_total)
        grad_probs = dot_nt(v_ref[...], grad_h)
        grad_scores = (probs * (grad_probs - row_dots)).astype(BF16)
        dv_acc[...] += dot_nn(probs.astype(BF16), grad_h)
        dk_acc[...] += dot_nn(grad_scores, query_h)
        dqs.append(dot_nn(kt_ref[head * d : (head + 1) * d, :], grad_scores) * scale)
    dq_ref[...] = jnp.concatenate(dqs, axis=0).T.astype(BF16)

    @pl.when(step == pl.num_programs(0) - 1)
    def _():
        dk_ref[...] = (dk_acc[...] * scale).astype(BF16)
        dv_ref[...] = dv_acc[...].astype(BF16)


def attend_backward(q, k, v, grad, mixed, lse):
    seq, two = q.shape
    block = 256
    whole = pl.BlockSpec((seq, two), lambda i: (0, 0))
    part = pl.BlockSpec((block, two), lambda i: (i, 0))
    out = jax.ShapeDtypeStruct((seq, two), BF16)
    return pl.pallas_call(
        attend_backward_kernel,
        grid=(seq // block,),
        in_specs=[part, whole, whole, part, part, pl.BlockSpec((8, block), lambda i: (0, i))],
        out_specs=[part, whole, whole],
        out_shape=[out, out, out],
        scratch_shapes=[
            pltpu.VMEM((two, seq), BF16),
            pltpu.VMEM((seq, two), F32),
            pltpu.VMEM((seq, two), F32),
        ],
        cost_estimate=pl.CostEstimate(
            flops=10 * seq * seq * two * 2,
            bytes_accessed=8 * seq * two * 2,
            transcendentals=2 * seq * seq,
        ),
        name="attend_backward",
    )(q, k, v, grad, mixed, lse)


def norm(resid, gain, shift):
    mean = jnp.mean(resid, axis=1, keepdims=True)
    centered = resid - mean
    inverse = lax.rsqrt(jnp.mean(jnp.square(centered), axis=1, keepdims=True) + EPSILON)
    hat = centered * inverse
    return (hat * gain + shift).astype(BF16), hat, inverse


def norm_back(grad, hat, inverse, gain):
    gain_grad = jnp.sum(grad * hat, axis=0)
    shift_grad = jnp.sum(grad, axis=0)
    grad_hat = grad * gain
    first = jnp.mean(grad_hat, axis=1, keepdims=True)
    second = jnp.mean(grad_hat * hat, axis=1, keepdims=True)
    return inverse * (grad_hat - first - hat * second), gain_grad, shift_grad


def gelu_tanh(values):
    return jax.nn.gelu(values, approximate=True)


def from_core_pair(own, other):
    return own + swap(other.astype(BF16), "core").astype(F32)


def make_local(rows):
    def local(
        layer_input,
        attn_gain,
        attn_shift,
        qkv_weight,
        qkv_bias,
        output_weight,
        output_bias,
        mlp_gain,
        mlp_shift,
        up_weight,
        up_bias,
        down_weight,
        down_bias,
        cotangent,
    ):
        tokens, width = layer_input.shape
        shard_rows, _, shard_cols = qkv_weight.shape
        heads = shard_cols // HEAD_DIM
        ff = up_weight.shape[1]
        d = HEAD_DIM
        y = lax.axis_index("y")

        bias_pack = jnp.concatenate([qkv_bias.reshape(-1), up_bias])
        bias_other = swap(bias_pack, "y")
        qkv_bias_other = bias_other[: 2 * shard_cols].reshape(2, shard_cols)
        up_bias_other = bias_other[2 * shard_cols :]

        residual = layer_input.astype(F32)
        attn_in, attn_hat, attn_inverse = norm(residual, attn_gain, attn_shift)
        attn_in_other = swap(attn_in, "core")
        attn_all = jnp.concatenate([attn_in, attn_in_other])

        def chunk_shard(h):
            cols = slice(h * d, (h + 1) * d)
            return jnp.concatenate(
                [qkv_weight[:, k, cols] for k in range(3)] + [output_weight[:, cols]], axis=1
            )

        chunks = [gather_rows(chunk_shard(h), rows) for h in range(heads)]
        up_own, up_other = gather_rows(up_weight, rows)
        down_own, down_other = gather_rows(down_weight, rows)
        cot_other = swap(cotangent, "core")
        grad_mlp = jnp.concatenate([cotangent, cot_other])

        attended = []
        zeros = jnp.zeros((d,), F32)
        for h in range(heads):
            cols = slice(h * d, (h + 1) * d)
            bias = jnp.concatenate(
                [
                    qkv_bias[0, cols],
                    qkv_bias_other[0, cols],
                    zeros,
                    zeros,
                    qkv_bias[1, cols],
                    qkv_bias_other[1, cols],
                ]
            )
            bias = jnp.broadcast_to(bias, (8, 6 * d))
            attended.append(attend_forward(attn_in, attn_in_other, *chunks[h], bias))
        mixed = jnp.concatenate([a[3] for a in attended], axis=1)
        out_pairs = [jnp.concatenate([a[:, 3 * d :], b[:, 3 * d :]], axis=1) for a, b in chunks]
        out_full = jnp.concatenate(out_pairs, axis=1)
        branch = dot_nt(mixed, out_full)
        attn_branch = from_core_pair(branch[:tokens], branch[tokens:]) + output_bias
        hidden_resid = residual + attn_branch
        mlp_in, mlp_hat, mlp_inverse = norm(hidden_resid, mlp_gain, mlp_shift)
        mlp_all = jnp.concatenate([mlp_in, swap(mlp_in, "core")])

        acts, slopes = [], []
        for weight, bias in ((up_own, up_bias), (up_other, up_bias_other)):
            pre = dot_nn(mlp_all, weight) + bias
            act, pull = jax.vjp(gelu_tanh, pre)
            acts.append(act.astype(BF16))
            slopes.append(pull(jnp.ones_like(pre))[0].astype(BF16))
        down_grads = [dot_tn(grad_mlp, act).astype(BF16) for act in acts]
        down_grad = scatter_rows(*down_grads, rows)
        branch = dot_nt(acts[0], down_own) + dot_nt(acts[1], down_other)
        mlp_branch = from_core_pair(branch[:tokens], branch[tokens:]) + down_bias
        result = hidden_resid + mlp_branch

        grad_out = cotangent.astype(F32)
        down_bias_grad = jnp.sum(grad_out, axis=0)
        pres = [
            (dot_nn(grad_mlp, w) * slope.astype(F32)).astype(BF16)
            for w, slope in ((down_own, slopes[0]), (down_other, slopes[1]))
        ]
        up_bias_grads = [jnp.sum(p.astype(F32), axis=0) for p in pres]
        up_grads = [dot_tn(mlp_all, p).astype(BF16) for p in pres]
        up_grad = scatter_rows(*up_grads, rows)
        back = dot_nt(pres[0], up_own) + dot_nt(pres[1], up_other)
        grad_mlp_in = from_core_pair(back[:tokens], back[tokens:])
        norm_grad, mlp_gain_grad, mlp_shift_grad = norm_back(
            grad_mlp_in, mlp_hat, mlp_inverse, mlp_gain
        )
        hidden_grad = grad_out + norm_grad
        grad_attn = hidden_grad.astype(BF16)
        output_bias_grad = jnp.sum(grad_attn.astype(F32), axis=0)
        grad_attn_all = jnp.concatenate([grad_attn, swap(grad_attn, "core")])
        output_grad = dot_tn(grad_attn_all, mixed).astype(BF16)
        grad_mixed = dot_nn(grad_attn_all, out_full).astype(BF16)

        back = 0.0
        attn_grads = []
        bias_grads = []
        for h in range(heads):
            q, k, v, mix, lse = attended[h]
            dq, dk, dv = attend_backward(
                q, k, v, grad_mixed[:, 2 * d * h : 2 * d * (h + 1)], mix, lse
            )
            bias_grads.append((jnp.sum(dq.astype(F32), axis=0), jnp.sum(dv.astype(F32), axis=0)))
            sides = []
            for side in range(2):
                cols = slice(side * d, (side + 1) * d)
                grad_proj = jnp.concatenate([dq[:, cols], dk[:, cols], dv[:, cols]], axis=1)
                back = back + dot_nt(grad_proj, chunks[h][side][:, : 3 * d])
                weight_grad = dot_tn(attn_all, grad_proj).astype(BF16)
                at = 2 * d * h + side * d
                sides.append(
                    jnp.concatenate([weight_grad, output_grad[:, at : at + d]], axis=1)
                )
            attn_grads.append(scatter_rows(*sides, rows))
        grad_attn_in = from_core_pair(back[:tokens], back[tokens:])
        norm_grad, attn_gain_grad, attn_shift_grad = norm_back(
            grad_attn_in, attn_hat, attn_inverse, attn_gain
        )
        input_grad = hidden_grad + norm_grad

        qkv_grad = jnp.stack(
            [
                jnp.concatenate([g[:, k * d : (k + 1) * d] for g in attn_grads], axis=1)
                for k in range(3)
            ],
            axis=1,
        )
        output_grad = jnp.concatenate([g[:, 3 * d :] for g in attn_grads], axis=1)

        squares = jnp.stack(
            [
                jnp.sum(result * result),
                jnp.sum(attn_branch * attn_branch),
                jnp.sum(mlp_branch * mlp_branch),
            ]
        )
        common = jnp.concatenate(
            [
                attn_gain_grad,
                attn_shift_grad,
                output_bias_grad,
                mlp_gain_grad,
                mlp_shift_grad,
                down_bias_grad,
                jnp.pad(squares, (0, 125)),
            ]
        )
        common = common + swap(common, "core")
        own = jnp.concatenate(
            [b[i][:d] for i in range(2) for b in bias_grads] + [up_bias_grads[0]]
        )
        other = jnp.concatenate(
            [b[i][d:] for i in range(2) for b in bias_grads] + [up_bias_grads[1]]
        )
        sums = jnp.concatenate([common, own])
        got = swap(jnp.concatenate([common, other]), "y")
        sums = sums + got
        for axis in reversed(rows):
            sums = sums + swap(sums, axis)
        entry_count = tokens * 2 ** (len(rows) + 2) * width
        vec = [sums[i * width : (i + 1) * width] for i in range(6)]
        rms_values = jnp.sqrt(sums[6 * width : 6 * width + 3] / entry_count)
        tail = sums[6 * width + 128 :]
        qkv_bias_grad = tail[: 2 * shard_cols].reshape(2, shard_cols)
        up_bias_grad = tail[2 * shard_cols :]
        return (
            result.astype(BF16),
            input_grad,
            vec[0],
            vec[1],
            qkv_grad,
            qkv_bias_grad,
            output_grad,
            vec[2],
            vec[3],
            vec[4],
            up_grad,
            up_bias_grad,
            down_grad,
            vec[5],
            rms_values,
        )

    return local


def solution(mesh):
    row_size, col_size = mesh.shape["row"], mesh.shape["col"]
    bits = row_size.bit_length() - 1
    rows = tuple(f"r{b}" for b in reversed(range(bits)))
    cube = Mesh(mesh.devices.reshape((2,) * bits + (col_size // 2, 2)), rows + ("y", "core"))
    col = ("y", "core")
    every = rows + col
    placed = (
        P(every, None),
        P(),
        P(),
        P(rows, None, col),
        P(None, col),
        P(rows, col),
        P(),
        P(),
        P(),
        P(rows, col),
        P(col),
        P(rows, col),
        P(),
        P(every, None),
    )
    return jax.shard_map(
        make_local(rows),
        mesh=cube,
        in_specs=placed,
        out_specs=(
            P(every, None),
            P(every, None),
            P(),
            P(),
            P(rows, None, col),
            P(None, col),
            P(rows, col),
            P(),
            P(),
            P(),
            P(rows, col),
            P(col),
            P(rows, col),
            P(),
            P(),
        ),
        check_vma=False,
    )
```

```python
import math
from functools import partial

import jax
import jax.numpy as jnp
from jax import lax
from jax.experimental import pallas as pl
from jax.experimental.pallas import tpu as pltpu
from jax.sharding import Mesh, PartitionSpec as P

HEAD_DIM = 64
EPSILON = 1e-06
SWAP = [(0, 1), (1, 0)]
LOG2E = math.log2(math.e)
BF16 = jnp.bfloat16
F32 = jnp.float32


def swap(array, axis):
    return lax.ppermute(array, axis, SWAP)


def dot_nn(left, right):
    return lax.dot_general(left, right, (((1,), (0,)), ((), ())), preferred_element_type=F32)


def dot_nt(left, right):
    return lax.dot_general(left, right, (((1,), (1,)), ((), ())), preferred_element_type=F32)


def dot_tn(left, right):
    return lax.dot_general(left, right, (((0,), (0,)), ((), ())), preferred_element_type=F32)


def xor_exchange(blocks_of, axes):
    got = {}
    count = len(axes)
    sizes = [2] * count
    for bits in range(1, 2**count):
        perm = [(i, i ^ bits) for i in range(math.prod(sizes))]
        got[bits] = lax.ppermute(blocks_of(bits), axes, perm)
    return got


def in_order(own, got, axes):
    parts = [own] + [got[bits] for bits in range(1, 2 ** len(axes))]
    for depth, axis in enumerate(reversed(axes)):
        bit = 2**depth
        flip = lax.axis_index(axis) == 1
        parts = [jnp.where(flip, parts[i ^ bit], parts[i]) for i in range(len(parts))]
    return jnp.stack(parts)


def pair_in_order(own, other, axis, dim):
    flip = lax.axis_index(axis) == 1
    return jnp.stack([jnp.where(flip, other, own), jnp.where(flip, own, other)], axis=dim)


def gather_rows(shard, rows):
    low, high = rows[-1], rows[:-1]
    n, c = shard.shape
    near = high[-2:]
    stack = in_order(shard, xor_exchange(lambda bits: shard, near), near)
    for axis in reversed(high[:-2]):
        other = swap(stack, axis)
        stack = pair_in_order(stack, other, axis, 0).reshape(-1, n, c)
    half = c // 2
    first, second = stack[:, :, :half], stack[:, :, half:]
    first_low, second_y = swap(first, low), swap(second, "y")
    first = pair_in_order(first, first_low, low, 1).reshape(-1, half)
    first_y = swap(first, "y")
    second_low = swap(jnp.stack([second, second_y]), low)
    second_own = pair_in_order(second, second_low[0], low, 1).reshape(-1, half)
    second_other = pair_in_order(second_y, second_low[1], low, 1).reshape(-1, half)
    return (
        jnp.concatenate([first, second_own], axis=1),
        jnp.concatenate([first_y, second_other], axis=1),
    )


def pick(array, axis, dim, other):
    zero = lax.index_in_dim(array, 0, dim, keepdims=False)
    one = lax.index_in_dim(array, 1, dim, keepdims=False)
    flip = lax.axis_index(axis) == (0 if other else 1)
    return jnp.where(flip, one, zero)


def scatter_rows(own, other, rows):
    low, high = rows[-1], rows[:-1]
    near = high[-2:]
    total = 2 ** len(rows)
    n, c = own.shape[0] // total, own.shape[1]
    half = c // 2
    own = own.reshape(total // 2, 2, n, c)
    other = other.reshape(total // 2, 2, n, c)
    a_own, a_other = own[..., :half], other[..., :half]
    b_own, b_other = own[..., half:], other[..., half:]
    a_got = swap(a_other, "y")
    b_send = jnp.stack([pick(b_own, low, 1, True), pick(b_other, low, 1, True)])
    b_got = swap(b_send, low)
    a_sum = a_own.astype(F32) + a_got.astype(F32)
    a_send = pick(a_sum, low, 1, True).astype(BF16)
    b_own = pick(b_own, low, 1, False).astype(F32) + b_got[0].astype(F32)
    b_other = (pick(b_other, low, 1, False).astype(F32) + b_got[1].astype(F32)).astype(BF16)
    a_got = swap(a_send, low)
    b_got = swap(b_other, "y")
    a_sum = pick(a_sum, low, 1, False) + a_got.astype(F32)
    b_sum = b_own + b_got.astype(F32)
    both = jnp.concatenate([a_sum, b_sum], axis=2)
    for axis in high[:-2]:
        both = both.reshape(2, -1, n, c)
        got = swap(pick(both, axis, 0, True).astype(BF16), axis)
        both = pick(both, axis, 0, False) + got.astype(F32)
    low_both = both.astype(BF16)
    place = lax.axis_index(near)
    take = lambda bits: lax.dynamic_index_in_dim(low_both, place ^ bits, 0, keepdims=False)
    got = xor_exchange(take, near)
    out = lax.dynamic_index_in_dim(both, place, 0, keepdims=False)
    for piece in got.values():
        out = out + piece.astype(F32)
    return out


def gather_near(shard, near):
    got = xor_exchange(lambda bits: shard, near)
    return jnp.stack([shard] + [got[bits] for bits in range(1, 2 ** len(near))])


def gather_far(stack, low):
    half = stack.shape[0] // 2
    from_low = swap(stack, low)
    from_y = swap(stack, "y")
    corner_a = swap(from_low[:half], "y")
    corner_b = swap(from_y[half:], low)
    return stack, from_low, from_y, corner_a, corner_b


def assemble_kernel(rows, xor, s_ref, x_ref, y_ref, a_ref, b_ref, out_ref, sems):
    count, n, c = s_ref.shape
    x = lax.axis_index(rows[-1])
    z = lax.axis_index(rows[:-1])
    half = count // 2
    copies = []
    for k in range(count):
        corner = a_ref.at[k] if k < half else b_ref.at[k - half]
        at = lax.bitwise_xor(z, k) if xor else k
        sources = ((s_ref.at[k], 0, 0), (x_ref.at[k], 1, 0), (y_ref.at[k], 0, 1), (corner, 1, 1))
        for source, flip, side in sources:
            row = pl.multiple_of((at * 2 + lax.bitwise_xor(x, flip)) * n, n)
            target = out_ref.at[pl.ds(row, n), pl.ds(side * c, c)]
            copies.append(pltpu.make_async_copy(source, target, sems.at[len(copies)]))
    for copy in copies:
        copy.start()
    for copy in copies:
        copy.wait()


def assemble(pieces, rows, xor):
    count, n, c = pieces[0].shape
    anywhere = pl.BlockSpec(memory_space=pl.ANY)
    return pl.pallas_call(
        partial(assemble_kernel, rows, xor),
        in_specs=[anywhere] * 5,
        out_specs=anywhere,
        out_shape=jax.ShapeDtypeStruct((count * 2 * n, 2 * c), BF16),
        scratch_shapes=[pltpu.SemaphoreType.DMA((4 * count,))],
        cost_estimate=pl.CostEstimate(
            flops=0, bytes_accessed=16 * count * n * c * 2, transcendentals=0
        ),
        name="assemble",
    )(*pieces)


def reduce_far(parts, low):
    own, to_low, to_y, corner_a, corner_b = parts
    half = own.shape[0] // 2
    got_a = swap(corner_a, "y")
    got_b = swap(corner_b, low)
    add = lambda a, b: (a.astype(F32) + b.astype(F32)).astype(BF16)
    to_low = jnp.concatenate([add(to_low[:half], got_a), to_low[half:]])
    to_y = jnp.concatenate([to_y[:half], add(to_y[half:], got_b)])
    got_low = swap(to_low, low)
    got_y = swap(to_y, "y")
    total = own.astype(F32) + got_low.astype(F32) + got_y.astype(F32)
    return total.astype(BF16)


def reduce_near(stack, near):
    n, c = stack.shape[1:]
    return lax.psum_scatter(stack.reshape(-1, c), near, scatter_dimension=0, tiled=True)


def turn(rows, n, left_refs, turned_ref):
    at = 0
    for ref in left_refs:
        tokens = ref.shape[0]
        turned = ref[...].T
        if rows is None:
            turned_ref[:, at : at + tokens] = turned
            at += tokens
            continue
        count = turned.shape[0] // n // 2
        for block in range(2 * count):
            z, x = divmod(block, 2)
            slot = lax.bitwise_xor(lax.axis_index(rows[-1]), x) * count + z
            turned_ref[pl.ds(pl.multiple_of(slot * n, n), n), at : at + tokens] = turned[
                block * n : (block + 1) * n, :
            ]
        at += tokens


def store_grads(own, other, refs, cols):
    s_ref, x_ref, y_ref, a_ref, b_ref = refs
    half = own.shape[0] // 2
    quarter = half // 2
    s_ref[:, cols] = own[:half].astype(BF16)
    x_ref[:, cols] = own[half:].astype(BF16)
    y_ref[:, cols] = other[:half].astype(BF16)
    a_ref[:, cols] = other[half : half + quarter].astype(BF16)
    b_ref[:, cols] = other[half + quarter :].astype(BF16)


def grad_shapes(width, c):
    return [
        jax.ShapeDtypeStruct((width // 2, c), BF16),
        jax.ShapeDtypeStruct((width // 2, c), BF16),
        jax.ShapeDtypeStruct((width // 2, c), BF16),
        jax.ShapeDtypeStruct((width // 4, c), BF16),
        jax.ShapeDtypeStruct((width // 4, c), BF16),
    ]


def whole(shape):
    return pl.BlockSpec(shape, lambda *_: (0,) * len(shape))


def attend_forward_kernel(
    xa_ref, xb_ref, w_ref, bias_ref, q_ref, k_ref, v_ref, mixed_ref, lse_ref, wcat_ref, vt_ref
):
    pair, step = pl.program_id(0), pl.program_id(1)
    block = mixed_ref.shape[0]
    d = HEAD_DIM
    pairs = q_ref.shape[0]
    side = pairs * d

    @pl.when((pair == 0) & (step == 0))
    def _():
        tokens = xa_ref.shape[0]
        for kind in range(4):
            weight = jnp.concatenate(
                [
                    w_ref[:, kind * side : (kind + 1) * side],
                    w_ref[:, (4 + kind) * side : (5 + kind) * side],
                ],
                axis=1,
            )
            wcat_ref[:, kind * 2 * side : (kind + 1) * 2 * side] = weight
            if kind == 3:
                break
            target = (q_ref, k_ref, v_ref)[kind]
            for half, ref in enumerate((xa_ref, xb_ref)):
                proj = (dot_nn(ref[...], weight) + bias_ref[kind : kind + 1, :]).astype(BF16)
                for p in range(pairs):
                    target[p, half * tokens : (half + 1) * tokens, :] = proj[
                        :, p * 2 * d : (p + 1) * 2 * d
                    ]

    @pl.when(step == 0)
    def _():
        vt = v_ref[pair].T
        for head in range(2):
            vt_ref[head, :d, :] = vt[head * d : (head + 1) * d, :]
            vt_ref[head, d:, :] = jnp.ones((vt_ref.shape[1] - d, vt.shape[1]), BF16)

    query = q_ref[pair, pl.ds(pl.multiple_of(step * block, block), block), :]
    lane = lax.broadcasted_iota(jnp.int32, query.shape, 1)
    outs = []
    for head in range(2):
        masked = jnp.where(lane // d == head, query, jnp.zeros_like(query)) * BF16(d**-0.5)
        scores = dot_nt(k_ref[pair], masked)
        top = jnp.max(scores, axis=0, keepdims=True)
        weights = jnp.exp2((scores - top) * LOG2E).astype(BF16)
        out = dot_nn(vt_ref[head], weights)
        total = out[d : d + 1, :]
        outs.append(out[:d, :] * (1.0 / total))
        lse_ref[0, head : head + 1, :] = top + jnp.log(total)
    mixed_ref[...] = jnp.concatenate(outs, axis=0).T.astype(BF16)


def attend_forward(xa, xb, weight, bias):
    seq = xa.shape[0] * 2
    width = xa.shape[1]
    block = 256
    two = 2 * HEAD_DIM
    pairs = weight.shape[1] // (4 * two)
    out = jax.ShapeDtypeStruct((pairs, seq, two), BF16)
    return pl.pallas_call(
        attend_forward_kernel,
        grid=(pairs, seq // block),
        in_specs=[whole(xa.shape), whole(xb.shape), whole(weight.shape), whole(bias.shape)],
        out_specs=[
            whole(out.shape),
            whole(out.shape),
            whole(out.shape),
            pl.BlockSpec((block, two), lambda p, i: (i, p)),
            pl.BlockSpec((1, 8, block), lambda p, i: (p, 0, i)),
            whole(weight.shape),
        ],
        out_shape=[
            out,
            out,
            out,
            jax.ShapeDtypeStruct((seq, pairs * two), BF16),
            jax.ShapeDtypeStruct((pairs, 8, seq), F32),
            jax.ShapeDtypeStruct(weight.shape, BF16),
        ],
        scratch_shapes=[pltpu.VMEM((2, HEAD_DIM + 16, seq), BF16)],
        cost_estimate=pl.CostEstimate(
            flops=pairs * 24 * seq * seq * two,
            bytes_accessed=16 * seq * width,
            transcendentals=pairs * 2 * seq * seq,
        ),
        name="attend_forward",
    )(xa, xb, weight, bias)


def attend_backward_kernel(
    q_ref, k_ref, v_ref, grad_ref, mixed_ref, lse_ref, dproj_ref, kt_ref, dk_acc, dv_acc
):
    pair, step = pl.program_id(0), pl.program_id(1)
    block = q_ref.shape[1]
    d = HEAD_DIM
    two = 2 * d
    scale = d**-0.5
    span = dproj_ref.shape[1] // 3

    @pl.when(step == 0)
    def _():
        kt_ref[...] = k_ref[0].T
        dk_acc[...] = jnp.zeros_like(dk_acc)
        dv_acc[...] = jnp.zeros_like(dv_acc)

    query = q_ref[0]
    grad = grad_ref[...]
    lane = lax.broadcasted_iota(jnp.int32, query.shape, 1)
    dots = (grad.astype(F32) * mixed_ref[...].astype(F32)).T
    dqs = []
    for head in range(2):
        mine = lane // d == head
        query_h = jnp.where(mine, query, jnp.zeros_like(query))
        grad_h = jnp.where(mine, grad, jnp.zeros_like(grad))
        row_dots = jnp.sum(dots[head * d : (head + 1) * d, :], axis=0, keepdims=True)
        log_total = lse_ref[0, head : head + 1, :] * LOG2E
        scores = dot_nt(k_ref[0], query_h * BF16(scale))
        probs = jnp.exp2(scores * LOG2E - log_total)
        grad_probs = dot_nt(v_ref[0], grad_h)
        grad_scores = (probs * (grad_probs - row_dots)).astype(BF16)
        dv_acc[...] += dot_nn(probs.astype(BF16), grad_h)
        dk_acc[...] += dot_nn(grad_scores, query_h)
        dqs.append(dot_nn(kt_ref[head * d : (head + 1) * d, :], grad_scores) * scale)
    rows = pl.ds(pl.multiple_of(step * block, block), block)
    col = pl.multiple_of(pair * two, two)
    dproj_ref[rows, pl.ds(col, two)] = jnp.concatenate(dqs, axis=0).T.astype(BF16)

    @pl.when(step == pl.num_programs(1) - 1)
    def _():
        dproj_ref[:, pl.ds(span + col, two)] = (dk_acc[...] * scale).astype(BF16)
        dproj_ref[:, pl.ds(2 * span + col, two)] = dv_acc[...].astype(BF16)


def attend_backward(q, k, v, grad, mixed, lse):
    pairs, seq, two = q.shape
    block = 256
    full = pl.BlockSpec((1, seq, two), lambda p, i: (p, 0, 0))
    part = pl.BlockSpec((block, two), lambda p, i: (i, p))
    return pl.pallas_call(
        attend_backward_kernel,
        grid=(pairs, seq // block),
        in_specs=[
            pl.BlockSpec((1, block, two), lambda p, i: (p, i, 0)),
            full,
            full,
            part,
            part,
            pl.BlockSpec((1, 8, block), lambda p, i: (p, 0, i)),
        ],
        out_specs=whole((seq, 3 * pairs * two)),
        out_shape=jax.ShapeDtypeStruct((seq, 3 * pairs * two), BF16),
        scratch_shapes=[
            pltpu.VMEM((two, seq), BF16),
            pltpu.VMEM((seq, two), F32),
            pltpu.VMEM((seq, two), F32),
        ],
        cost_estimate=pl.CostEstimate(
            flops=pairs * 50 * seq * seq * two,
            bytes_accessed=pairs * 20 * seq * two,
            transcendentals=pairs * 2 * seq * seq,
        ),
        name="attend_backward",
    )(q, k, v, grad, mixed, lse)


def attention_grads_kernel(
    rows, n, xa_ref, xb_ref, ga_ref, gb_ref, dproj_ref, mixed_ref, s_ref, x_ref, y_ref, a_ref, b_ref,
    turned_ref,
):
    refs = (s_ref, x_ref, y_ref, a_ref, b_ref)
    side = mixed_ref.shape[1] // 2
    turn(rows, n, (xa_ref, xb_ref), turned_ref)
    for kind in range(3):
        both = dproj_ref[:, kind * 2 * side : (kind + 1) * 2 * side]
        grads = dot_nn(turned_ref[...], both)
        store_grads(
            grads[:, :side], grads[:, side:], refs, slice(kind * side, (kind + 1) * side)
        )
    turn(rows, n, (ga_ref, gb_ref), turned_ref)
    grads = dot_nn(turned_ref[...], mixed_ref[...])
    store_grads(grads[:, :side], grads[:, side:], refs, slice(3 * side, 4 * side))


def attention_grads(xa, xb, ga, gb, dproj, mixed, rows, n):
    tokens, width = xa.shape
    c = 2 * mixed.shape[1]
    return pl.pallas_call(
        partial(attention_grads_kernel, rows, n),
        out_shape=grad_shapes(width, c),
        scratch_shapes=[pltpu.VMEM((width, 2 * tokens), BF16)],
        cost_estimate=pl.CostEstimate(
            flops=4 * tokens * width * 2 * c, bytes_accessed=8 * width * c, transcendentals=0
        ),
        name="attention_grads",
    )(xa, xb, ga, gb, dproj, mixed)


def gelu_parts(u):
    c0 = math.sqrt(2.0 / math.pi)
    square = u * u
    t = jnp.tanh(u * (c0 + (c0 * 0.044715) * square))
    half = 0.5 * u
    act = half + half * t
    slope = 0.5 + 0.5 * t + half * (1.0 - t * t) * (c0 + (3.0 * c0 * 0.044715) * square)
    return act, slope


def up_kernel(
    rows, n, xa_ref, xb_ref, ga_ref, gb_ref, w_ref, wo_ref, bias_ref, bias_o_ref,
    act_ref, slope_ref, act_o_ref, slope_o_ref, s_ref, x_ref, y_ref, a_ref, b_ref, turned_ref,
):
    @pl.when(pl.program_id(0) == 0)
    def _():
        turn(rows, n, (ga_ref, gb_ref), turned_ref)

    tokens = xa_ref.shape[0]
    grads = []
    for weight, bias, acts, slopes in (
        (w_ref, bias_ref, act_ref, slope_ref),
        (wo_ref, bias_o_ref, act_o_ref, slope_o_ref),
    ):
        for half, ref in enumerate((xa_ref, xb_ref)):
            act, slope = gelu_parts(dot_nn(ref[...], weight[...]) + bias[0:1, :])
            acts[half * tokens : (half + 1) * tokens, :] = act.astype(BF16)
            slopes[half * tokens : (half + 1) * tokens, :] = slope.astype(BF16)
        grads.append(dot_nn(turned_ref[...], acts[...]))
    store_grads(*grads, (s_ref, x_ref, y_ref, a_ref, b_ref), slice(None))


def up_and_down_grads(xa, xb, ga, gb, weight, bias, bias_o, rows, n):
    tokens, width = xa.shape
    c = weight.shape[1] // 2
    tile = 256
    steps = c // tile
    hidden = jax.ShapeDtypeStruct((2 * tokens, c), BF16)
    cols = lambda r: pl.BlockSpec((r, tile), lambda j: (0, j))
    return pl.pallas_call(
        partial(up_kernel, rows, n),
        grid=(steps,),
        in_specs=[whole(xa.shape)] * 4
        + [
            cols(width),
            pl.BlockSpec((width, tile), lambda j: (0, j + steps)),
            cols(8),
            cols(8),
        ],
        out_specs=[cols(2 * tokens)] * 4 + [cols(s.shape[0]) for s in grad_shapes(width, c)],
        out_shape=[hidden] * 4 + grad_shapes(width, c),
        scratch_shapes=[pltpu.VMEM((width, 2 * tokens), BF16)],
        cost_estimate=pl.CostEstimate(
            flops=16 * tokens * width * c,
            bytes_accessed=24 * tokens * c,
            transcendentals=4 * tokens * c,
        ),
        name="up_and_down_grads",
    )(xa, xb, ga, gb, weight, weight, bias, bias_o)


def hidden_back_kernel(
    ga_ref, gb_ref, w_ref, wo_ref, u_ref, uo_ref, slope_ref, slope_o_ref,
    pre_ref, pre_o_ref, sum_ref, own_ref, other_ref, acc_ref,
):
    step = pl.program_id(0)
    tokens = ga_ref.shape[0]

    @pl.when(step == 0)
    def _():
        acc_ref[...] = jnp.zeros_like(acc_ref)

    for side, (weight, up, slopes, pres) in enumerate(
        ((w_ref, u_ref, slope_ref, pre_ref), (wo_ref, uo_ref, slope_o_ref, pre_o_ref))
    ):
        totals = 0.0
        for half, ref in enumerate((ga_ref, gb_ref)):
            at = slice(half * tokens, (half + 1) * tokens)
            back = dot_nn(ref[...], weight[...]) * slopes[at, :].astype(F32)
            pre = back.astype(BF16)
            pres[at, :] = pre
            totals = totals + jnp.sum(pre.astype(F32), axis=0, keepdims=True)
            acc_ref[at, :] += dot_nt(pre, up[...])
        sum_ref[side : side + 1, :] = totals

    @pl.when(step == pl.num_programs(0) - 1)
    def _():
        own_ref[...] = acc_ref[:tokens, :]
        other_ref[...] = acc_ref[tokens:, :].astype(BF16)


def hidden_back(ga, gb, down, up, slope, slope_o):
    tokens, width = ga.shape
    c = down.shape[1] // 2
    tile = 256
    steps = c // tile
    cols = lambda r: pl.BlockSpec((r, tile), lambda j: (0, j))
    far = lambda r: pl.BlockSpec((r, tile), lambda j: (0, j + steps))
    hidden = jax.ShapeDtypeStruct((2 * tokens, c), BF16)
    return pl.pallas_call(
        hidden_back_kernel,
        grid=(steps,),
        in_specs=[
            whole(ga.shape),
            whole(ga.shape),
            cols(width),
            far(width),
            cols(width),
            far(width),
            cols(2 * tokens),
            cols(2 * tokens),
        ],
        out_specs=[
            cols(2 * tokens),
            cols(2 * tokens),
            cols(8),
            whole(ga.shape),
            whole(ga.shape),
        ],
        out_shape=[
            hidden,
            hidden,
            jax.ShapeDtypeStruct((8, c), F32),
            jax.ShapeDtypeStruct(ga.shape, F32),
            jax.ShapeDtypeStruct(ga.shape, BF16),
        ],
        scratch_shapes=[pltpu.VMEM((2 * tokens, width), F32)],
        cost_estimate=pl.CostEstimate(
            flops=16 * tokens * width * c, bytes_accessed=24 * tokens * c, transcendentals=0
        ),
        name="hidden_back",
    )(ga, gb, down, down, up, up, slope, slope_o)


def weight_grads_kernel(
    rows, n, xa_ref, xb_ref, g_ref, go_ref, s_ref, x_ref, y_ref, a_ref, b_ref, turned_ref
):
    @pl.when(pl.program_id(0) == 0)
    def _():
        turn(rows, n, (xa_ref, xb_ref), turned_ref)

    own = dot_nn(turned_ref[...], g_ref[...])
    other = dot_nn(turned_ref[...], go_ref[...])
    store_grads(own, other, (s_ref, x_ref, y_ref, a_ref, b_ref), slice(None))


def weight_grads(xa, xb, grad, grad_o, rows, n):
    tokens, width = xa.shape
    c = grad.shape[1]
    tile = 256
    cols = lambda r: pl.BlockSpec((r, tile), lambda j: (0, j))
    return pl.pallas_call(
        partial(weight_grads_kernel, rows, n),
        grid=(c // tile,),
        in_specs=[whole(xa.shape), whole(xa.shape), cols(2 * tokens), cols(2 * tokens)],
        out_specs=[cols(s.shape[0]) for s in grad_shapes(width, c)],
        out_shape=grad_shapes(width, c),
        scratch_shapes=[pltpu.VMEM((width, 2 * tokens), BF16)],
        cost_estimate=pl.CostEstimate(
            flops=8 * tokens * width * c, bytes_accessed=12 * tokens * c, transcendentals=0
        ),
        name="weight_grads",
    )(xa, xb, grad, grad_o)


def norm(resid, gain, shift):
    mean = jnp.mean(resid, axis=1, keepdims=True)
    centered = resid - mean
    inverse = lax.rsqrt(jnp.mean(jnp.square(centered), axis=1, keepdims=True) + EPSILON)
    hat = centered * inverse
    return (hat * gain + shift).astype(BF16), hat, inverse


def norm_back(grad, hat, inverse, gain):
    gain_grad = jnp.sum(grad * hat, axis=0)
    shift_grad = jnp.sum(grad, axis=0)
    grad_hat = grad * gain
    first = jnp.mean(grad_hat, axis=1, keepdims=True)
    second = jnp.mean(grad_hat * hat, axis=1, keepdims=True)
    return inverse * (grad_hat - first - hat * second), gain_grad, shift_grad


def make_local(rows):
    low, near = rows[-1], rows[:-1]

    def local(
        layer_input,
        attn_gain,
        attn_shift,
        qkv_weight,
        qkv_bias,
        output_weight,
        output_bias,
        mlp_gain,
        mlp_shift,
        up_weight,
        up_bias,
        down_weight,
        down_bias,
        cotangent,
    ):
        tokens, width = layer_input.shape
        n, _, side = qkv_weight.shape
        hidden = up_weight.shape[1]
        fast = n % 16 == 0 and len(near) == 2
        order = rows if fast else None

        def gather(shard, xor):
            if not fast:
                return jnp.concatenate(gather_rows(shard, rows), axis=1)
            if xor:
                stack = gather_near(shard, near)
            else:
                stack = shard
            return assemble(gather_far(stack, low), rows, xor)

        def reduce(parts):
            if not fast:
                own = jnp.concatenate(parts[:2])
                other = jnp.concatenate(parts[2:])
                return scatter_rows(own, other, rows)
            shape = (-1, n, parts[0].shape[1])
            stack = reduce_far([p.reshape(shape) for p in parts], low)
            return reduce_near(stack, near).astype(F32)

        attn_shard = jnp.concatenate([qkv_weight.reshape(n, -1), output_weight], axis=1)
        bias_pack = jnp.concatenate([qkv_bias.reshape(-1), up_bias])
        bias_other = swap(bias_pack, "y")
        qkv_bias_other = bias_other[: 2 * side].reshape(2, side)
        up_bias_other = bias_other[2 * side :]

        residual = layer_input.astype(F32)
        attn_in, attn_hat, attn_inverse = norm(residual, attn_gain, attn_shift)
        attn_in_other = swap(attn_in, "core")
        attn_full = gather(attn_shard, True)
        if fast:
            both = lax.all_gather(jnp.stack([up_weight, down_weight]), near, axis=0)
            both = both.reshape(-1, 2, n, hidden)
            up_full = gather(both[:, 0], False)
            down_full = gather(both[:, 1], False)
        else:
            up_full, down_full = gather(up_weight, True), gather(down_weight, True)
        cot_other = swap(cotangent, "core")

        both_bias = jnp.concatenate([qkv_bias, qkv_bias_other], axis=1)
        bias = jnp.stack([both_bias[0], jnp.zeros_like(both_bias[0]), both_bias[1]])
        bias = jnp.pad(bias, ((0, 5), (0, 0)))
        q, k, v, mixed, lse, attn_cat = attend_forward(attn_in, attn_in_other, attn_full, bias)
        out_full = attn_cat[:, 6 * side :]
        sent = swap(dot_nt(mixed[tokens:], out_full).astype(BF16), "core")
        attn_branch = dot_nt(mixed[:tokens], out_full) + sent.astype(F32) + output_bias
        hidden_resid = residual + attn_branch
        mlp_in, mlp_hat, mlp_inverse = norm(hidden_resid, mlp_gain, mlp_shift)
        mlp_in_other = swap(mlp_in, "core")

        rows8 = lambda b: jnp.broadcast_to(b, (8, hidden))
        act, slope, act_o, slope_o, *down_parts = up_and_down_grads(
            mlp_in,
            mlp_in_other,
            cotangent,
            cot_other,
            up_full,
            rows8(up_bias),
            rows8(up_bias_other),
            order,
            n,
        )
        down_grad = reduce(down_parts)

        pre, pre_o, up_sums, back, back_other = hidden_back(
            cotangent, cot_other, down_full, up_full, slope, slope_o
        )
        grad_mlp_in = back + swap(back_other, "core").astype(F32)
        up_parts = weight_grads(mlp_in, mlp_in_other, pre, pre_o, order, n)
        up_grad = reduce(up_parts)

        grad_out = cotangent.astype(F32)
        norm_grad, mlp_gain_grad, mlp_shift_grad = norm_back(
            grad_mlp_in, mlp_hat, mlp_inverse, mlp_gain
        )
        hidden_grad = grad_out + norm_grad
        grad_attn = hidden_grad.astype(BF16)
        grad_attn_other = swap(grad_attn, "core")

        down_own, down_far = down_full[:, :hidden], down_full[:, hidden:]
        branch = lambda at: dot_nt(act[at], down_own) + dot_nt(act_o[at], down_far)
        sent = swap(branch(slice(tokens, None)).astype(BF16), "core")
        mlp_branch = branch(slice(0, tokens)) + sent.astype(F32) + down_bias
        result = hidden_resid + mlp_branch

        grad_mixed = jnp.concatenate(
            [dot_nn(g, out_full).astype(BF16) for g in (grad_attn, grad_attn_other)]
        )
        dproj = attend_backward(q, k, v, grad_mixed, mixed, lse)
        attn_parts = attention_grads(
            attn_in, attn_in_other, grad_attn, grad_attn_other, dproj, mixed, order, n
        )
        attn_grad = reduce(attn_parts)
        qkv_full = attn_cat[:, : 6 * side]
        sent = swap(dot_nt(dproj[tokens:], qkv_full).astype(BF16), "core")
        grad_attn_in = dot_nt(dproj[:tokens], qkv_full) + sent.astype(F32)
        norm_grad, attn_gain_grad, attn_shift_grad = norm_back(
            grad_attn_in, attn_hat, attn_inverse, attn_gain
        )
        input_grad = hidden_grad + norm_grad
        qkv_grad = attn_grad[:, : 3 * side].reshape(n, 3, side)
        output_grad = attn_grad[:, 3 * side :]

        squares = jnp.stack(
            [
                jnp.sum(result * result),
                jnp.sum(attn_branch * attn_branch),
                jnp.sum(mlp_branch * mlp_branch),
            ]
        )
        common = jnp.concatenate(
            [
                attn_gain_grad,
                attn_shift_grad,
                jnp.sum(grad_attn.astype(F32), axis=0),
                mlp_gain_grad,
                mlp_shift_grad,
                jnp.sum(grad_out, axis=0),
                jnp.pad(squares, (0, 125)),
            ]
        )
        common = common + swap(common, "core")
        proj_sums = jnp.sum(dproj.astype(F32), axis=0)
        own = jnp.concatenate([proj_sums[:side], proj_sums[4 * side : 5 * side], up_sums[0]])
        other = jnp.concatenate([proj_sums[side : 2 * side], proj_sums[5 * side :], up_sums[1]])
        sums = jnp.concatenate([common, own])
        sums = sums + swap(jnp.concatenate([common, other]), "y")
        for axis in reversed(rows):
            sums = sums + swap(sums, axis)
        entry_count = tokens * 2 ** (len(rows) + 2) * width
        vec = [sums[i * width : (i + 1) * width] for i in range(6)]
        rms_values = jnp.sqrt(sums[6 * width : 6 * width + 3] / entry_count)
        tail = sums[6 * width + 128 :]
        return (
            result.astype(BF16),
            input_grad,
            vec[0],
            vec[1],
            qkv_grad,
            tail[: 2 * side].reshape(2, side),
            output_grad,
            vec[2],
            vec[3],
            vec[4],
            up_grad,
            tail[2 * side :],
            down_grad,
            vec[5],
            rms_values,
        )

    return local


def solution(mesh):
    row_size, col_size = mesh.shape["row"], mesh.shape["col"]
    bits = row_size.bit_length() - 1
    rows = tuple(f"r{b}" for b in reversed(range(bits)))
    cube = Mesh(mesh.devices.reshape((2,) * bits + (col_size // 2, 2)), rows + ("y", "core"))
    col = ("y", "core")
    every = rows + col
    placed = (
        P(every, None),
        P(),
        P(),
        P(rows, None, col),
        P(None, col),
        P(rows, col),
        P(),
        P(),
        P(),
        P(rows, col),
        P(col),
        P(rows, col),
        P(),
        P(every, None),
    )
    return jax.shard_map(
        make_local(rows),
        mesh=cube,
        in_specs=placed,
        out_specs=(
            P(every, None),
            P(every, None),
            P(),
            P(),
            P(rows, None, col),
            P(None, col),
            P(rows, col),
            P(),
            P(),
            P(),
            P(rows, col),
            P(col),
            P(rows, col),
            P(),
            P(),
        ),
        check_vma=False,
    )
```

```python
import math
from functools import partial

import jax
import jax.numpy as jnp
from jax import lax
from jax.experimental import pallas as pl
from jax.experimental.pallas import tpu as pltpu
from jax.sharding import Mesh, PartitionSpec as P

HEAD_DIM = 64
EPSILON = 1e-06
SWAP = [(0, 1), (1, 0)]
LOG2E = math.log2(math.e)
BF16 = jnp.bfloat16
F32 = jnp.float32
VMEM_BYTES = 16 * 2**20


def call(kernel, **kwargs):
    params = pltpu.CompilerParams(vmem_limit_bytes=VMEM_BYTES)
    return pl.pallas_call(kernel, compiler_params=params, **kwargs)


def cost(flops, bytes_accessed, transcendentals):
    return pl.CostEstimate(flops=0, bytes_accessed=0, transcendentals=0)


def after(arrays, *others):
    return lax.optimization_barrier((arrays, others))[0]


def swap(array, axis):
    return lax.ppermute(array, axis, SWAP)


def dot_nn(left, right):
    return lax.dot_general(left, right, (((1,), (0,)), ((), ())), preferred_element_type=F32)


def dot_nt(left, right):
    return lax.dot_general(left, right, (((1,), (1,)), ((), ())), preferred_element_type=F32)


def dot_tn(left, right):
    return lax.dot_general(left, right, (((0,), (0,)), ((), ())), preferred_element_type=F32)


def xor_exchange(blocks_of, axes):
    got = {}
    count = len(axes)
    sizes = [2] * count
    for bits in range(1, 2**count):
        perm = [(i, i ^ bits) for i in range(math.prod(sizes))]
        got[bits] = lax.ppermute(blocks_of(bits), axes, perm)
    return got


def in_order(own, got, axes):
    parts = [own] + [got[bits] for bits in range(1, 2 ** len(axes))]
    for depth, axis in enumerate(reversed(axes)):
        bit = 2**depth
        flip = lax.axis_index(axis) == 1
        parts = [jnp.where(flip, parts[i ^ bit], parts[i]) for i in range(len(parts))]
    return jnp.stack(parts)


def pair_in_order(own, other, axis, dim):
    flip = lax.axis_index(axis) == 1
    return jnp.stack([jnp.where(flip, other, own), jnp.where(flip, own, other)], axis=dim)


def gather_rows(shard, rows):
    low, high = rows[-1], rows[:-1]
    n, c = shard.shape
    near = high[-2:]
    stack = in_order(shard, xor_exchange(lambda bits: shard, near), near)
    for axis in reversed(high[:-2]):
        other = swap(stack, axis)
        stack = pair_in_order(stack, other, axis, 0).reshape(-1, n, c)
    half = c // 2
    first, second = stack[:, :, :half], stack[:, :, half:]
    first_low, second_y = swap(first, low), swap(second, "y")
    first = pair_in_order(first, first_low, low, 1).reshape(-1, half)
    first_y = swap(first, "y")
    second_low = swap(jnp.stack([second, second_y]), low)
    second_own = pair_in_order(second, second_low[0], low, 1).reshape(-1, half)
    second_other = pair_in_order(second_y, second_low[1], low, 1).reshape(-1, half)
    return (
        jnp.concatenate([first, second_own], axis=1),
        jnp.concatenate([first_y, second_other], axis=1),
    )


def pick(array, axis, dim, other):
    zero = lax.index_in_dim(array, 0, dim, keepdims=False)
    one = lax.index_in_dim(array, 1, dim, keepdims=False)
    flip = lax.axis_index(axis) == (0 if other else 1)
    return jnp.where(flip, one, zero)


def scatter_rows(own, other, rows):
    low, high = rows[-1], rows[:-1]
    near = high[-2:]
    total = 2 ** len(rows)
    n, c = own.shape[0] // total, own.shape[1]
    half = c // 2
    own = own.reshape(total // 2, 2, n, c)
    other = other.reshape(total // 2, 2, n, c)
    a_own, a_other = own[..., :half], other[..., :half]
    b_own, b_other = own[..., half:], other[..., half:]
    a_got = swap(a_other, "y")
    b_send = jnp.stack([pick(b_own, low, 1, True), pick(b_other, low, 1, True)])
    b_got = swap(b_send, low)
    a_sum = a_own.astype(F32) + a_got.astype(F32)
    a_send = pick(a_sum, low, 1, True).astype(BF16)
    b_own = pick(b_own, low, 1, False).astype(F32) + b_got[0].astype(F32)
    b_other = (pick(b_other, low, 1, False).astype(F32) + b_got[1].astype(F32)).astype(BF16)
    a_got = swap(a_send, low)
    b_got = swap(b_other, "y")
    a_sum = pick(a_sum, low, 1, False) + a_got.astype(F32)
    b_sum = b_own + b_got.astype(F32)
    both = jnp.concatenate([a_sum, b_sum], axis=2)
    for axis in high[:-2]:
        both = both.reshape(2, -1, n, c)
        got = swap(pick(both, axis, 0, True).astype(BF16), axis)
        both = pick(both, axis, 0, False) + got.astype(F32)
    low_both = both.astype(BF16)
    place = lax.axis_index(near)
    take = lambda bits: lax.dynamic_index_in_dim(low_both, place ^ bits, 0, keepdims=False)
    got = xor_exchange(take, near)
    out = lax.dynamic_index_in_dim(both, place, 0, keepdims=False)
    for piece in got.values():
        out = out + piece.astype(F32)
    return out


BLOCKS = 8


def gather_near(shard, near):
    got = xor_exchange(lambda bits: shard, near)
    return [shard] + [got[bits] for bits in range(1, 2 ** len(near))]


def gather_far(stack, low):
    return stack, swap(stack, low), swap(stack, "y")


def gather_corners(far, low):
    stack, from_low, from_y = far
    half = stack.shape[0] // 2
    return (*far, swap(from_low[:half], "y"), swap(from_y[half:], low))


def gather_plain(shard, rows):
    pieces = []
    for side in gather_rows(shard, rows):
        width, c = side.shape
        blocks = side.reshape(BLOCKS // 2, 2, width // BLOCKS, c)
        pieces += [blocks[:, 0], blocks[:, 1]]
    half = BLOCKS // 4
    return (*pieces[:3], pieces[3][:half], pieces[3][half:])


def reduce_corners(parts, low):
    return swap(parts[3], "y"), swap(parts[4], low)


def reduce_far(parts, got, low):
    _, to_low, to_y, _, _ = parts
    half = to_low.shape[0] // 2
    add = lambda a, b: (a.astype(F32) + b.astype(F32)).astype(BF16)
    to_low = jnp.concatenate([add(to_low[:half], got[0]), to_low[half:]])
    to_y = jnp.concatenate([to_y[:half], add(to_y[half:], got[1])])
    return swap(to_low, low), swap(to_y, "y")


def send_near(stack, near):
    low = stack.astype(BF16)
    return stack[0], xor_exchange(lambda bits: low[bits], near)


def sum_near(own, got):
    for piece in got.values():
        own = own + piece.astype(F32)
    return own


def here(rows):
    if rows is None:
        return 0, 0
    return lax.axis_index(rows[:-1]), lax.axis_index(rows[-1])


def flip(at, by):
    return by if isinstance(at, int) else lax.bitwise_xor(at, by)


def slot_of(rows, block):
    z, x = here(rows)
    block_z, block_x = divmod(block, 2)
    return flip(x, block_x) * (BLOCKS // 2) + flip(z, block_z)


def whole(shape):
    return pl.BlockSpec(shape, lambda *_: (0,) * len(shape))


def side_pieces(raw, sides):
    return [p for side in sides for p in (raw[:2] if side == 0 else raw[2:])]


def put_together(rows, refs, out_ref, source=slice(None), target=slice(None)):
    z, x = here(rows)
    at = 0
    for ref, x_flip in zip(refs, (0, 1, 1)):
        for k in range(ref.shape[0]):
            n = ref.shape[1]
            slot = k + (at if x_flip else 0)
            row = (flip(z, slot) * 2 + flip(x, x_flip)) * n
            out_ref[pl.ds(pl.multiple_of(row, n), n), target] = ref[k, :, source]
        at += ref.shape[0] * x_flip


def turn_kernel(rows, a_ref, b_ref, out_ref):
    tokens, width = a_ref.shape
    n = width // BLOCKS
    for half, ref in enumerate((a_ref, b_ref)):
        turned = ref[...].T
        for block in range(BLOCKS):
            at = pl.multiple_of(slot_of(rows, block) * n, n)
            out_ref[pl.ds(at, n), half * tokens : (half + 1) * tokens] = turned[
                block * n : (block + 1) * n, :
            ]


def turn(a, b, rows):
    tokens, width = a.shape
    return call(
        partial(turn_kernel, rows),
        out_shape=jax.ShapeDtypeStruct((width, 2 * tokens), BF16),
        cost_estimate=cost(
            flops=0, bytes_accessed=8 * tokens * width, transcendentals=0
        ),
        name="turn",
    )(a, b)


GRAD_PARTS = {0: (2, 2), 1: (2, 4, 4)}


def store_parts(grads, refs):
    at = 0
    for ref in refs:
        ref[...] = grads[at : at + ref.shape[0]].astype(BF16)
        at += ref.shape[0]


def grad_shapes(width, c):
    return [jax.ShapeDtypeStruct((width // f, c), BF16) for side in (0, 1) for f in GRAD_PARTS[side]]


def pair_sources(pair):
    return {0: [(0, 0, 2)], 1: [(0, 2, 1), (1, 2, 1)], 2: [(1, 0, 2)]}[pair]


def attend_forward_kernel(rows, pair, *refs):
    xa_ref, xb_ref, *raw, bias_ref, q_ref, k_ref, v_ref, w_ref, mixed_ref, lse_ref, vt_ref = refs
    raw = {0: [raw], 1: [raw[:2], raw[2:]], 2: [raw]}[pair]
    d = HEAD_DIM
    two = 2 * d
    tokens = xa_ref.shape[0]
    step = pl.program_id(0)
    block = mixed_ref.shape[0]

    @pl.when(step == 0)
    def _():
        for kind in range(4):
            at = kind * two
            for pieces, (_, first, heads) in zip(raw, pair_sources(pair)):
                source = (kind * 3 + first) * d
                put_together(
                    rows,
                    pieces,
                    w_ref,
                    slice(source, source + heads * d),
                    slice(at, at + heads * d),
                )
                at += heads * d
        for half, ref in enumerate((xa_ref, xb_ref)):
            at = slice(half * tokens, (half + 1) * tokens)
            proj = dot_nn(ref[...], w_ref[:, : 3 * two]) + bias_ref[pair : pair + 1, :]
            proj = proj.astype(BF16)
            q_ref[at, :] = proj[:, :two]
            k_ref[at, :] = proj[:, two : 2 * two]
            v_ref[at, :] = proj[:, 2 * two :]
        turned = v_ref[...].T
        for head in range(2):
            vt_ref[head, :d, :] = turned[head * d : (head + 1) * d, :]
            vt_ref[head, d:, :] = jnp.ones((vt_ref.shape[1] - d, turned.shape[1]), BF16)

    query = q_ref[pl.ds(pl.multiple_of(step * block, block), block), :]
    lane = lax.broadcasted_iota(jnp.int32, query.shape, 1)
    outs = []
    for head in range(2):
        masked = jnp.where(lane // d == head, query, jnp.zeros_like(query)) * BF16(d**-0.5)
        scores = dot_nt(k_ref[...], masked)
        top = jnp.max(scores, axis=0, keepdims=True)
        weights = jnp.exp2((scores - top) * LOG2E).astype(BF16)
        out = dot_nn(vt_ref[head], weights)
        total = out[d : d + 1, :]
        outs.append(out[:d, :] * (1.0 / total))
        lse_ref[head : head + 1, :] = top + jnp.log(total)
    mixed_ref[...] = jnp.concatenate(outs, axis=0).T.astype(BF16)


def attend_forward(xa, xb, raw, bias, rows, pair):
    tokens, width = xa.shape
    seq = 2 * tokens
    two = 2 * HEAD_DIM
    block = 512
    part = jax.ShapeDtypeStruct((seq, two), BF16)
    weight = jax.ShapeDtypeStruct((width, 4 * two), BF16)
    ins = [xa, xb, *side_pieces(raw, [side for side, *_ in pair_sources(pair)]), bias]
    return call(
        partial(attend_forward_kernel, rows, pair),
        grid=(seq // block,),
        in_specs=[whole(a.shape) for a in ins],
        out_specs=[
            whole(part.shape),
            whole(part.shape),
            whole(part.shape),
            whole(weight.shape),
            pl.BlockSpec((block, two), lambda i: (i, 0)),
            pl.BlockSpec((8, block), lambda i: (0, i)),
        ],
        out_shape=[part, part, part, weight, part, jax.ShapeDtypeStruct((8, seq), F32)],
        scratch_shapes=[pltpu.VMEM((2, HEAD_DIM + 16, seq), BF16)],
        cost_estimate=cost(
            flops=24 * seq * seq * two, bytes_accessed=16 * seq * width, transcendentals=seq * seq
        ),
        name=f"attend_forward_{pair}",
    )(*ins)


def attend_backward_kernel(rows, pair, *refs):
    q_ref, k_ref, v_ref, w_ref, ga_ref, gb_ref, turned_ref, mixed_ref, lse_ref = refs[:9]
    kt_ref, dk_acc, dv_acc, gmix_ref, gall_ref, out_ref = refs[-6:]
    *grads_refs, dproj_ref, sum_ref = refs[9:-6]
    step = pl.program_id(0)
    d = HEAD_DIM
    two = 2 * d
    scale = d**-0.5
    tokens = ga_ref.shape[0]
    block = lse_ref.shape[1]

    @pl.when(step == 0)
    def _():
        kt_ref[...] = k_ref[...].T
        dk_acc[...] = jnp.zeros_like(dk_acc)
        dv_acc[...] = jnp.zeros_like(dv_acc)
        for half, ref in enumerate((ga_ref, gb_ref)):
            at = slice(half * tokens, (half + 1) * tokens)
            gall_ref[at, :] = ref[...]
            gmix_ref[at, :] = dot_nn(ref[...], w_ref[:, 3 * two :]).astype(BF16)

    here_rows = pl.ds(pl.multiple_of(step * block, block), block)
    query = q_ref[here_rows, :]
    grad = gmix_ref[here_rows, :]
    lane = lax.broadcasted_iota(jnp.int32, query.shape, 1)
    dots = (grad.astype(F32) * mixed_ref[here_rows, :].astype(F32)).T
    dqs = []
    for head in range(2):
        mine = lane // d == head
        query_h = jnp.where(mine, query, jnp.zeros_like(query))
        grad_h = jnp.where(mine, grad, jnp.zeros_like(grad))
        row_dots = jnp.sum(dots[head * d : (head + 1) * d, :], axis=0, keepdims=True)
        log_total = lse_ref[head : head + 1, :] * LOG2E
        scores = dot_nt(k_ref[...], query_h * BF16(scale))
        probs = jnp.exp2(scores * LOG2E - log_total)
        grad_probs = dot_nt(v_ref[...], grad_h)
        grad_scores = (probs * (grad_probs - row_dots)).astype(BF16)
        dv_acc[...] += dot_nn(probs.astype(BF16), grad_h)
        dk_acc[...] += dot_nn(grad_scores, query_h)
        dqs.append(dot_nn(kt_ref[head * d : (head + 1) * d, :], grad_scores) * scale)
    dproj_ref[here_rows, :two] = jnp.concatenate(dqs, axis=0).T.astype(BF16)

    @pl.when(step == pl.num_programs(0) - 1)
    def _():
        dproj_ref[:, two : 2 * two] = (dk_acc[...] * scale).astype(BF16)
        dproj_ref[:, 2 * two :] = dv_acc[...].astype(BF16)
        dproj = dproj_ref[...]
        sum_ref[0:1, :] = jnp.sum(dproj.astype(F32), axis=0, keepdims=True)
        out_ref[:, : 3 * two] = dot_nn(turned_ref[...], dproj).astype(BF16)
        grads = dot_nn(mixed_ref[...].T, gall_ref[...]).T.astype(BF16)
        n = grads.shape[0] // BLOCKS
        for at_block in range(BLOCKS):
            at = pl.multiple_of(slot_of(rows, at_block) * n, n)
            out_ref[pl.ds(at, n), 3 * two :] = grads[at_block * n : (at_block + 1) * n, :]
        if len(grads_refs) == 1:
            grads_refs[0][...] = out_ref[...]
        else:
            for kind in range(4):
                for side, ref in enumerate(grads_refs):
                    ref[:, kind * d : (kind + 1) * d] = out_ref[
                        :, kind * two + side * d : kind * two + (side + 1) * d
                    ]


def attend_backward(q, k, v, w, ga, gb, turned, mixed, lse, rows, pair):
    seq, two = q.shape
    width = ga.shape[1]
    block = 256
    count = len(pair_sources(pair))
    outs = [jax.ShapeDtypeStruct((width, 4 * two // count), BF16)] * count + [
        jax.ShapeDtypeStruct((seq, 3 * two), BF16),
        jax.ShapeDtypeStruct((8, 3 * two), F32),
    ]
    ins = [q, k, v, w, ga, gb, turned, mixed]
    *grads, dproj, sums = call(
        partial(attend_backward_kernel, rows, pair),
        grid=(seq // block,),
        in_specs=[whole(a.shape) for a in ins] + [pl.BlockSpec((8, block), lambda i: (0, i))],
        out_specs=[whole(o.shape) for o in outs],
        out_shape=outs,
        scratch_shapes=[
            pltpu.VMEM((two, seq), BF16),
            pltpu.VMEM((seq, two), F32),
            pltpu.VMEM((seq, two), F32),
            pltpu.VMEM((seq, two), BF16),
            pltpu.VMEM((seq, width), BF16),
            pltpu.VMEM((width, 4 * two), BF16),
        ],
        cost_estimate=cost(
            flops=50 * seq * seq * two, bytes_accessed=16 * seq * width, transcendentals=seq * seq
        ),
        name=f"attend_backward_{pair}",
    )(*ins, lse)
    return grads, dproj, sums


def project_kernel(first, cols, *refs):
    count = (len(refs) - 1) // 2
    total = 0.0
    for part, weight in zip(refs[:count], refs[count:-1]):
        total = total + dot_nt(part[...], weight[...])
    refs[-1][...] = total.astype(refs[-1].dtype)


def project(parts, weights, half, first, dtype):
    seq, cols = parts[0].shape
    width = weights[0].shape[0]
    tokens = seq // 2
    return call(
        partial(project_kernel, first, cols),
        grid=(1,),
        in_specs=[pl.BlockSpec((tokens, cols), lambda i: (half, 0)) for _ in parts]
        + [pl.BlockSpec((width, cols), lambda i: (0, first // cols)) for _ in weights],
        out_specs=whole((tokens, width)),
        out_shape=jax.ShapeDtypeStruct((tokens, width), dtype),
        cost_estimate=cost(
            flops=2 * tokens * width * cols * 3, bytes_accessed=0, transcendentals=0
        ),
        name="project",
    )(*parts, *weights)


def statistics(rows):
    mean = jnp.mean(rows, axis=1, keepdims=True)
    centered = rows - mean
    inverse = lax.rsqrt(jnp.mean(jnp.square(centered), axis=1, keepdims=True) + EPSILON)
    return centered * inverse, inverse


def add_rows(sum_ref, values):
    @pl.when(pl.program_id(0) == 0)
    def _():
        sum_ref[...] = jnp.zeros_like(sum_ref)

    for i, value in enumerate(values):
        sum_ref[i : i + 1, :] += jnp.sum(value, axis=0, keepdims=True)


ATTN_GAIN, ATTN_SHIFT, MLP_GAIN, MLP_SHIFT, OUTPUT_BIAS, DOWN_BIAS = range(6)


def vector(ref, at):
    return ref[at : at + 1, :]


def norm_kernel(x_ref, vec_ref, out_ref):
    hat, _ = statistics(x_ref[...].astype(F32))
    out_ref[...] = (hat * vector(vec_ref, ATTN_GAIN) + vector(vec_ref, ATTN_SHIFT)).astype(BF16)


def resid_kernel(x_ref, own_ref, got_ref, vec_ref, resid_ref, out_ref, sum_ref):
    branch = own_ref[...] + got_ref[...].astype(F32) + vector(vec_ref, OUTPUT_BIAS)
    resid = x_ref[...].astype(F32) + branch
    resid_ref[...] = resid
    hat, _ = statistics(resid)
    out_ref[...] = (hat * vector(vec_ref, MLP_GAIN) + vector(vec_ref, MLP_SHIFT)).astype(BF16)
    add_rows(sum_ref, [branch * branch])


def result_kernel(resid_ref, own_ref, got_ref, vec_ref, out_ref, sum_ref):
    branch = own_ref[...] + got_ref[...].astype(F32) + vector(vec_ref, DOWN_BIAS)
    result = resid_ref[...] + branch
    out_ref[...] = result.astype(BF16)
    add_rows(sum_ref, [result * result, branch * branch])


def norm_gradient(grad, rows, gain):
    hat, inverse = statistics(rows)
    grad_hat = grad * gain
    first = jnp.mean(grad_hat, axis=1, keepdims=True)
    second = jnp.mean(grad_hat * hat, axis=1, keepdims=True)
    return inverse * (grad_hat - first - hat * second), grad * hat


def middle_kernel(resid_ref, own_ref, got_ref, cot_ref, vec_ref, grad_ref, low_ref, sum_ref):
    grad = own_ref[...] + got_ref[...].astype(F32)
    back, gains = norm_gradient(grad, resid_ref[...], vector(vec_ref, MLP_GAIN))
    cot = cot_ref[...].astype(F32)
    hidden = cot + back
    grad_ref[...] = hidden
    low = hidden.astype(BF16)
    low_ref[...] = low
    add_rows(sum_ref, [gains, grad, low.astype(F32), cot])


def last_kernel(x_ref, own_ref, got_ref, hidden_ref, vec_ref, grad_ref, sum_ref):
    grad = own_ref[...] + got_ref[...].astype(F32)
    back, gains = norm_gradient(grad, x_ref[...].astype(F32), vector(vec_ref, ATTN_GAIN))
    grad_ref[...] = hidden_ref[...] + back
    add_rows(sum_ref, [gains, grad])


def by_rows(kernel, name, rows, vectors, outs, sums=False):
    tokens, width = rows[0].shape
    block = tokens // 2
    part = pl.BlockSpec((block, width), lambda i: (i, 0))
    out_shape = [jax.ShapeDtypeStruct((tokens, width), t) for t in outs]
    out_specs = [part] * len(outs)
    if sums:
        out_shape.append(jax.ShapeDtypeStruct((8, width), F32))
        out_specs.append(whole((8, width)))
    return call(
        kernel,
        grid=(tokens // block,),
        in_specs=[part] * len(rows) + [whole(vectors.shape)],
        out_specs=out_specs,
        out_shape=out_shape,
        cost_estimate=cost(flops=0, bytes_accessed=0, transcendentals=0),
        name=name,
    )(*rows, vectors)


def gelu_parts(u):
    c0 = math.sqrt(2.0 / math.pi)
    square = u * u
    t = jnp.tanh(u * (c0 + (c0 * 0.044715) * square))
    half = 0.5 * u
    act = half + half * t
    slope = 0.5 + 0.5 * t + half * (1.0 - t * t) * (c0 + (3.0 * c0 * 0.044715) * square)
    return act, slope


def up_kernel(rows, side, *refs):
    xa_ref, xb_ref, turned_ref, *raw, bias_ref, act_ref, slope_ref = refs[: -1 - len(GRAD_PARTS[side])]
    outs, w_ref = refs[-1 - len(GRAD_PARTS[side]) : -1], refs[-1]
    tokens = xa_ref.shape[0]
    put_together(rows, raw, w_ref)
    for half, ref in enumerate((xa_ref, xb_ref)):
        act, slope = gelu_parts(dot_nn(ref[...], w_ref[...]) + bias_ref[side : side + 1, :])
        act_ref[half * tokens : (half + 1) * tokens, :] = act.astype(BF16)
        slope_ref[half * tokens : (half + 1) * tokens, :] = slope.astype(BF16)
    store_parts(dot_nn(turned_ref[...], act_ref[...]), outs)


TILE = 256


def tiles(*dims):
    return pl.BlockSpec((*dims, TILE), lambda j: (0,) * len(dims) + (j,))


def raw_tiles(raw):
    return [tiles(*r.shape[:2]) for r in raw]


def up_and_down_grads(xa, xb, turned, raw, bias, rows, side):
    tokens, width = xa.shape
    c = bias.shape[1]
    hidden = jax.ShapeDtypeStruct((2 * tokens, c), BF16)
    grads = [jax.ShapeDtypeStruct((width // f, c), BF16) for f in GRAD_PARTS[side]]
    raw = side_pieces(raw, [side])
    act, slope, *grads = call(
        partial(up_kernel, rows, side),
        grid=(c // TILE,),
        in_specs=[whole(xa.shape), whole(xb.shape), whole(turned.shape)]
        + raw_tiles(raw)
        + [tiles(8)],
        out_specs=[tiles(2 * tokens)] * 2 + [tiles(g.shape[0]) for g in grads],
        out_shape=[hidden] * 2 + grads,
        scratch_shapes=[pltpu.VMEM((width, TILE), BF16)],
        cost_estimate=cost(
            flops=8 * tokens * width * c, bytes_accessed=0, transcendentals=2 * tokens * c
        ),
        name=f"up_and_down_grads_{side}",
    )(xa, xb, turned, *raw, bias)
    return act, slope, grads


def hidden_back_kernel(rows, *refs):
    ga_ref, gb_ref = refs[:2]
    down, up = refs[2:7], refs[7:12]
    slope_ref, slope_o_ref, pre_ref, pre_o_ref, sum_ref, own_ref, other_ref = refs[12:19]
    acc_ref, w_ref, u_ref = refs[19:]
    step = pl.program_id(0)
    tokens = ga_ref.shape[0]

    @pl.when(step == 0)
    def _():
        acc_ref[...] = jnp.zeros_like(acc_ref)

    for side, (slopes, pres) in enumerate(((slope_ref, pre_ref), (slope_o_ref, pre_o_ref))):
        put_together(rows, down[:2] if side == 0 else down[2:], w_ref.at[side])
        put_together(rows, up[:2] if side == 0 else up[2:], u_ref.at[side])
        totals = 0.0
        for half, ref in enumerate((ga_ref, gb_ref)):
            at = slice(half * tokens, (half + 1) * tokens)
            back = dot_nn(ref[...], w_ref[side]) * slopes[at, :].astype(F32)
            pre = back.astype(BF16)
            pres[at, :] = pre
            totals = totals + jnp.sum(pre.astype(F32), axis=0, keepdims=True)
            acc_ref[at, :] += dot_nt(pre, u_ref[side])
        sum_ref[side : side + 1, :] = totals

    @pl.when(step == pl.num_programs(0) - 1)
    def _():
        own_ref[...] = acc_ref[:tokens, :]
        other_ref[...] = acc_ref[tokens:, :].astype(BF16)


def hidden_back(ga, gb, down, up, slope, slope_o, rows):
    tokens, width = ga.shape
    c = slope.shape[1]
    hidden = jax.ShapeDtypeStruct((2 * tokens, c), BF16)
    return call(
        partial(hidden_back_kernel, rows),
        grid=(c // TILE,),
        in_specs=[whole(ga.shape), whole(gb.shape)]
        + raw_tiles(down)
        + raw_tiles(up)
        + [tiles(2 * tokens)] * 2,
        out_specs=[tiles(2 * tokens)] * 2 + [tiles(8), whole(ga.shape), whole(ga.shape)],
        out_shape=[
            hidden,
            hidden,
            jax.ShapeDtypeStruct((8, c), F32),
            jax.ShapeDtypeStruct(ga.shape, F32),
            jax.ShapeDtypeStruct(ga.shape, BF16),
        ],
        scratch_shapes=[
            pltpu.VMEM((2 * tokens, width), F32),
            pltpu.VMEM((2, width, TILE), BF16),
            pltpu.VMEM((2, width, TILE), BF16),
        ],
        cost_estimate=cost(
            flops=16 * tokens * width * c, bytes_accessed=24 * tokens * c, transcendentals=0
        ),
        name="hidden_back",
    )(ga, gb, *down, *up, slope, slope_o)


def mlp_out_kernel(rows, *refs):
    act_ref, act_o_ref = refs[:2]
    down = refs[2:7]
    own_ref, other_ref, acc_ref, w_ref = refs[7:]
    step = pl.program_id(0)
    tokens = own_ref.shape[0]

    @pl.when(step == 0)
    def _():
        acc_ref[...] = jnp.zeros_like(acc_ref)

    put_together(rows, down[:2], w_ref.at[0])
    put_together(rows, down[2:], w_ref.at[1])
    acc_ref[...] += dot_nt(act_ref[...], w_ref[0]) + dot_nt(act_o_ref[...], w_ref[1])

    @pl.when(step == pl.num_programs(0) - 1)
    def _():
        own_ref[...] = acc_ref[:tokens, :]
        other_ref[...] = acc_ref[tokens:, :].astype(BF16)


def mlp_out(act, act_o, down, width, rows):
    seq, c = act.shape
    outs = [jax.ShapeDtypeStruct((seq // 2, width), t) for t in (F32, BF16)]
    return call(
        partial(mlp_out_kernel, rows),
        grid=(c // TILE,),
        in_specs=[tiles(seq)] * 2 + raw_tiles(down),
        out_specs=[whole(o.shape) for o in outs],
        out_shape=outs,
        scratch_shapes=[pltpu.VMEM((seq, width), F32), pltpu.VMEM((2, width, TILE), BF16)],
        cost_estimate=cost(
            flops=4 * seq * width * c, bytes_accessed=4 * seq * c, transcendentals=0
        ),
        name="mlp_out",
    )(act, act_o, *down)


def weight_grads_kernel(turned_ref, g_ref, go_ref, *outs):
    store_parts(dot_nn(turned_ref[...], g_ref[...]), outs[:2])
    store_parts(dot_nn(turned_ref[...], go_ref[...]), outs[2:])


def weight_grads(turned, grad, grad_o):
    width, seq = turned.shape
    c = grad.shape[1]
    return call(
        weight_grads_kernel,
        grid=(c // TILE,),
        in_specs=[whole(turned.shape), tiles(seq), tiles(seq)],
        out_specs=[tiles(s.shape[0]) for s in grad_shapes(width, c)],
        out_shape=grad_shapes(width, c),
        cost_estimate=cost(
            flops=4 * seq * width * c, bytes_accessed=6 * seq * c, transcendentals=0
        ),
        name="weight_grads",
    )(turned, grad, grad_o)


def make_local(rows):
    low, near = rows[-1], rows[:-1]
    fast = 2 ** len(rows) == BLOCKS
    order = rows if fast else None

    def to_blocks(parts):
        width, c = parts[0].shape[0] * 2, parts[0].shape[1]
        return [p.reshape(-1, width // BLOCKS, c) for p in parts]

    def reduce_plain(parts):
        blocks = to_blocks(parts)
        own = jnp.stack(blocks[:2], axis=1)
        other = jnp.stack([blocks[2], jnp.concatenate(blocks[3:])], axis=1)
        width, c = parts[0].shape[0] * 2, parts[0].shape[1]
        return scatter_rows(own.reshape(width, c), other.reshape(width, c), rows)

    def natural(grads):
        width, c = grads.shape
        blocks = grads.reshape(2, BLOCKS // 2, width // BLOCKS, c)
        return jnp.swapaxes(blocks, 0, 1).reshape(width, c)

    def local(
        layer_input,
        attn_gain,
        attn_shift,
        qkv_weight,
        qkv_bias,
        output_weight,
        output_bias,
        mlp_gain,
        mlp_shift,
        up_weight,
        up_bias,
        down_weight,
        down_bias,
        cotangent,
    ):
        tokens, width = layer_input.shape
        n, _, side = qkv_weight.shape
        hidden = up_weight.shape[1]
        d = HEAD_DIM

        attn_shard = jnp.concatenate([qkv_weight.reshape(n, -1), output_weight], axis=1)
        vectors = jnp.concatenate(
            [attn_gain, attn_shift, mlp_gain, mlp_shift, output_bias, down_bias]
        ).reshape(6, width)
        (attn_in,) = by_rows(norm_kernel, "norm", [layer_input], vectors, [BF16])
        attn_in_other = swap(attn_in, "core")
        cot_other = swap(cotangent, "core")
        bias_other = swap(jnp.concatenate([qkv_bias.reshape(-1), up_bias]), "y")
        if fast:
            attn_near = gather_near(attn_shard, near)
            attn_near = after(attn_near, attn_in_other, cot_other, bias_other)
            attn_stack = jnp.stack(attn_near)
            mlp_near = gather_near(jnp.stack([up_weight, down_weight]), near)
            attn_far = gather_far(attn_stack, low)
            attn_raw = gather_corners(attn_far, low)
        else:
            attn_raw, up_raw, down_raw = (
                gather_plain(w, rows) for w in (attn_shard, up_weight, down_weight)
            )
        qkv_bias_other = bias_other[: 2 * side].reshape(2, side)
        up_bias_other = bias_other[2 * side :]
        halves = (attn_in, attn_in_other, cotangent, cot_other)
        if fast:
            halves = after(halves, attn_stack)
        attn_turned = turn(*halves[:2], order)
        cot_turned = turn(*halves[2:], order)
        table = []
        for pair in range(3):
            for kind in range(3):
                for at, first, heads in pair_sources(pair):
                    if kind == 1:
                        table.append(jnp.zeros((heads * d,), F32))
                        continue
                    source = (qkv_bias, qkv_bias_other)[at][kind // 2]
                    table.append(source[first * d : (first + heads) * d])
        table = jnp.pad(jnp.concatenate(table).reshape(3, 6 * d), ((0, 5), (0, 0)))
        up_biases = jnp.pad(jnp.stack([up_bias, up_bias_other]), ((0, 6), (0, 0)))

        attended = []
        for pair in range(3):
            bias = table
            if fast and pair == 0:
                bias = after(bias, attn_far, attn_turned, cot_turned)
            if pair:
                bias = after(bias, attended[pair - 1][4])
            if fast and pair == 1:
                mlp_near = after(mlp_near, attended[0][4], attn_raw)
                up_far = gather_far(jnp.stack([m[0] for m in mlp_near]), low)
                down_stack = jnp.stack([m[1] for m in mlp_near])
                bias = after(bias, up_far[0], down_stack)
            if fast and pair == 2:
                down_far = gather_far(after(down_stack, attended[1][4]), low)
                bias = after(bias, down_far[0])
            attended.append(attend_forward(attn_in, attn_in_other, attn_raw, bias, order, pair))
        mixed = [a[4] for a in attended]
        weights = [a[3] for a in attended]
        if fast:
            mixed, up_far = after((mixed, up_far))
            up_raw = gather_corners(up_far, low)
        got = swap(project(mixed, weights, 1, 6 * d, BF16), "core")
        own = project(mixed, weights, 0, 6 * d, F32)
        hidden_resid, mlp_in, branch_sums = by_rows(
            resid_kernel,
            "resid",
            [layer_input, own, got],
            vectors,
            [F32, BF16],
            True,
        )
        mlp_in, up_raw = after((mlp_in, up_raw))
        mlp_in_other = swap(mlp_in, "core")

        ins = (mlp_in, mlp_in_other, cot_turned)
        act, slope, down_own = up_and_down_grads(*ins, up_raw, up_biases, order, 0)
        if fast:
            up_biases, down_far = after((up_biases, down_far), act)
            down_raw = gather_corners(down_far, low)
        act_o, slope_o, down_other = up_and_down_grads(*ins, up_raw, up_biases, order, 1)
        down_parts = down_own + down_other
        if fast:
            down_parts = to_blocks(down_parts)
            down_got = reduce_corners(down_parts, low)
        else:
            down_grad = reduce_plain(down_parts)
        pre, pre_o, up_sums, back, back_other = hidden_back(
            cotangent, cot_other, down_raw, up_raw, slope, slope_o, order
        )
        back_got = swap(back_other, "core")
        if fast:
            act, act_o, down_got = after((act, act_o, down_got), pre)
            down_sent = reduce_far(down_parts, down_got, low)
        branch, branch_other = mlp_out(act, act_o, down_raw, width, order)
        back = after(back, branch)
        hidden_grad, grad_attn, middle_sums = by_rows(
            middle_kernel,
            "middle",
            [hidden_resid, back, back_got, cotangent],
            vectors,
            [F32, BF16],
            True,
        )
        grad_attn_other = swap(grad_attn, "core")
        branch_got = swap(after(branch_other, grad_attn), "core")
        mlp_turned = turn(*after((mlp_in, mlp_in_other), grad_attn), order)
        up_parts = weight_grads(mlp_turned, pre, pre_o)
        resid, branch, branch_got = after((hidden_resid, branch, branch_got), up_parts)
        layer_output, result_sums = by_rows(
            result_kernel, "result", [resid, branch, branch_got], vectors, [BF16], True
        )
        if fast:
            up_parts = to_blocks(up_parts)
            up_got = reduce_corners(up_parts, low)
            down_sent = after(down_sent, layer_output)
            total = down_parts[0].astype(F32) + sum(g.astype(F32) for g in down_sent)
            total, down_got = total[:2], swap(total[2:].astype(BF16), near[0])
        else:
            up_grad = reduce_plain(up_parts)

        pair_grads, pair_sums, dprojs = {}, {}, {}
        for pair in (1, 2, 0):
            q, k, v, w, mix, lse = attended[pair]
            if pair == 1:
                lse = after(lse, layer_output)
            if fast and pair == 2:
                lse, up_got, down_got = after((lse, up_got, down_got), pair_grads[1])
                up_sent = reduce_far(up_parts, up_got, low)
                total = total + down_got.astype(F32)
                down_grad, down_got = total[0], swap(total[1].astype(BF16), near[1])
            if fast and pair == 0:
                lse, down_got, small_got, up_sent = after(
                    (lse, down_got, small_got, up_sent), pair_grads[2]
                )
                down_grad = down_grad + down_got.astype(F32)
                small = pair_grads[1][0].astype(F32) + small_got.astype(F32)
                small_sent = swap(small[width // 2 :].astype(BF16), low)
                total = up_parts[0].astype(F32) + sum(g.astype(F32) for g in up_sent)
                up_near = send_near(total, near)
            pair_grads[pair], dprojs[pair], pair_sums[pair] = attend_backward(
                q, k, v, w, grad_attn, grad_attn_other, attn_turned, mix, lse, order, pair
            )
            if fast and pair == 1:
                small_got = swap(pair_grads[1][1], "y")
            if fast and pair == 2:
                large_got = swap(pair_grads[2][0], "y")

        dprojs = [dprojs[pair] for pair in range(3)]
        if fast:
            half = width // 2
            block = width // BLOCKS
            large_got, small_sent, up_near = after((large_got, small_sent, up_near), pair_grads[0])
            up_grad = sum_near(*up_near)
            small = small[:half] + small_sent.astype(F32)
            small_near = send_near(small.reshape(-1, block, small.shape[1]), near)
            large = pair_grads[0][0].astype(F32) + large_got.astype(F32)
            large_sent = swap(large[half:].astype(BF16), low)
            dprojs = after(dprojs, large, small)
        got = swap(project(dprojs, weights, 1, 0, BF16), "core")
        own = project(dprojs, weights, 0, 0, F32)
        input_grad, last_sums = by_rows(
            last_kernel, "last", [layer_input, own, got, hidden_grad], vectors, [F32], True
        )
        if not fast:
            own, other = (
                natural(jnp.concatenate(p, axis=1))
                for p in (
                    (pair_grads[1][0], pair_grads[0][0]),
                    (pair_grads[1][1], pair_grads[2][0]),
                )
            )
            attn_grad = scatter_rows(own, other, rows)
            small, large = attn_grad[:, : 4 * d], attn_grad[:, 4 * d :]

        own, other = [], []
        for kind in (0, 2):
            at = 2 * d * kind
            own += [pair_sums[0][0, at : at + 2 * d], pair_sums[1][0, at : at + d]]
            other += [pair_sums[2][0, at : at + 2 * d], pair_sums[1][0, at + d : at + 2 * d]]
        pad = [jnp.zeros((width - 2 * side,), F32)]
        row_of = lambda parts: jnp.concatenate(parts + pad).reshape(1, width)
        common = jnp.concatenate(
            [middle_sums[:4], branch_sums[:1], result_sums[:2], last_sums[:2]], axis=0
        )
        common = common + swap(common, "core")
        if fast:
            large = large[:half] + after(large_sent, common).astype(F32)
            large_near = send_near(large.reshape(-1, block, large.shape[1]), near)
            small, large = sum_near(*small_near), sum_near(*large_near)
        own = jnp.concatenate([common, row_of(own), up_sums[:1]], axis=0)
        other = jnp.concatenate([common, row_of(other), up_sums[1:2]], axis=0)
        sums = own + swap(other, "y")
        for axis in reversed(rows):
            sums = sums + swap(sums, axis)
        kinds = [
            jnp.concatenate(
                [large[:, 2 * d * kind : 2 * d * (kind + 1)], small[:, d * kind : d * (kind + 1)]],
                axis=1,
            )
            for kind in range(4)
        ]
        qkv_grad = jnp.stack(kinds[:3], axis=1)
        output_grad = kinds[3]

        entry_count = tokens * 2 ** (len(rows) + 2) * width
        squares = jnp.sum(sums[4:7], axis=1) / entry_count
        rms_values = jnp.sqrt(jnp.stack([squares[1], squares[0], squares[2]]))
        return (
            layer_output,
            input_grad,
            sums[7],
            sums[8],
            qkv_grad,
            sums[9, : 2 * side].reshape(2, side),
            output_grad,
            sums[2],
            sums[0],
            sums[1],
            up_grad,
            sums[10],
            down_grad,
            sums[3],
            rms_values,
        )

    return local


def solution(mesh):
    row_size, col_size = mesh.shape["row"], mesh.shape["col"]
    bits = row_size.bit_length() - 1
    rows = tuple(f"r{b}" for b in reversed(range(bits)))
    cube = Mesh(mesh.devices.reshape((2,) * bits + (col_size // 2, 2)), rows + ("y", "core"))
    col = ("y", "core")
    every = rows + col
    placed = (
        P(every, None),
        P(),
        P(),
        P(rows, None, col),
        P(None, col),
        P(rows, col),
        P(),
        P(),
        P(),
        P(rows, col),
        P(col),
        P(rows, col),
        P(),
        P(every, None),
    )
    return jax.shard_map(
        make_local(rows),
        mesh=cube,
        in_specs=placed,
        out_specs=(
            P(every, None),
            P(every, None),
            P(),
            P(),
            P(rows, None, col),
            P(None, col),
            P(rows, col),
            P(),
            P(),
            P(),
            P(rows, col),
            P(col),
            P(rows, col),
            P(),
            P(),
        ),
        check_vma=False,
    )
```

```python
import math
from functools import partial

import jax
import jax.numpy as jnp
from jax import lax
from jax.experimental import pallas as pl
from jax.experimental.pallas import tpu as pltpu
from jax.sharding import Mesh, PartitionSpec as P

HEAD_DIM = 64
EPSILON = 1e-06
SWAP = [(0, 1), (1, 0)]
LOG2E = math.log2(math.e)
BF16 = jnp.bfloat16
F32 = jnp.float32
VMEM_BYTES = 16 * 2**20


def call(kernel, **kwargs):
    params = pltpu.CompilerParams(vmem_limit_bytes=VMEM_BYTES)
    return pl.pallas_call(kernel, compiler_params=params, **kwargs)


def cost(flops, bytes_accessed, transcendentals):
    return pl.CostEstimate(flops=0, bytes_accessed=0, transcendentals=0)


def after(arrays, *others):
    return lax.optimization_barrier((arrays, others))[0]


def table_of(*vectors):
    row = lax.broadcasted_iota(jnp.int32, (8, vectors[0].shape[0]), 0)
    out = jnp.zeros(row.shape, F32)
    for i, v in enumerate(vectors):
        out = jnp.where(row == i, v[None, :], out)
    return out


def swap(array, axis):
    return lax.ppermute(array, axis, SWAP)


def dot_nn(left, right):
    return lax.dot_general(left, right, (((1,), (0,)), ((), ())), preferred_element_type=F32)


def dot_nt(left, right):
    return lax.dot_general(left, right, (((1,), (1,)), ((), ())), preferred_element_type=F32)


def dot_tn(left, right):
    return lax.dot_general(left, right, (((0,), (0,)), ((), ())), preferred_element_type=F32)


def xor_exchange(blocks_of, axes):
    got = {}
    count = len(axes)
    sizes = [2] * count
    for bits in range(1, 2**count):
        perm = [(i, i ^ bits) for i in range(math.prod(sizes))]
        got[bits] = lax.ppermute(blocks_of(bits), axes, perm)
    return got


def in_order(own, got, axes):
    parts = [own] + [got[bits] for bits in range(1, 2 ** len(axes))]
    for depth, axis in enumerate(reversed(axes)):
        bit = 2**depth
        flip = lax.axis_index(axis) == 1
        parts = [jnp.where(flip, parts[i ^ bit], parts[i]) for i in range(len(parts))]
    return jnp.stack(parts)


def pair_in_order(own, other, axis, dim):
    flip = lax.axis_index(axis) == 1
    return jnp.stack([jnp.where(flip, other, own), jnp.where(flip, own, other)], axis=dim)


def gather_rows(shard, rows):
    low, high = rows[-1], rows[:-1]
    n, c = shard.shape
    near = high[-2:]
    stack = in_order(shard, xor_exchange(lambda bits: shard, near), near)
    for axis in reversed(high[:-2]):
        other = swap(stack, axis)
        stack = pair_in_order(stack, other, axis, 0).reshape(-1, n, c)
    half = c // 2
    first, second = stack[:, :, :half], stack[:, :, half:]
    first_low, second_y = swap(first, low), swap(second, "y")
    first = pair_in_order(first, first_low, low, 1).reshape(-1, half)
    first_y = swap(first, "y")
    second_low = swap(jnp.stack([second, second_y]), low)
    second_own = pair_in_order(second, second_low[0], low, 1).reshape(-1, half)
    second_other = pair_in_order(second_y, second_low[1], low, 1).reshape(-1, half)
    return (
        jnp.concatenate([first, second_own], axis=1),
        jnp.concatenate([first_y, second_other], axis=1),
    )


def pick(array, axis, dim, other):
    zero = lax.index_in_dim(array, 0, dim, keepdims=False)
    one = lax.index_in_dim(array, 1, dim, keepdims=False)
    flip = lax.axis_index(axis) == (0 if other else 1)
    return jnp.where(flip, one, zero)


def scatter_rows(own, other, rows):
    low, high = rows[-1], rows[:-1]
    near = high[-2:]
    total = 2 ** len(rows)
    n, c = own.shape[0] // total, own.shape[1]
    half = c // 2
    own = own.reshape(total // 2, 2, n, c)
    other = other.reshape(total // 2, 2, n, c)
    a_own, a_other = own[..., :half], other[..., :half]
    b_own, b_other = own[..., half:], other[..., half:]
    a_got = swap(a_other, "y")
    b_send = jnp.stack([pick(b_own, low, 1, True), pick(b_other, low, 1, True)])
    b_got = swap(b_send, low)
    a_sum = a_own.astype(F32) + a_got.astype(F32)
    a_send = pick(a_sum, low, 1, True).astype(BF16)
    b_own = pick(b_own, low, 1, False).astype(F32) + b_got[0].astype(F32)
    b_other = (pick(b_other, low, 1, False).astype(F32) + b_got[1].astype(F32)).astype(BF16)
    a_got = swap(a_send, low)
    b_got = swap(b_other, "y")
    a_sum = pick(a_sum, low, 1, False) + a_got.astype(F32)
    b_sum = b_own + b_got.astype(F32)
    both = jnp.concatenate([a_sum, b_sum], axis=2)
    for axis in high[:-2]:
        both = both.reshape(2, -1, n, c)
        got = swap(pick(both, axis, 0, True).astype(BF16), axis)
        both = pick(both, axis, 0, False) + got.astype(F32)
    low_both = both.astype(BF16)
    place = lax.axis_index(near)
    take = lambda bits: lax.dynamic_index_in_dim(low_both, place ^ bits, 0, keepdims=False)
    got = xor_exchange(take, near)
    out = lax.dynamic_index_in_dim(both, place, 0, keepdims=False)
    for piece in got.values():
        out = out + piece.astype(F32)
    return out


BLOCKS = 8


def gather_near(shard, near):
    got = xor_exchange(lambda bits: shard, near)
    return [shard] + [got[bits] for bits in range(1, 2 ** len(near))]


def gather_far(stack, low):
    return stack, swap(stack, low), swap(stack, "y")


def gather_corners(far, low):
    stack, from_low, from_y = far
    half = stack.shape[0] // 2
    return (*far, swap(from_low[:half], "y"), swap(from_y[half:], low))


def gather_plain(shard, rows):
    pieces = []
    for side in gather_rows(shard, rows):
        width, c = side.shape
        blocks = side.reshape(BLOCKS // 2, 2, width // BLOCKS, c)
        pieces += [blocks[:, 0], blocks[:, 1]]
    half = BLOCKS // 4
    return (*pieces[:3], pieces[3][:half], pieces[3][half:])


def reduce_corners(parts, low):
    return swap(parts[3], "y"), swap(parts[4], low)


def reduce_far(parts, got, low):
    _, to_low, to_y, _, _ = parts
    half = to_low.shape[0] // 2
    add = lambda a, b: (a.astype(F32) + b.astype(F32)).astype(BF16)
    to_low = jnp.concatenate([add(to_low[:half], got[0]), to_low[half:]])
    to_y = jnp.concatenate([to_y[:half], add(to_y[half:], got[1])])
    return swap(to_low, low), swap(to_y, "y")


def send_near(stack, near):
    low = stack.astype(BF16)
    return stack[0], xor_exchange(lambda bits: low[bits], near)


def sum_near(own, got):
    for piece in got.values():
        own = own + piece.astype(F32)
    return own


def here(rows):
    if rows is None:
        return 0, 0
    return lax.axis_index(rows[:-1]), lax.axis_index(rows[-1])


def flip(at, by):
    return by if isinstance(at, int) else lax.bitwise_xor(at, by)


def slot_of(rows, block):
    z, x = here(rows)
    block_z, block_x = divmod(block, 2)
    return flip(x, block_x) * (BLOCKS // 2) + flip(z, block_z)


def whole(shape):
    return pl.BlockSpec(shape, lambda *_: (0,) * len(shape))


def side_pieces(raw, sides):
    return [p for side in sides for p in (raw[:2] if side == 0 else raw[2:])]


def put_together(rows, refs, out_ref, source=slice(None), target=slice(None)):
    z, x = here(rows)
    at = 0
    for ref, x_flip in zip(refs, (0, 1, 1)):
        for k in range(ref.shape[0]):
            n = ref.shape[1]
            slot = k + (at if x_flip else 0)
            row = (flip(z, slot) * 2 + flip(x, x_flip)) * n
            out_ref[pl.ds(pl.multiple_of(row, n), n), target] = ref[k, :, source]
        at += ref.shape[0] * x_flip


def turn_kernel(rows, a_ref, b_ref, out_ref):
    tokens, width = a_ref.shape
    n = width // BLOCKS
    for half, ref in enumerate((a_ref, b_ref)):
        turned = ref[...].T
        for block in range(BLOCKS):
            at = pl.multiple_of(slot_of(rows, block) * n, n)
            out_ref[pl.ds(at, n), half * tokens : (half + 1) * tokens] = turned[
                block * n : (block + 1) * n, :
            ]


def turn(a, b, rows):
    tokens, width = a.shape
    return call(
        partial(turn_kernel, rows),
        out_shape=jax.ShapeDtypeStruct((width, 2 * tokens), BF16),
        cost_estimate=cost(
            flops=0, bytes_accessed=8 * tokens * width, transcendentals=0
        ),
        name="turn",
    )(a, b)


GRAD_PARTS = {0: (2, 2), 1: (2, 4, 4)}


def store_parts(grads, refs):
    at = 0
    for ref in refs:
        ref[...] = grads[at : at + ref.shape[0]].astype(BF16)
        at += ref.shape[0]


def grad_shapes(width, c):
    return [jax.ShapeDtypeStruct((width // f, c), BF16) for side in (0, 1) for f in GRAD_PARTS[side]]


def pair_sources(pair):
    return {0: [(0, 0, 2)], 1: [(0, 2, 1), (1, 2, 1)], 2: [(1, 0, 2)]}[pair]


Q_BIAS, V_BIAS, UP_BIAS = range(3)


def attend_forward_kernel(rows, pair, *refs):
    *refs, q_ref, k_ref, v_ref, w_ref, mixed_ref, lse_ref, vt_ref = refs
    xa_ref, xb_ref, *raw, own_ref, other_ref = refs
    raw = {0: [raw], 1: [raw[:2], raw[2:]], 2: [raw]}[pair]
    d = HEAD_DIM
    two = 2 * d
    tokens = xa_ref.shape[0]
    step = pl.program_id(0)
    block = mixed_ref.shape[0]

    @pl.when(step == 0)
    def _():
        for kind in range(4):
            at = kind * two
            for pieces, (_, first, heads) in zip(raw, pair_sources(pair)):
                source = (kind * 3 + first) * d
                put_together(
                    rows,
                    pieces,
                    w_ref,
                    slice(source, source + heads * d),
                    slice(at, at + heads * d),
                )
                at += heads * d
        bias = []
        for row in (Q_BIAS, None, V_BIAS):
            for side, first, heads in pair_sources(pair):
                cols = slice(first * d, (first + heads) * d)
                if row is None:
                    bias.append(jnp.zeros((1, heads * d), F32))
                else:
                    bias.append((own_ref, other_ref)[side][row : row + 1, cols])
        bias = jnp.concatenate(bias, axis=1)
        for half, ref in enumerate((xa_ref, xb_ref)):
            at = slice(half * tokens, (half + 1) * tokens)
            proj = (dot_nn(ref[...], w_ref[:, : 3 * two]) + bias).astype(BF16)
            q_ref[at, :] = proj[:, :two]
            k_ref[at, :] = proj[:, two : 2 * two]
            v_ref[at, :] = proj[:, 2 * two :]
        turned = v_ref[...].T
        for head in range(2):
            vt_ref[head, :d, :] = turned[head * d : (head + 1) * d, :]
            vt_ref[head, d:, :] = jnp.ones((vt_ref.shape[1] - d, turned.shape[1]), BF16)

    query = q_ref[pl.ds(pl.multiple_of(step * block, block), block), :]
    lane = lax.broadcasted_iota(jnp.int32, query.shape, 1)
    outs = []
    for head in range(2):
        masked = jnp.where(lane // d == head, query, jnp.zeros_like(query)) * BF16(d**-0.5)
        scores = dot_nt(k_ref[...], masked)
        top = jnp.max(scores, axis=0, keepdims=True)
        weights = jnp.exp2((scores - top) * LOG2E).astype(BF16)
        out = dot_nn(vt_ref[head], weights)
        total = out[d : d + 1, :]
        outs.append(out[:d, :] * (1.0 / total))
        lse_ref[head : head + 1, :] = top + jnp.log(total)
    mixed_ref[...] = jnp.concatenate(outs, axis=0).T.astype(BF16)


def attend_forward(xa, xb, raw, own, other, rows, pair):
    tokens, width = xa.shape
    seq = 2 * tokens
    two = 2 * HEAD_DIM
    block = 512
    part = jax.ShapeDtypeStruct((seq, two), BF16)
    weight = jax.ShapeDtypeStruct((width, 4 * two), BF16)
    ins = [xa, xb, *side_pieces(raw, [side for side, *_ in pair_sources(pair)]), own, other]
    return call(
        partial(attend_forward_kernel, rows, pair),
        grid=(seq // block,),
        in_specs=[whole(a.shape) for a in ins],
        out_specs=[
            whole(part.shape),
            whole(part.shape),
            whole(part.shape),
            whole(weight.shape),
            pl.BlockSpec((block, two), lambda i: (i, 0)),
            pl.BlockSpec((8, block), lambda i: (0, i)),
        ],
        out_shape=[part, part, part, weight, part, jax.ShapeDtypeStruct((8, seq), F32)],
        scratch_shapes=[pltpu.VMEM((2, HEAD_DIM + 16, seq), BF16)],
        cost_estimate=cost(
            flops=24 * seq * seq * two, bytes_accessed=16 * seq * width, transcendentals=seq * seq
        ),
        name=f"attend_forward_{pair}",
    )(*ins)


def attend_backward_kernel(rows, pair, *refs):
    q_ref, k_ref, v_ref, w_ref, ga_ref, gb_ref, turned_ref, mixed_ref, lse_ref = refs[:9]
    kt_ref, dk_acc, dv_acc, gmix_ref, gall_ref, out_ref = refs[-6:]
    *grads_refs, dproj_ref, sum_ref = refs[9:-6]
    step = pl.program_id(0)
    d = HEAD_DIM
    two = 2 * d
    scale = d**-0.5
    tokens = ga_ref.shape[0]
    block = lse_ref.shape[1]

    @pl.when(step == 0)
    def _():
        kt_ref[...] = k_ref[...].T
        dk_acc[...] = jnp.zeros_like(dk_acc)
        dv_acc[...] = jnp.zeros_like(dv_acc)
        for half, ref in enumerate((ga_ref, gb_ref)):
            at = slice(half * tokens, (half + 1) * tokens)
            gall_ref[at, :] = ref[...]
            gmix_ref[at, :] = dot_nn(ref[...], w_ref[:, 3 * two :]).astype(BF16)

    here_rows = pl.ds(pl.multiple_of(step * block, block), block)
    query = q_ref[here_rows, :]
    grad = gmix_ref[here_rows, :]
    lane = lax.broadcasted_iota(jnp.int32, query.shape, 1)
    dots = (grad.astype(F32) * mixed_ref[here_rows, :].astype(F32)).T
    dqs = []
    for head in range(2):
        mine = lane // d == head
        query_h = jnp.where(mine, query, jnp.zeros_like(query))
        grad_h = jnp.where(mine, grad, jnp.zeros_like(grad))
        row_dots = jnp.sum(dots[head * d : (head + 1) * d, :], axis=0, keepdims=True)
        log_total = lse_ref[head : head + 1, :] * LOG2E
        scores = dot_nt(k_ref[...], query_h * BF16(scale))
        probs = jnp.exp2(scores * LOG2E - log_total)
        grad_probs = dot_nt(v_ref[...], grad_h)
        grad_scores = (probs * (grad_probs - row_dots)).astype(BF16)
        dv_acc[...] += dot_nn(probs.astype(BF16), grad_h)
        dk_acc[...] += dot_nn(grad_scores, query_h)
        dqs.append(dot_nn(kt_ref[head * d : (head + 1) * d, :], grad_scores) * scale)
    dproj_ref[here_rows, :two] = jnp.concatenate(dqs, axis=0).T.astype(BF16)

    @pl.when(step == pl.num_programs(0) - 1)
    def _():
        dproj_ref[:, two : 2 * two] = (dk_acc[...] * scale).astype(BF16)
        dproj_ref[:, 2 * two :] = dv_acc[...].astype(BF16)
        dproj = dproj_ref[...]
        sum_ref[0:1, :] = jnp.sum(dproj.astype(F32), axis=0, keepdims=True)
        out_ref[:, : 3 * two] = dot_nn(turned_ref[...], dproj).astype(BF16)
        grads = dot_nn(mixed_ref[...].T, gall_ref[...]).T.astype(BF16)
        n = grads.shape[0] // BLOCKS
        for at_block in range(BLOCKS):
            at = pl.multiple_of(slot_of(rows, at_block) * n, n)
            out_ref[pl.ds(at, n), 3 * two :] = grads[at_block * n : (at_block + 1) * n, :]
        if pair != 1:
            store_parts(out_ref[...], grads_refs)
        else:
            for kind in range(4):
                for side, ref in enumerate(grads_refs):
                    ref[:, kind * d : (kind + 1) * d] = out_ref[
                        :, kind * two + side * d : kind * two + (side + 1) * d
                    ]


def attend_backward(q, k, v, w, ga, gb, turned, mixed, lse, rows, pair):
    seq, two = q.shape
    width = ga.shape[1]
    block = 256
    grads = (width, 2 * two) if pair == 1 else (width // 2, 4 * two)
    outs = [jax.ShapeDtypeStruct(grads, BF16)] * 2 + [
        jax.ShapeDtypeStruct((seq, 3 * two), BF16),
        jax.ShapeDtypeStruct((8, 3 * two), F32),
    ]
    ins = [q, k, v, w, ga, gb, turned, mixed]
    *grads, dproj, sums = call(
        partial(attend_backward_kernel, rows, pair),
        grid=(seq // block,),
        in_specs=[whole(a.shape) for a in ins] + [pl.BlockSpec((8, block), lambda i: (0, i))],
        out_specs=[whole(o.shape) for o in outs],
        out_shape=outs,
        scratch_shapes=[
            pltpu.VMEM((two, seq), BF16),
            pltpu.VMEM((seq, two), F32),
            pltpu.VMEM((seq, two), F32),
            pltpu.VMEM((seq, two), BF16),
            pltpu.VMEM((seq, width), BF16),
            pltpu.VMEM((width, 4 * two), BF16),
        ],
        cost_estimate=cost(
            flops=50 * seq * seq * two, bytes_accessed=16 * seq * width, transcendentals=seq * seq
        ),
        name=f"attend_backward_{pair}",
    )(*ins, lse)
    return grads, dproj, sums


def project_kernel(first, cols, *refs):
    count = (len(refs) - 1) // 2
    total = 0.0
    for part, weight in zip(refs[:count], refs[count:-1]):
        total = total + dot_nt(part[...], weight[...])
    refs[-1][...] = total.astype(refs[-1].dtype)


def project(parts, weights, half, first, dtype):
    seq, cols = parts[0].shape
    width = weights[0].shape[0]
    tokens = seq // 2
    return call(
        partial(project_kernel, first, cols),
        grid=(1,),
        in_specs=[pl.BlockSpec((tokens, cols), lambda i: (half, 0)) for _ in parts]
        + [pl.BlockSpec((width, cols), lambda i: (0, first // cols)) for _ in weights],
        out_specs=whole((tokens, width)),
        out_shape=jax.ShapeDtypeStruct((tokens, width), dtype),
        cost_estimate=cost(
            flops=2 * tokens * width * cols * 3, bytes_accessed=0, transcendentals=0
        ),
        name="project",
    )(*parts, *weights)


def statistics(rows):
    mean = jnp.mean(rows, axis=1, keepdims=True)
    centered = rows - mean
    inverse = lax.rsqrt(jnp.mean(jnp.square(centered), axis=1, keepdims=True) + EPSILON)
    return centered * inverse, inverse


def add_rows(sum_ref, values):
    @pl.when(pl.program_id(0) == 0)
    def _():
        sum_ref[...] = jnp.zeros_like(sum_ref)

    for i, value in enumerate(values):
        sum_ref[i : i + 1, :] += jnp.sum(value, axis=0, keepdims=True)


ATTN_GAIN, ATTN_SHIFT, MLP_GAIN, MLP_SHIFT, OUTPUT_BIAS, DOWN_BIAS = range(6)


def vector(ref, at):
    return ref[at : at + 1, :]


def norm_kernel(x_ref, vec_ref, out_ref):
    hat, _ = statistics(x_ref[...].astype(F32))
    out_ref[...] = (hat * vector(vec_ref, ATTN_GAIN) + vector(vec_ref, ATTN_SHIFT)).astype(BF16)


def resid_kernel(x_ref, own_ref, got_ref, vec_ref, resid_ref, out_ref, sum_ref):
    branch = own_ref[...] + got_ref[...].astype(F32) + vector(vec_ref, OUTPUT_BIAS)
    resid = x_ref[...].astype(F32) + branch
    resid_ref[...] = resid
    hat, _ = statistics(resid)
    out_ref[...] = (hat * vector(vec_ref, MLP_GAIN) + vector(vec_ref, MLP_SHIFT)).astype(BF16)
    add_rows(sum_ref, [branch * branch])


def result_kernel(resid_ref, own_ref, got_ref, vec_ref, out_ref, sum_ref):
    branch = own_ref[...] + got_ref[...].astype(F32) + vector(vec_ref, DOWN_BIAS)
    result = resid_ref[...] + branch
    out_ref[...] = result.astype(BF16)
    add_rows(sum_ref, [result * result, branch * branch])


def norm_gradient(grad, rows, gain):
    hat, inverse = statistics(rows)
    grad_hat = grad * gain
    first = jnp.mean(grad_hat, axis=1, keepdims=True)
    second = jnp.mean(grad_hat * hat, axis=1, keepdims=True)
    return inverse * (grad_hat - first - hat * second), grad * hat


def middle_kernel(resid_ref, own_ref, got_ref, cot_ref, vec_ref, grad_ref, low_ref, sum_ref):
    grad = own_ref[...] + got_ref[...].astype(F32)
    back, gains = norm_gradient(grad, resid_ref[...], vector(vec_ref, MLP_GAIN))
    cot = cot_ref[...].astype(F32)
    hidden = cot + back
    grad_ref[...] = hidden
    low = hidden.astype(BF16)
    low_ref[...] = low
    add_rows(sum_ref, [gains, grad, low.astype(F32), cot])


def last_kernel(x_ref, own_ref, got_ref, hidden_ref, vec_ref, grad_ref, sum_ref):
    grad = own_ref[...] + got_ref[...].astype(F32)
    back, gains = norm_gradient(grad, x_ref[...].astype(F32), vector(vec_ref, ATTN_GAIN))
    grad_ref[...] = hidden_ref[...] + back
    add_rows(sum_ref, [gains, grad])


def by_rows(kernel, name, rows, vectors, outs, sums=False):
    tokens, width = rows[0].shape
    block = tokens // 2
    part = pl.BlockSpec((block, width), lambda i: (i, 0))
    out_shape = [jax.ShapeDtypeStruct((tokens, width), t) for t in outs]
    out_specs = [part] * len(outs)
    if sums:
        out_shape.append(jax.ShapeDtypeStruct((8, width), F32))
        out_specs.append(whole((8, width)))
    return call(
        kernel,
        grid=(tokens // block,),
        in_specs=[part] * len(rows) + [whole(vectors.shape)],
        out_specs=out_specs,
        out_shape=out_shape,
        cost_estimate=cost(flops=0, bytes_accessed=0, transcendentals=0),
        name=name,
    )(*rows, vectors)


def gelu_parts(u):
    c0 = math.sqrt(2.0 / math.pi)
    square = u * u
    t = jnp.tanh(u * (c0 + (c0 * 0.044715) * square))
    half = 0.5 * u
    act = half + half * t
    slope = 0.5 + 0.5 * t + half * (1.0 - t * t) * (c0 + (3.0 * c0 * 0.044715) * square)
    return act, slope


def up_kernel(rows, side, *refs):
    xa_ref, xb_ref, turned_ref, *raw, bias_ref, act_ref, slope_ref = refs[: -1 - len(GRAD_PARTS[side])]
    outs, w_ref = refs[-1 - len(GRAD_PARTS[side]) : -1], refs[-1]
    tokens = xa_ref.shape[0]
    put_together(rows, raw, w_ref)
    for half, ref in enumerate((xa_ref, xb_ref)):
        act, slope = gelu_parts(dot_nn(ref[...], w_ref[...]) + vector(bias_ref, UP_BIAS))
        act_ref[half * tokens : (half + 1) * tokens, :] = act.astype(BF16)
        slope_ref[half * tokens : (half + 1) * tokens, :] = slope.astype(BF16)
    store_parts(dot_nn(turned_ref[...], act_ref[...]), outs)


TILE = 256


def tiles(*dims):
    return pl.BlockSpec((*dims, TILE), lambda j: (0,) * len(dims) + (j,))


def raw_tiles(raw):
    return [tiles(*r.shape[:2]) for r in raw]


def up_and_down_grads(xa, xb, turned, raw, bias, rows, side):
    tokens, width = xa.shape
    c = bias.shape[1]
    hidden = jax.ShapeDtypeStruct((2 * tokens, c), BF16)
    grads = [jax.ShapeDtypeStruct((width // f, c), BF16) for f in GRAD_PARTS[side]]
    raw = side_pieces(raw, [side])
    act, slope, *grads = call(
        partial(up_kernel, rows, side),
        grid=(c // TILE,),
        in_specs=[whole(xa.shape), whole(xb.shape), whole(turned.shape)]
        + raw_tiles(raw)
        + [tiles(8)],
        out_specs=[tiles(2 * tokens)] * 2 + [tiles(g.shape[0]) for g in grads],
        out_shape=[hidden] * 2 + grads,
        scratch_shapes=[pltpu.VMEM((width, TILE), BF16)],
        cost_estimate=cost(
            flops=8 * tokens * width * c, bytes_accessed=0, transcendentals=2 * tokens * c
        ),
        name=f"up_and_down_grads_{side}",
    )(xa, xb, turned, *raw, bias)
    return act, slope, grads


def hidden_back_kernel(rows, side, *refs):
    ga_ref, gb_ref, *raw = refs[: 6 + 2 * side]
    down, up = raw[: len(raw) // 2], raw[len(raw) // 2 :]
    slope_ref, *before, pre_ref, sum_ref = refs[6 + 2 * side : 9 + 3 * side]
    *outs, acc_ref, w_ref, u_ref = refs[9 + 3 * side :]
    step = pl.program_id(0)
    tokens = ga_ref.shape[0]

    @pl.when(step == 0)
    def _():
        acc_ref[...] = before[0][...] if side else jnp.zeros_like(acc_ref)

    put_together(rows, down, w_ref)
    put_together(rows, up, u_ref)
    totals = 0.0
    for half, ref in enumerate((ga_ref, gb_ref)):
        at = slice(half * tokens, (half + 1) * tokens)
        back = dot_nn(ref[...], w_ref[...]) * slope_ref[at, :].astype(F32)
        pre = back.astype(BF16)
        pre_ref[at, :] = pre
        totals = totals + jnp.sum(pre.astype(F32), axis=0, keepdims=True)
        acc_ref[at, :] += dot_nt(pre, u_ref[...])
    sum_ref[0:1, :] = totals

    @pl.when(step == pl.num_programs(0) - 1)
    def _():
        if side:
            outs[0][...] = acc_ref[:tokens, :]
            outs[1][...] = acc_ref[tokens:, :].astype(BF16)
        else:
            outs[0][...] = acc_ref[...]


def hidden_back(ga, gb, down, up, slope, before, rows, side):
    tokens, width = ga.shape
    seq, c = slope.shape
    if side:
        backs = [jax.ShapeDtypeStruct(ga.shape, t) for t in (F32, BF16)]
    else:
        backs = [jax.ShapeDtypeStruct((seq, width), F32)]
    return call(
        partial(hidden_back_kernel, rows, side),
        grid=(c // TILE,),
        in_specs=[whole(ga.shape), whole(gb.shape)]
        + raw_tiles(down)
        + raw_tiles(up)
        + [tiles(seq)]
        + [whole(b.shape) for b in before],
        out_specs=[tiles(seq), tiles(8)] + [whole(b.shape) for b in backs],
        out_shape=[jax.ShapeDtypeStruct((seq, c), BF16), jax.ShapeDtypeStruct((8, c), F32)] + backs,
        scratch_shapes=[
            pltpu.VMEM((seq, width), F32),
            pltpu.VMEM((width, TILE), BF16),
            pltpu.VMEM((width, TILE), BF16),
        ],
        cost_estimate=cost(
            flops=8 * tokens * width * c, bytes_accessed=12 * tokens * c, transcendentals=0
        ),
        name=f"hidden_back_{side}",
    )(ga, gb, *down, *up, slope, *before)


def mlp_out_kernel(rows, *refs):
    act_ref, act_o_ref = refs[:2]
    down = refs[2:7]
    own_ref, other_ref, acc_ref, w_ref = refs[7:]
    step = pl.program_id(0)
    tokens = own_ref.shape[0]

    @pl.when(step == 0)
    def _():
        acc_ref[...] = jnp.zeros_like(acc_ref)

    put_together(rows, down[:2], w_ref.at[0])
    put_together(rows, down[2:], w_ref.at[1])
    acc_ref[...] += dot_nt(act_ref[...], w_ref[0]) + dot_nt(act_o_ref[...], w_ref[1])

    @pl.when(step == pl.num_programs(0) - 1)
    def _():
        own_ref[...] = acc_ref[:tokens, :]
        other_ref[...] = acc_ref[tokens:, :].astype(BF16)


def mlp_out(act, act_o, down, width, rows):
    seq, c = act.shape
    outs = [jax.ShapeDtypeStruct((seq // 2, width), t) for t in (F32, BF16)]
    return call(
        partial(mlp_out_kernel, rows),
        grid=(c // TILE,),
        in_specs=[tiles(seq)] * 2 + raw_tiles(down),
        out_specs=[whole(o.shape) for o in outs],
        out_shape=outs,
        scratch_shapes=[pltpu.VMEM((seq, width), F32), pltpu.VMEM((2, width, TILE), BF16)],
        cost_estimate=cost(
            flops=4 * seq * width * c, bytes_accessed=4 * seq * c, transcendentals=0
        ),
        name="mlp_out",
    )(act, act_o, *down)


def weight_grads_kernel(turned_ref, g_ref, go_ref, *outs):
    store_parts(dot_nn(turned_ref[...], g_ref[...]), outs[:2])
    store_parts(dot_nn(turned_ref[...], go_ref[...]), outs[2:])


def weight_grads(turned, grad, grad_o):
    width, seq = turned.shape
    c = grad.shape[1]
    return call(
        weight_grads_kernel,
        grid=(c // TILE,),
        in_specs=[whole(turned.shape), tiles(seq), tiles(seq)],
        out_specs=[tiles(s.shape[0]) for s in grad_shapes(width, c)],
        out_shape=grad_shapes(width, c),
        cost_estimate=cost(
            flops=4 * seq * width * c, bytes_accessed=6 * seq * c, transcendentals=0
        ),
        name="weight_grads",
    )(turned, grad, grad_o)


def make_local(rows):
    low, near = rows[-1], rows[:-1]
    fast = 2 ** len(rows) == BLOCKS
    order = rows if fast else None

    def to_blocks(parts):
        width, c = parts[0].shape[0] * 2, parts[0].shape[1]
        return [p.reshape(-1, width // BLOCKS, c) for p in parts]

    def reduce_plain(parts):
        blocks = to_blocks(parts)
        own = jnp.stack(blocks[:2], axis=1)
        other = jnp.stack([blocks[2], jnp.concatenate(blocks[3:])], axis=1)
        width, c = parts[0].shape[0] * 2, parts[0].shape[1]
        return scatter_rows(own.reshape(width, c), other.reshape(width, c), rows)

    def natural(grads):
        width, c = grads.shape
        blocks = grads.reshape(2, BLOCKS // 2, width // BLOCKS, c)
        return jnp.swapaxes(blocks, 0, 1).reshape(width, c)

    def local(
        layer_input,
        attn_gain,
        attn_shift,
        qkv_weight,
        qkv_bias,
        output_weight,
        output_bias,
        mlp_gain,
        mlp_shift,
        up_weight,
        up_bias,
        down_weight,
        down_bias,
        cotangent,
    ):
        tokens, width = layer_input.shape
        n, _, side = qkv_weight.shape
        hidden = up_weight.shape[1]
        d = HEAD_DIM

        attn_shard = jnp.concatenate([qkv_weight.reshape(n, -1), output_weight], axis=1)
        vectors = table_of(attn_gain, attn_shift, mlp_gain, mlp_shift, output_bias, down_bias)
        (attn_in,) = by_rows(norm_kernel, "norm", [layer_input], vectors, [BF16])
        attn_in_other = swap(attn_in, "core")
        cot_other = swap(cotangent, "core")
        bias_own = jnp.pad(qkv_bias, ((0, 6), (0, hidden - side)))
        bias_own = bias_own + jnp.pad(up_bias[None, :], ((UP_BIAS, 7 - UP_BIAS), (0, 0)))
        bias_other = swap(bias_own, "y")
        if fast:
            attn_near = gather_near(attn_shard, near)
            attn_near = after(attn_near, cot_other, bias_other)
            attn_stack = jnp.stack(attn_near)
            mlp_near = gather_near(jnp.stack([up_weight, down_weight]), near)
            attn_far = gather_far(attn_stack, low)
            attn_raw = gather_corners(attn_far, low)
        else:
            attn_raw, up_raw, down_raw = (
                gather_plain(w, rows) for w in (attn_shard, up_weight, down_weight)
            )
        halves = (attn_in, attn_in_other, cotangent, cot_other)
        if fast:
            halves = after(halves, attn_stack)
        attn_turned = turn(*halves[:2], order)
        cot_turned = turn(*halves[2:], order)
        attended = []
        for pair in range(3):
            bias = bias_own
            if fast and pair == 0:
                bias = after(bias, attn_far, attn_turned, cot_turned)
            if pair:
                bias = after(bias, attended[pair - 1][4])
            if fast and pair == 1:
                mlp_near = after(mlp_near, attended[0][4], attn_raw)
                up_far = gather_far(jnp.stack([m[0] for m in mlp_near]), low)
                down_stack = jnp.stack([m[1] for m in mlp_near])
                bias = after(bias, up_far[0], down_stack)
            attended.append(
                attend_forward(attn_in, attn_in_other, attn_raw, bias, bias_other, order, pair)
            )
        mixed = [a[4] for a in attended]
        weights = [a[3] for a in attended]
        if fast:
            mixed, up_far = after((mixed, up_far))
            up_raw = gather_corners(up_far, low)
        got = swap(project(mixed, weights, 1, 6 * d, BF16), "core")
        own = project(mixed, weights, 0, 6 * d, F32)
        hidden_resid, mlp_in, branch_sums = by_rows(
            resid_kernel,
            "resid",
            [layer_input, own, got],
            vectors,
            [F32, BF16],
            True,
        )
        mlp_in_other = swap(mlp_in, "core")
        if fast:
            down_far = gather_far(after(down_stack, mlp_in_other), low)
        ins = (mlp_in, mlp_in_other, cot_turned)
        act, slope, down_own = up_and_down_grads(*ins, up_raw, bias_own, order, 0)
        if fast:
            down_raw = gather_corners(after(down_far, act), low)
        bias_other = after(bias_other, act)
        act_o, slope_o, down_other = up_and_down_grads(*ins, up_raw, bias_other, order, 1)
        down_parts = down_own + down_other
        if fast:
            down_parts = to_blocks(down_parts)
            down_got = reduce_corners(down_parts, low)
        else:
            down_grad = reduce_plain(down_parts)
        grads = (cotangent, cot_other)
        pre, up_sums, back = hidden_back(*grads, down_raw[:2], up_raw[:2], slope, (), order, 0)
        if fast:
            slope_o, down_got = after((slope_o, down_got), pre)
        pre_o, up_sums_o, back, back_other = hidden_back(
            *grads, down_raw[2:], up_raw[2:], slope_o, (back,), order, 1
        )
        back_got = swap(back_other, "core")
        act, act_o = after((act, act_o), pre_o)
        if fast:
            down_sent = reduce_far(down_parts, down_got, low)
        branch, branch_other = mlp_out(act, act_o, down_raw, width, order)
        back = after(back, branch)
        hidden_grad, grad_attn, middle_sums = by_rows(
            middle_kernel,
            "middle",
            [hidden_resid, back, back_got, cotangent],
            vectors,
            [F32, BF16],
            True,
        )
        grad_attn_other = swap(grad_attn, "core")
        branch_got = swap(after(branch_other, grad_attn), "core")
        mlp_turned = turn(*after((mlp_in, mlp_in_other), grad_attn), order)
        up_parts = weight_grads(mlp_turned, pre, pre_o)
        resid, branch, branch_got = after((hidden_resid, branch, branch_got), up_parts)
        layer_output, result_sums = by_rows(
            result_kernel, "result", [resid, branch, branch_got], vectors, [BF16], True
        )
        if fast:
            up_parts = to_blocks(up_parts)
            up_got = reduce_corners(up_parts, low)
        else:
            up_grad = reduce_plain(up_parts)

        half, block = width // 2, width // BLOCKS
        pair_grads, pair_sums, dprojs = {}, {}, {}
        for pair in (1, 2, 0):
            q, k, v, w, mix, lse = attended[pair]
            if pair == 1:
                lse = after(lse, layer_output)
            if fast and pair == 2:
                lse, up_got, down_sent = after((lse, up_got, down_sent), pair_grads[1])
                up_sent = reduce_far(up_parts, up_got, low)
                total = down_parts[0].astype(F32) + sum(g.astype(F32) for g in down_sent)
                down_sum, down_got = total[:2], swap(total[2:].astype(BF16), near[0])
            if fast and pair == 0:
                lse, down_got, small_got = after((lse, down_got, small_got), pair_grads[2])
                total = down_sum + down_got.astype(F32)
                down_sum, down_got = total[0], swap(total[1].astype(BF16), near[1])
                small = pair_grads[1][0].astype(F32) + small_got.astype(F32)
            pair_grads[pair], dprojs[pair], pair_sums[pair] = attend_backward(
                q, k, v, w, grad_attn, grad_attn_other, attn_turned, mix, lse, order, pair
            )
            if fast and pair == 1:
                small_got = swap(pair_grads[1][1], "y")
            if fast and pair == 2:
                large_got = swap(pair_grads[2][1], low)

        dprojs = [dprojs[pair] for pair in range(3)]
        if fast:
            large_got, down_got, up_sent = after((large_got, down_got, up_sent), pair_grads[0])
            total = up_parts[0].astype(F32) + sum(g.astype(F32) for g in up_sent)
            up_sum, up_got = total[:2], swap(total[2:].astype(BF16), near[0])
            down_grad = down_sum + down_got.astype(F32)
            large_y = (pair_grads[2][0].astype(F32) + large_got.astype(F32)).astype(BF16)
            large_sent = (swap(pair_grads[0][1], low), swap(large_y, "y"))
            small_sent = swap(small[half:].astype(BF16), low)
            dprojs = after(dprojs, large_y)
        got = swap(project(dprojs, weights, 1, 0, BF16), "core")
        own = project(dprojs, weights, 0, 0, F32)
        input_grad, last_sums = by_rows(
            last_kernel, "last", [layer_input, own, got, hidden_grad], vectors, [F32], True
        )
        if not fast:
            own, other = (
                natural(jnp.concatenate(p, axis=1))
                for p in (
                    (jnp.concatenate(pair_grads[0]), pair_grads[1][0]),
                    (jnp.concatenate(pair_grads[2]), pair_grads[1][1]),
                )
            )
            attn_grad = scatter_rows(own, other, rows)

        def bias_row(large, small, at):
            row = 0.0
            for i, kind in enumerate((0, 2)):
                source = 2 * d * kind
                for piece, to in (
                    (large[:1, source : source + 2 * d], 0),
                    (small[:1, source + at : source + at + d], 2 * d),
                ):
                    to = i * side + to
                    row = row + jnp.pad(piece, ((0, 0), (to, width - to - piece.shape[1])))
            return row

        common = jnp.concatenate(
            [middle_sums[:4], branch_sums[:1], result_sums[:2], last_sums[:2]], axis=0
        )
        common = common + swap(common, "core")
        own = jnp.concatenate([common, bias_row(pair_sums[0], pair_sums[1], 0), up_sums[:1]], axis=0)
        other = jnp.concatenate([common, bias_row(pair_sums[2], pair_sums[1], d), up_sums_o[:1]], axis=0)
        sums = own + swap(other, "y")
        if fast:
            large_sent, small_sent = after((large_sent, small_sent), last_sums)
            large = pair_grads[0][0].astype(F32) + sum(g.astype(F32) for g in large_sent)
            small = small[:half] + small_sent.astype(F32)
            both = jnp.concatenate([large, small], axis=1).reshape(-1, block, 12 * d)
            attn_near = send_near(both, near)
            total = up_sum + after(up_got, sums).astype(F32)
            up_grad = total[0] + swap(total[1].astype(BF16), near[1]).astype(F32)
            attn_grad = sum_near(*attn_near)
        for axis in reversed(rows):
            sums = sums + swap(sums, axis)
        kinds = [
            jnp.concatenate(
                [
                    attn_grad[:, 2 * d * kind : 2 * d * (kind + 1)],
                    attn_grad[:, d * (8 + kind) : d * (9 + kind)],
                ],
                axis=1,
            )
            for kind in range(4)
        ]
        qkv_grad = jnp.stack(kinds[:3], axis=1)
        output_grad = kinds[3]

        entry_count = tokens * 2 ** (len(rows) + 2) * width
        squares = jnp.sum(sums[4:7], axis=1) / entry_count
        rms_values = jnp.sqrt(jnp.stack([squares[1], squares[0], squares[2]]))
        return (
            layer_output,
            input_grad,
            sums[7],
            sums[8],
            qkv_grad,
            jnp.concatenate([sums[9:10, :side], sums[9:10, side : 2 * side]]),
            output_grad,
            sums[2],
            sums[0],
            sums[1],
            up_grad,
            sums[10],
            down_grad,
            sums[3],
            rms_values,
        )

    return local


def solution(mesh):
    row_size, col_size = mesh.shape["row"], mesh.shape["col"]
    bits = row_size.bit_length() - 1
    rows = tuple(f"r{b}" for b in reversed(range(bits)))
    cube = Mesh(mesh.devices.reshape((2,) * bits + (col_size // 2, 2)), rows + ("y", "core"))
    col = ("y", "core")
    every = rows + col
    placed = (
        P(every, None),
        P(),
        P(),
        P(rows, None, col),
        P(None, col),
        P(rows, col),
        P(),
        P(),
        P(),
        P(rows, col),
        P(col),
        P(rows, col),
        P(),
        P(every, None),
    )
    return jax.shard_map(
        make_local(rows),
        mesh=cube,
        in_specs=placed,
        out_specs=(
            P(every, None),
            P(every, None),
            P(),
            P(),
            P(rows, None, col),
            P(None, col),
            P(rows, col),
            P(),
            P(),
            P(),
            P(rows, col),
            P(col),
            P(rows, col),
            P(),
            P(),
        ),
        check_vma=False,
    )
```

```python
import math
from functools import partial

import jax
import jax.numpy as jnp
from jax import lax
from jax.experimental import pallas as pl
from jax.experimental.pallas import tpu as pltpu
from jax.sharding import Mesh, PartitionSpec as P

HEAD_DIM = 64
EPSILON = 1e-06
SWAP = [(0, 1), (1, 0)]
LOG2E = math.log2(math.e)
BF16 = jnp.bfloat16
F32 = jnp.float32
VMEM_BYTES = 16 * 2**20


def call(kernel, **kwargs):
    params = pltpu.CompilerParams(vmem_limit_bytes=VMEM_BYTES)
    return pl.pallas_call(kernel, compiler_params=params, **kwargs)


def cost(flops, bytes_accessed, transcendentals):
    return pl.CostEstimate(flops=0, bytes_accessed=0, transcendentals=0)


def after(arrays, *others):
    return lax.optimization_barrier((arrays, others))[0]


def table_of(*vectors):
    row = lax.broadcasted_iota(jnp.int32, (8, vectors[0].shape[0]), 0)
    out = jnp.zeros(row.shape, F32)
    for i, v in enumerate(vectors):
        out = jnp.where(row == i, v[None, :], out)
    return out


def swap(array, axis):
    return lax.ppermute(array, axis, SWAP)


def dot_nn(left, right):
    return lax.dot_general(left, right, (((1,), (0,)), ((), ())), preferred_element_type=F32)


def dot_nt(left, right):
    return lax.dot_general(left, right, (((1,), (1,)), ((), ())), preferred_element_type=F32)


def dot_tn(left, right):
    return lax.dot_general(left, right, (((0,), (0,)), ((), ())), preferred_element_type=F32)


def xor_exchange(blocks_of, axes):
    got = {}
    count = len(axes)
    sizes = [2] * count
    for bits in range(1, 2**count):
        perm = [(i, i ^ bits) for i in range(math.prod(sizes))]
        got[bits] = lax.ppermute(blocks_of(bits), axes, perm)
    return got


def in_order(own, got, axes):
    parts = [own] + [got[bits] for bits in range(1, 2 ** len(axes))]
    for depth, axis in enumerate(reversed(axes)):
        bit = 2**depth
        flip = lax.axis_index(axis) == 1
        parts = [jnp.where(flip, parts[i ^ bit], parts[i]) for i in range(len(parts))]
    return jnp.stack(parts)


def pair_in_order(own, other, axis, dim):
    flip = lax.axis_index(axis) == 1
    return jnp.stack([jnp.where(flip, other, own), jnp.where(flip, own, other)], axis=dim)


def gather_rows(shard, rows):
    low, high = rows[-1], rows[:-1]
    n, c = shard.shape
    near = high[-2:]
    stack = in_order(shard, xor_exchange(lambda bits: shard, near), near)
    for axis in reversed(high[:-2]):
        other = swap(stack, axis)
        stack = pair_in_order(stack, other, axis, 0).reshape(-1, n, c)
    half = c // 2
    first, second = stack[:, :, :half], stack[:, :, half:]
    first_low, second_y = swap(first, low), swap(second, "y")
    first = pair_in_order(first, first_low, low, 1).reshape(-1, half)
    first_y = swap(first, "y")
    second_low = swap(jnp.stack([second, second_y]), low)
    second_own = pair_in_order(second, second_low[0], low, 1).reshape(-1, half)
    second_other = pair_in_order(second_y, second_low[1], low, 1).reshape(-1, half)
    return (
        jnp.concatenate([first, second_own], axis=1),
        jnp.concatenate([first_y, second_other], axis=1),
    )


def pick(array, axis, dim, other):
    zero = lax.index_in_dim(array, 0, dim, keepdims=False)
    one = lax.index_in_dim(array, 1, dim, keepdims=False)
    flip = lax.axis_index(axis) == (0 if other else 1)
    return jnp.where(flip, one, zero)


def scatter_rows(own, other, rows):
    low, high = rows[-1], rows[:-1]
    near = high[-2:]
    total = 2 ** len(rows)
    n, c = own.shape[0] // total, own.shape[1]
    half = c // 2
    own = own.reshape(total // 2, 2, n, c)
    other = other.reshape(total // 2, 2, n, c)
    a_own, a_other = own[..., :half], other[..., :half]
    b_own, b_other = own[..., half:], other[..., half:]
    a_got = swap(a_other, "y")
    b_send = jnp.stack([pick(b_own, low, 1, True), pick(b_other, low, 1, True)])
    b_got = swap(b_send, low)
    a_sum = a_own.astype(F32) + a_got.astype(F32)
    a_send = pick(a_sum, low, 1, True).astype(BF16)
    b_own = pick(b_own, low, 1, False).astype(F32) + b_got[0].astype(F32)
    b_other = (pick(b_other, low, 1, False).astype(F32) + b_got[1].astype(F32)).astype(BF16)
    a_got = swap(a_send, low)
    b_got = swap(b_other, "y")
    a_sum = pick(a_sum, low, 1, False) + a_got.astype(F32)
    b_sum = b_own + b_got.astype(F32)
    both = jnp.concatenate([a_sum, b_sum], axis=2)
    for axis in high[:-2]:
        both = both.reshape(2, -1, n, c)
        got = swap(pick(both, axis, 0, True).astype(BF16), axis)
        both = pick(both, axis, 0, False) + got.astype(F32)
    low_both = both.astype(BF16)
    place = lax.axis_index(near)
    take = lambda bits: lax.dynamic_index_in_dim(low_both, place ^ bits, 0, keepdims=False)
    got = xor_exchange(take, near)
    out = lax.dynamic_index_in_dim(both, place, 0, keepdims=False)
    for piece in got.values():
        out = out + piece.astype(F32)
    return out


BLOCKS = 8


def gather_near(shard, near):
    got = xor_exchange(lambda bits: shard, near)
    return [shard] + [got[bits] for bits in range(1, 2 ** len(near))]


def gather_far(stack, low):
    return stack, swap(stack, low), swap(stack, "y")


def gather_corners(far, low):
    stack, from_low, from_y = far
    half = stack.shape[0] // 2
    return (*far, swap(from_low[:half], "y"), swap(from_y[half:], low))


def gather_plain(shard, rows):
    pieces = []
    for side in gather_rows(shard, rows):
        width, c = side.shape
        blocks = side.reshape(BLOCKS // 2, 2, width // BLOCKS, c)
        pieces += [blocks[:, 0], blocks[:, 1]]
    half = BLOCKS // 4
    return (*pieces[:3], pieces[3][:half], pieces[3][half:])


def reduce_corners(parts, low):
    return swap(parts[3], "y"), swap(parts[4], low)


def reduce_far(parts, got, low):
    _, to_low, to_y, _, _ = parts
    half = to_low.shape[0] // 2
    add = lambda a, b: (a.astype(F32) + b.astype(F32)).astype(BF16)
    to_low = jnp.concatenate([add(to_low[:half], got[0]), to_low[half:]])
    to_y = jnp.concatenate([to_y[:half], add(to_y[half:], got[1])])
    return swap(to_low, low), swap(to_y, "y")


def send_near(stack, near):
    low = stack.astype(BF16)
    return stack[0], xor_exchange(lambda bits: low[bits], near)


def sum_near(own, got):
    for piece in got.values():
        own = own + piece.astype(F32)
    return own


def here(rows):
    if rows is None:
        return 0, 0
    return lax.axis_index(rows[:-1]), lax.axis_index(rows[-1])


def flip(at, by):
    return by if isinstance(at, int) else lax.bitwise_xor(at, by)


def slot_of(rows, block):
    z, x = here(rows)
    block_z, block_x = divmod(block, 2)
    return flip(x, block_x) * (BLOCKS // 2) + flip(z, block_z)


def whole(shape):
    return pl.BlockSpec(shape, lambda *_: (0,) * len(shape))


def side_pieces(raw, sides):
    return [p for side in sides for p in (raw[:2] if side == 0 else raw[2:])]


def put_together(rows, refs, out_ref, source=slice(None), target=slice(None)):
    z, x = here(rows)
    at = 0
    for ref, x_flip in zip(refs, (0, 1, 1)):
        for k in range(ref.shape[0]):
            n = ref.shape[1]
            slot = k + (at if x_flip else 0)
            row = (flip(z, slot) * 2 + flip(x, x_flip)) * n
            out_ref[pl.ds(pl.multiple_of(row, n), n), target] = ref[k, :, source]
        at += ref.shape[0] * x_flip


def turn_kernel(rows, a_ref, b_ref, out_ref):
    tokens, width = a_ref.shape
    n = width // BLOCKS
    for half, ref in enumerate((a_ref, b_ref)):
        turned = ref[...].T
        for block in range(BLOCKS):
            at = pl.multiple_of(slot_of(rows, block) * n, n)
            out_ref[pl.ds(at, n), half * tokens : (half + 1) * tokens] = turned[
                block * n : (block + 1) * n, :
            ]


def turn(a, b, rows):
    tokens, width = a.shape
    return call(
        partial(turn_kernel, rows),
        out_shape=jax.ShapeDtypeStruct((width, 2 * tokens), BF16),
        cost_estimate=cost(
            flops=0, bytes_accessed=8 * tokens * width, transcendentals=0
        ),
        name="turn",
    )(a, b)


GRAD_PARTS = {0: (2, 2), 1: (2, 4, 4)}


def store_parts(grads, refs):
    at = 0
    for ref in refs:
        ref[...] = grads[at : at + ref.shape[0]].astype(BF16)
        at += ref.shape[0]


def grad_shapes(width, c):
    return [jax.ShapeDtypeStruct((width // f, c), BF16) for side in (0, 1) for f in GRAD_PARTS[side]]


def pair_sources(pair):
    return {0: [(0, 0, 2)], 1: [(0, 2, 1), (1, 2, 1)], 2: [(1, 0, 2)]}[pair]


Q_BIAS, V_BIAS, UP_BIAS = range(3)


def attend_forward_kernel(rows, pair, *refs):
    *refs, q_ref, k_ref, v_ref, w_ref, mixed_ref, lse_ref, vt_ref = refs
    xa_ref, xb_ref, *raw, own_ref, other_ref = refs
    raw = {0: [raw], 1: [raw[:2], raw[2:]], 2: [raw]}[pair]
    d = HEAD_DIM
    two = 2 * d
    tokens = xa_ref.shape[0]
    step = pl.program_id(0)
    block = mixed_ref.shape[0]

    @pl.when(step == 0)
    def _():
        for kind in range(4):
            at = kind * two
            for pieces, (_, first, heads) in zip(raw, pair_sources(pair)):
                source = (kind * 3 + first) * d
                put_together(
                    rows,
                    pieces,
                    w_ref,
                    slice(source, source + heads * d),
                    slice(at, at + heads * d),
                )
                at += heads * d
        bias = []
        for row in (Q_BIAS, None, V_BIAS):
            for side, first, heads in pair_sources(pair):
                cols = slice(first * d, (first + heads) * d)
                if row is None:
                    bias.append(jnp.zeros((1, heads * d), F32))
                else:
                    bias.append((own_ref, other_ref)[side][row : row + 1, cols])
        bias = jnp.concatenate(bias, axis=1)
        for half, ref in enumerate((xa_ref, xb_ref)):
            at = slice(half * tokens, (half + 1) * tokens)
            proj = (dot_nn(ref[...], w_ref[:, : 3 * two]) + bias).astype(BF16)
            q_ref[at, :] = proj[:, :two]
            k_ref[at, :] = proj[:, two : 2 * two]
            v_ref[at, :] = proj[:, 2 * two :]
        turned = v_ref[...].T
        for head in range(2):
            vt_ref[head, :d, :] = turned[head * d : (head + 1) * d, :]
            vt_ref[head, d:, :] = jnp.ones((vt_ref.shape[1] - d, turned.shape[1]), BF16)

    query = q_ref[pl.ds(pl.multiple_of(step * block, block), block), :]
    lane = lax.broadcasted_iota(jnp.int32, query.shape, 1)
    outs = []
    for head in range(2):
        masked = jnp.where(lane // d == head, query, jnp.zeros_like(query)) * BF16(d**-0.5)
        scores = dot_nt(k_ref[...], masked)
        top = jnp.max(scores, axis=0, keepdims=True)
        weights = jnp.exp2((scores - top) * LOG2E).astype(BF16)
        out = dot_nn(vt_ref[head], weights)
        total = out[d : d + 1, :]
        outs.append(out[:d, :] * (1.0 / total))
        lse_ref[head : head + 1, :] = top + jnp.log(total)
    mixed_ref[...] = jnp.concatenate(outs, axis=0).T.astype(BF16)


def attend_forward(xa, xb, raw, own, other, rows, pair):
    tokens, width = xa.shape
    seq = 2 * tokens
    two = 2 * HEAD_DIM
    block = 512
    part = jax.ShapeDtypeStruct((seq, two), BF16)
    weight = jax.ShapeDtypeStruct((width, 4 * two), BF16)
    ins = [xa, xb, *side_pieces(raw, [side for side, *_ in pair_sources(pair)]), own, other]
    return call(
        partial(attend_forward_kernel, rows, pair),
        grid=(seq // block,),
        in_specs=[whole(a.shape) for a in ins],
        out_specs=[
            whole(part.shape),
            whole(part.shape),
            whole(part.shape),
            whole(weight.shape),
            pl.BlockSpec((block, two), lambda i: (i, 0)),
            pl.BlockSpec((8, block), lambda i: (0, i)),
        ],
        out_shape=[part, part, part, weight, part, jax.ShapeDtypeStruct((8, seq), F32)],
        scratch_shapes=[pltpu.VMEM((2, HEAD_DIM + 16, seq), BF16)],
        cost_estimate=cost(
            flops=24 * seq * seq * two, bytes_accessed=16 * seq * width, transcendentals=seq * seq
        ),
        name=f"attend_forward_{pair}",
    )(*ins)


def attend_backward_kernel(rows, pair, *refs):
    q_ref, k_ref, v_ref, w_ref, ga_ref, gb_ref, turned_ref, mixed_ref, lse_ref = refs[:9]
    kt_ref, dk_acc, dv_acc, gmix_ref, gall_ref, out_ref = refs[-6:]
    *grads_refs, dproj_ref, sum_ref = refs[9:-6]
    step = pl.program_id(0)
    d = HEAD_DIM
    two = 2 * d
    scale = d**-0.5
    tokens = ga_ref.shape[0]
    block = lse_ref.shape[1]

    @pl.when(step == 0)
    def _():
        kt_ref[...] = k_ref[...].T
        dk_acc[...] = jnp.zeros_like(dk_acc)
        dv_acc[...] = jnp.zeros_like(dv_acc)
        for half, ref in enumerate((ga_ref, gb_ref)):
            at = slice(half * tokens, (half + 1) * tokens)
            gall_ref[at, :] = ref[...]
            gmix_ref[at, :] = dot_nn(ref[...], w_ref[:, 3 * two :]).astype(BF16)

    here_rows = pl.ds(pl.multiple_of(step * block, block), block)
    query = q_ref[here_rows, :]
    grad = gmix_ref[here_rows, :]
    lane = lax.broadcasted_iota(jnp.int32, query.shape, 1)
    dots = (grad.astype(F32) * mixed_ref[here_rows, :].astype(F32)).T
    dqs = []
    for head in range(2):
        mine = lane // d == head
        query_h = jnp.where(mine, query, jnp.zeros_like(query))
        grad_h = jnp.where(mine, grad, jnp.zeros_like(grad))
        row_dots = jnp.sum(dots[head * d : (head + 1) * d, :], axis=0, keepdims=True)
        log_total = lse_ref[head : head + 1, :] * LOG2E
        scores = dot_nt(k_ref[...], query_h * BF16(scale))
        probs = jnp.exp2(scores * LOG2E - log_total)
        grad_probs = dot_nt(v_ref[...], grad_h)
        grad_scores = (probs * (grad_probs - row_dots)).astype(BF16)
        dv_acc[...] += dot_nn(probs.astype(BF16), grad_h)
        dk_acc[...] += dot_nn(grad_scores, query_h)
        dqs.append(dot_nn(kt_ref[head * d : (head + 1) * d, :], grad_scores) * scale)
    dproj_ref[here_rows, :two] = jnp.concatenate(dqs, axis=0).T.astype(BF16)

    @pl.when(step == pl.num_programs(0) - 1)
    def _():
        dproj_ref[:, two : 2 * two] = (dk_acc[...] * scale).astype(BF16)
        dproj_ref[:, 2 * two :] = dv_acc[...].astype(BF16)
        dproj = dproj_ref[...]
        sum_ref[0:1, :] = jnp.sum(dproj.astype(F32), axis=0, keepdims=True)
        out_ref[:, : 3 * two] = dot_nn(turned_ref[...], dproj).astype(BF16)
        grads = dot_nn(mixed_ref[...].T, gall_ref[...]).T.astype(BF16)
        n = grads.shape[0] // BLOCKS
        for at_block in range(BLOCKS):
            at = pl.multiple_of(slot_of(rows, at_block) * n, n)
            out_ref[pl.ds(at, n), 3 * two :] = grads[at_block * n : (at_block + 1) * n, :]
        if pair != 1:
            store_parts(out_ref[...], grads_refs)
        else:
            for kind in range(4):
                for side, ref in enumerate(grads_refs):
                    ref[:, kind * d : (kind + 1) * d] = out_ref[
                        :, kind * two + side * d : kind * two + (side + 1) * d
                    ]


def attend_backward(q, k, v, w, ga, gb, turned, mixed, lse, rows, pair):
    seq, two = q.shape
    width = ga.shape[1]
    block = 256
    grads = (width, 2 * two) if pair == 1 else (width // 2, 4 * two)
    outs = [jax.ShapeDtypeStruct(grads, BF16)] * 2 + [
        jax.ShapeDtypeStruct((seq, 3 * two), BF16),
        jax.ShapeDtypeStruct((8, 3 * two), F32),
    ]
    ins = [q, k, v, w, ga, gb, turned, mixed]
    *grads, dproj, sums = call(
        partial(attend_backward_kernel, rows, pair),
        grid=(seq // block,),
        in_specs=[whole(a.shape) for a in ins] + [pl.BlockSpec((8, block), lambda i: (0, i))],
        out_specs=[whole(o.shape) for o in outs],
        out_shape=outs,
        scratch_shapes=[
            pltpu.VMEM((two, seq), BF16),
            pltpu.VMEM((seq, two), F32),
            pltpu.VMEM((seq, two), F32),
            pltpu.VMEM((seq, two), BF16),
            pltpu.VMEM((seq, width), BF16),
            pltpu.VMEM((width, 4 * two), BF16),
        ],
        cost_estimate=cost(
            flops=50 * seq * seq * two, bytes_accessed=16 * seq * width, transcendentals=seq * seq
        ),
        name=f"attend_backward_{pair}",
    )(*ins, lse)
    return grads, dproj, sums


def project_kernel(first, cols, *refs):
    count = (len(refs) - 1) // 2
    total = 0.0
    for part, weight in zip(refs[:count], refs[count:-1]):
        total = total + dot_nt(part[...], weight[...])
    refs[-1][...] = total.astype(refs[-1].dtype)


def project(parts, weights, half, first, dtype):
    seq, cols = parts[0].shape
    width = weights[0].shape[0]
    tokens = seq // 2
    return call(
        partial(project_kernel, first, cols),
        grid=(1,),
        in_specs=[pl.BlockSpec((tokens, cols), lambda i: (half, 0)) for _ in parts]
        + [pl.BlockSpec((width, cols), lambda i: (0, first // cols)) for _ in weights],
        out_specs=whole((tokens, width)),
        out_shape=jax.ShapeDtypeStruct((tokens, width), dtype),
        cost_estimate=cost(
            flops=2 * tokens * width * cols * 3, bytes_accessed=0, transcendentals=0
        ),
        name="project",
    )(*parts, *weights)


def statistics(rows):
    mean = jnp.mean(rows, axis=1, keepdims=True)
    centered = rows - mean
    inverse = lax.rsqrt(jnp.mean(jnp.square(centered), axis=1, keepdims=True) + EPSILON)
    return centered * inverse, inverse


def add_rows(sum_ref, values):
    @pl.when(pl.program_id(0) == 0)
    def _():
        sum_ref[...] = jnp.zeros_like(sum_ref)

    for i, value in enumerate(values):
        sum_ref[i : i + 1, :] += jnp.sum(value, axis=0, keepdims=True)


ATTN_GAIN, ATTN_SHIFT, MLP_GAIN, MLP_SHIFT, OUTPUT_BIAS, DOWN_BIAS = range(6)


def vector(ref, at):
    return ref[at : at + 1, :]


def norm_kernel(x_ref, vec_ref, out_ref):
    hat, _ = statistics(x_ref[...].astype(F32))
    out_ref[...] = (hat * vector(vec_ref, ATTN_GAIN) + vector(vec_ref, ATTN_SHIFT)).astype(BF16)


def resid_kernel(x_ref, own_ref, got_ref, vec_ref, resid_ref, out_ref, sum_ref):
    branch = own_ref[...] + got_ref[...].astype(F32) + vector(vec_ref, OUTPUT_BIAS)
    resid = x_ref[...].astype(F32) + branch
    resid_ref[...] = resid
    hat, _ = statistics(resid)
    out_ref[...] = (hat * vector(vec_ref, MLP_GAIN) + vector(vec_ref, MLP_SHIFT)).astype(BF16)
    add_rows(sum_ref, [branch * branch])


def result_kernel(resid_ref, own_ref, got_ref, vec_ref, out_ref, sum_ref):
    branch = own_ref[...] + got_ref[...].astype(F32) + vector(vec_ref, DOWN_BIAS)
    result = resid_ref[...] + branch
    out_ref[...] = result.astype(BF16)
    add_rows(sum_ref, [result * result, branch * branch])


def norm_gradient(grad, rows, gain):
    hat, inverse = statistics(rows)
    grad_hat = grad * gain
    first = jnp.mean(grad_hat, axis=1, keepdims=True)
    second = jnp.mean(grad_hat * hat, axis=1, keepdims=True)
    return inverse * (grad_hat - first - hat * second), grad * hat


def middle_kernel(resid_ref, own_ref, got_ref, cot_ref, vec_ref, grad_ref, low_ref, sum_ref):
    grad = own_ref[...] + got_ref[...].astype(F32)
    back, gains = norm_gradient(grad, resid_ref[...], vector(vec_ref, MLP_GAIN))
    cot = cot_ref[...].astype(F32)
    hidden = cot + back
    grad_ref[...] = hidden
    low = hidden.astype(BF16)
    low_ref[...] = low
    add_rows(sum_ref, [gains, grad, low.astype(F32), cot])


def last_kernel(x_ref, own_ref, got_ref, hidden_ref, vec_ref, grad_ref, sum_ref):
    grad = own_ref[...] + got_ref[...].astype(F32)
    back, gains = norm_gradient(grad, x_ref[...].astype(F32), vector(vec_ref, ATTN_GAIN))
    grad_ref[...] = hidden_ref[...] + back
    add_rows(sum_ref, [gains, grad])


def attention_sum_kernel(own_ref, *refs):
    *got_refs, qkv_ref, out_ref = refs
    d = HEAD_DIM
    total = own_ref[...]
    for ref in got_refs:
        total = total + ref[...].astype(F32)
    for kind in range(4):
        large = total[:, 2 * d * kind : 2 * d * (kind + 1)]
        small = total[:, d * (8 + kind) : d * (9 + kind)]
        if kind < 3:
            qkv_ref[:, kind, : 2 * d] = large
            qkv_ref[:, kind, 2 * d :] = small
        else:
            out_ref[:, : 2 * d] = large
            out_ref[:, 2 * d :] = small


def attention_sum(own, got):
    n = own.shape[0]
    side = 3 * HEAD_DIM
    return call(
        attention_sum_kernel,
        out_shape=[
            jax.ShapeDtypeStruct((n, 3, side), F32),
            jax.ShapeDtypeStruct((n, side), F32),
        ],
        cost_estimate=cost(flops=0, bytes_accessed=0, transcendentals=0),
        name="attention_sum",
    )(own, *got)


def small_sums_kernel(entries, own_ref, got_ref, *outs):
    total = own_ref[...] + got_ref[...]
    *vector_refs, qkv_ref, rms_ref = outs
    for ref, row in zip(vector_refs, (7, 8, 2, 0, 1, 10, 3)):
        ref[...] = total[row]
    side = qkv_ref.shape[1]
    qkv_ref[0:1, :] = total[9:10, :side]
    qkv_ref[1:2, :] = total[9:10, side : 2 * side]
    means = jnp.sum(total[4:7, :], axis=1, keepdims=True) / entries
    means = jnp.broadcast_to(jnp.sqrt(means), (3, rms_ref.shape[1]))
    rms_ref[0:1, :] = means[1:2]
    rms_ref[1:2, :] = means[0:1]
    rms_ref[2:3, :] = means[2:3]


def small_sums(own, got, side, entries):
    width = own.shape[1]
    return call(
        partial(small_sums_kernel, entries),
        out_shape=[jax.ShapeDtypeStruct((width,), F32)] * 7
        + [jax.ShapeDtypeStruct((2, side), F32), jax.ShapeDtypeStruct((3, 128), F32)],
        cost_estimate=cost(flops=0, bytes_accessed=0, transcendentals=0),
        name="small_sums",
    )(own, got)


def by_rows(kernel, name, rows, vectors, outs, sums=False):
    tokens, width = rows[0].shape
    block = tokens // 2
    part = pl.BlockSpec((block, width), lambda i: (i, 0))
    out_shape = [jax.ShapeDtypeStruct((tokens, width), t) for t in outs]
    out_specs = [part] * len(outs)
    if sums:
        out_shape.append(jax.ShapeDtypeStruct((8, width), F32))
        out_specs.append(whole((8, width)))
    return call(
        kernel,
        grid=(tokens // block,),
        in_specs=[part] * len(rows) + [whole(vectors.shape)],
        out_specs=out_specs,
        out_shape=out_shape,
        cost_estimate=cost(flops=0, bytes_accessed=0, transcendentals=0),
        name=name,
    )(*rows, vectors)


def gelu_parts(u):
    c0 = math.sqrt(2.0 / math.pi)
    square = u * u
    t = jnp.tanh(u * (c0 + (c0 * 0.044715) * square))
    half = 0.5 * u
    act = half + half * t
    slope = 0.5 + 0.5 * t + half * (1.0 - t * t) * (c0 + (3.0 * c0 * 0.044715) * square)
    return act, slope


def up_kernel(rows, side, *refs):
    xa_ref, xb_ref, turned_ref, *raw, bias_ref, act_ref, slope_ref = refs[: -1 - len(GRAD_PARTS[side])]
    outs, w_ref = refs[-1 - len(GRAD_PARTS[side]) : -1], refs[-1]
    tokens = xa_ref.shape[0]
    put_together(rows, raw, w_ref)
    for half, ref in enumerate((xa_ref, xb_ref)):
        act, slope = gelu_parts(dot_nn(ref[...], w_ref[...]) + vector(bias_ref, UP_BIAS))
        act_ref[half * tokens : (half + 1) * tokens, :] = act.astype(BF16)
        slope_ref[half * tokens : (half + 1) * tokens, :] = slope.astype(BF16)
    store_parts(dot_nn(turned_ref[...], act_ref[...]), outs)


TILE = 256


def tiles(*dims):
    return pl.BlockSpec((*dims, TILE), lambda j: (0,) * len(dims) + (j,))


def raw_tiles(raw):
    return [tiles(*r.shape[:2]) for r in raw]


def up_and_down_grads(xa, xb, turned, raw, bias, rows, side):
    tokens, width = xa.shape
    c = bias.shape[1]
    hidden = jax.ShapeDtypeStruct((2 * tokens, c), BF16)
    grads = [jax.ShapeDtypeStruct((width // f, c), BF16) for f in GRAD_PARTS[side]]
    raw = side_pieces(raw, [side])
    act, slope, *grads = call(
        partial(up_kernel, rows, side),
        grid=(c // TILE,),
        in_specs=[whole(xa.shape), whole(xb.shape), whole(turned.shape)]
        + raw_tiles(raw)
        + [tiles(8)],
        out_specs=[tiles(2 * tokens)] * 2 + [tiles(g.shape[0]) for g in grads],
        out_shape=[hidden] * 2 + grads,
        scratch_shapes=[pltpu.VMEM((width, TILE), BF16)],
        cost_estimate=cost(
            flops=8 * tokens * width * c, bytes_accessed=0, transcendentals=2 * tokens * c
        ),
        name=f"up_and_down_grads_{side}",
    )(xa, xb, turned, *raw, bias)
    return act, slope, grads


def hidden_back_kernel(rows, side, *refs):
    ga_ref, gb_ref, *raw = refs[: 6 + 2 * side]
    down, up = raw[: len(raw) // 2], raw[len(raw) // 2 :]
    slope_ref, *before, pre_ref, sum_ref = refs[6 + 2 * side : 9 + 3 * side]
    *outs, acc_ref, w_ref, u_ref = refs[9 + 3 * side :]
    step = pl.program_id(0)
    tokens = ga_ref.shape[0]

    @pl.when(step == 0)
    def _():
        acc_ref[...] = before[0][...] if side else jnp.zeros_like(acc_ref)

    put_together(rows, down, w_ref)
    put_together(rows, up, u_ref)
    totals = 0.0
    for half, ref in enumerate((ga_ref, gb_ref)):
        at = slice(half * tokens, (half + 1) * tokens)
        back = dot_nn(ref[...], w_ref[...]) * slope_ref[at, :].astype(F32)
        pre = back.astype(BF16)
        pre_ref[at, :] = pre
        totals = totals + jnp.sum(pre.astype(F32), axis=0, keepdims=True)
        acc_ref[at, :] += dot_nt(pre, u_ref[...])
    sum_ref[0:1, :] = totals

    @pl.when(step == pl.num_programs(0) - 1)
    def _():
        if side:
            outs[0][...] = acc_ref[:tokens, :]
            outs[1][...] = acc_ref[tokens:, :].astype(BF16)
        else:
            outs[0][...] = acc_ref[...]


def hidden_back(ga, gb, down, up, slope, before, rows, side):
    tokens, width = ga.shape
    seq, c = slope.shape
    if side:
        backs = [jax.ShapeDtypeStruct(ga.shape, t) for t in (F32, BF16)]
    else:
        backs = [jax.ShapeDtypeStruct((seq, width), F32)]
    return call(
        partial(hidden_back_kernel, rows, side),
        grid=(c // TILE,),
        in_specs=[whole(ga.shape), whole(gb.shape)]
        + raw_tiles(down)
        + raw_tiles(up)
        + [tiles(seq)]
        + [whole(b.shape) for b in before],
        out_specs=[tiles(seq), tiles(8)] + [whole(b.shape) for b in backs],
        out_shape=[jax.ShapeDtypeStruct((seq, c), BF16), jax.ShapeDtypeStruct((8, c), F32)] + backs,
        scratch_shapes=[
            pltpu.VMEM((seq, width), F32),
            pltpu.VMEM((width, TILE), BF16),
            pltpu.VMEM((width, TILE), BF16),
        ],
        cost_estimate=cost(
            flops=8 * tokens * width * c, bytes_accessed=12 * tokens * c, transcendentals=0
        ),
        name=f"hidden_back_{side}",
    )(ga, gb, *down, *up, slope, *before)


def mlp_out_kernel(rows, *refs):
    act_ref, act_o_ref = refs[:2]
    down = refs[2:7]
    own_ref, other_ref, acc_ref, w_ref = refs[7:]
    step = pl.program_id(0)
    tokens = own_ref.shape[0]

    @pl.when(step == 0)
    def _():
        acc_ref[...] = jnp.zeros_like(acc_ref)

    put_together(rows, down[:2], w_ref.at[0])
    put_together(rows, down[2:], w_ref.at[1])
    acc_ref[...] += dot_nt(act_ref[...], w_ref[0]) + dot_nt(act_o_ref[...], w_ref[1])

    @pl.when(step == pl.num_programs(0) - 1)
    def _():
        own_ref[...] = acc_ref[:tokens, :]
        other_ref[...] = acc_ref[tokens:, :].astype(BF16)


def mlp_out(act, act_o, down, width, rows):
    seq, c = act.shape
    outs = [jax.ShapeDtypeStruct((seq // 2, width), t) for t in (F32, BF16)]
    return call(
        partial(mlp_out_kernel, rows),
        grid=(c // TILE,),
        in_specs=[tiles(seq)] * 2 + raw_tiles(down),
        out_specs=[whole(o.shape) for o in outs],
        out_shape=outs,
        scratch_shapes=[pltpu.VMEM((seq, width), F32), pltpu.VMEM((2, width, TILE), BF16)],
        cost_estimate=cost(
            flops=4 * seq * width * c, bytes_accessed=4 * seq * c, transcendentals=0
        ),
        name="mlp_out",
    )(act, act_o, *down)


def weight_grads_kernel(turned_ref, g_ref, go_ref, *outs):
    store_parts(dot_nn(turned_ref[...], g_ref[...]), outs[:2])
    store_parts(dot_nn(turned_ref[...], go_ref[...]), outs[2:])


def weight_grads(turned, grad, grad_o):
    width, seq = turned.shape
    c = grad.shape[1]
    return call(
        weight_grads_kernel,
        grid=(c // TILE,),
        in_specs=[whole(turned.shape), tiles(seq), tiles(seq)],
        out_specs=[tiles(s.shape[0]) for s in grad_shapes(width, c)],
        out_shape=grad_shapes(width, c),
        cost_estimate=cost(
            flops=4 * seq * width * c, bytes_accessed=6 * seq * c, transcendentals=0
        ),
        name="weight_grads",
    )(turned, grad, grad_o)


def make_local(rows):
    low, near = rows[-1], rows[:-1]
    fast = 2 ** len(rows) == BLOCKS
    order = rows if fast else None

    def to_blocks(parts):
        width, c = parts[0].shape[0] * 2, parts[0].shape[1]
        return [p.reshape(-1, width // BLOCKS, c) for p in parts]

    def reduce_plain(parts):
        blocks = to_blocks(parts)
        own = jnp.stack(blocks[:2], axis=1)
        other = jnp.stack([blocks[2], jnp.concatenate(blocks[3:])], axis=1)
        width, c = parts[0].shape[0] * 2, parts[0].shape[1]
        return scatter_rows(own.reshape(width, c), other.reshape(width, c), rows)

    def natural(grads):
        width, c = grads.shape
        blocks = grads.reshape(2, BLOCKS // 2, width // BLOCKS, c)
        return jnp.swapaxes(blocks, 0, 1).reshape(width, c)

    def local(
        layer_input,
        attn_gain,
        attn_shift,
        qkv_weight,
        qkv_bias,
        output_weight,
        output_bias,
        mlp_gain,
        mlp_shift,
        up_weight,
        up_bias,
        down_weight,
        down_bias,
        cotangent,
    ):
        tokens, width = layer_input.shape
        n, _, side = qkv_weight.shape
        hidden = up_weight.shape[1]
        d = HEAD_DIM

        attn_shard = jnp.concatenate([qkv_weight.reshape(n, -1), output_weight], axis=1)
        vectors = table_of(attn_gain, attn_shift, mlp_gain, mlp_shift, output_bias, down_bias)
        (attn_in,) = by_rows(norm_kernel, "norm", [layer_input], vectors, [BF16])
        attn_in_other = swap(attn_in, "core")
        cot_other = swap(cotangent, "core")
        bias_own = jnp.pad(qkv_bias, ((0, 6), (0, hidden - side)))
        bias_own = bias_own + jnp.pad(up_bias[None, :], ((UP_BIAS, 7 - UP_BIAS), (0, 0)))
        bias_other = swap(bias_own, "y")
        if fast:
            attn_near = gather_near(attn_shard, near)
            attn_near = after(attn_near, cot_other, bias_other)
            attn_stack = jnp.stack(attn_near)
            mlp_near = gather_near(jnp.stack([up_weight, down_weight]), near)
            attn_far = gather_far(attn_stack, low)
            attn_raw = gather_corners(attn_far, low)
        else:
            attn_raw, up_raw, down_raw = (
                gather_plain(w, rows) for w in (attn_shard, up_weight, down_weight)
            )
        halves = (attn_in, attn_in_other, cotangent, cot_other)
        if fast:
            halves = after(halves, attn_stack)
        attn_turned = turn(*halves[:2], order)
        cot_turned = turn(*halves[2:], order)
        attended = []
        for pair in range(3):
            bias = bias_own
            if fast and pair == 0:
                bias = after(bias, attn_far, attn_turned, cot_turned)
            if pair:
                bias = after(bias, attended[pair - 1][4])
            if fast and pair == 1:
                mlp_near = after(mlp_near, attended[0][4], attn_raw)
                up_far = gather_far(jnp.stack([m[0] for m in mlp_near]), low)
                down_stack = jnp.stack([m[1] for m in mlp_near])
                bias = after(bias, up_far[0], down_stack)
            attended.append(
                attend_forward(attn_in, attn_in_other, attn_raw, bias, bias_other, order, pair)
            )
        mixed = [a[4] for a in attended]
        weights = [a[3] for a in attended]
        if fast:
            mixed, up_far = after((mixed, up_far))
            up_raw = gather_corners(up_far, low)
        got = swap(project(mixed, weights, 1, 6 * d, BF16), "core")
        own = project(mixed, weights, 0, 6 * d, F32)
        hidden_resid, mlp_in, branch_sums = by_rows(
            resid_kernel,
            "resid",
            [layer_input, own, got],
            vectors,
            [F32, BF16],
            True,
        )
        mlp_in_other = swap(mlp_in, "core")
        if fast:
            down_far = gather_far(after(down_stack, mlp_in_other), low)
        ins = (mlp_in, mlp_in_other, cot_turned)
        grads = (cotangent, cot_other)
        act, slope, down_own = up_and_down_grads(*ins, up_raw, bias_own, order, 0)
        if fast:
            down_raw = gather_corners(after(down_far, act), low)
        pre, up_sums, back = hidden_back(*grads, down_raw[:2], up_raw[:2], slope, (), order, 0)
        bias_other = after(bias_other, pre)
        act_o, slope_o, down_other = up_and_down_grads(*ins, up_raw, bias_other, order, 1)
        down_parts = down_own + down_other
        if fast:
            down_parts = to_blocks(down_parts)
            down_got = reduce_corners(down_parts, low)
        else:
            down_grad = reduce_plain(down_parts)
        pre_o, up_sums_o, back, back_other = hidden_back(
            *grads, down_raw[2:], up_raw[2:], slope_o, (back,), order, 1
        )
        back_got = swap(back_other, "core")
        act, act_o = after((act, act_o), pre_o)
        branch, branch_other = mlp_out(act, act_o, down_raw, width, order)
        back = after(back, branch)
        hidden_grad, grad_attn, middle_sums = by_rows(
            middle_kernel,
            "middle",
            [hidden_resid, back, back_got, cotangent],
            vectors,
            [F32, BF16],
            True,
        )
        grad_attn_other = swap(grad_attn, "core")
        branch_got = swap(after(branch_other, grad_attn), "core")
        halves = after((mlp_in, mlp_in_other), grad_attn)
        if fast:
            halves, down_got = after((halves, down_got))
            down_sent = reduce_far(down_parts, down_got, low)
        mlp_turned = turn(*halves, order)
        up_parts = weight_grads(mlp_turned, pre, pre_o)
        resid, branch, branch_got = after((hidden_resid, branch, branch_got), up_parts)
        layer_output, result_sums = by_rows(
            result_kernel, "result", [resid, branch, branch_got], vectors, [BF16], True
        )
        if fast:
            up_parts = to_blocks(up_parts)
            up_got = reduce_corners(up_parts, low)
        else:
            up_grad = reduce_plain(up_parts)

        half, block = width // 2, width // BLOCKS
        pair_grads, pair_sums, dprojs = {}, {}, {}
        for pair in (2, 1, 0):
            q, k, v, w, mix, lse = attended[pair]
            if pair == 2:
                lse = after(lse, layer_output)
            else:
                lse = after(lse, pair_grads[pair + 1])
            if fast and pair == 1:
                lse, up_got, down_sent = after((lse, up_got, down_sent))
                total = down_parts[0].astype(F32) + sum(g.astype(F32) for g in down_sent)
                down_sum, down_got = total[:2], swap(total[2:].astype(BF16), near[0])
                up_sent = reduce_far(up_parts, up_got, low)
            if fast and pair == 0:
                lse, large_got = after((lse, large_got))
                large_y = (pair_grads[2][0].astype(F32) + large_got.astype(F32)).astype(BF16)
                large_y = swap(large_y, "y")
            pair_grads[pair], dprojs[pair], pair_sums[pair] = attend_backward(
                q, k, v, w, grad_attn, grad_attn_other, attn_turned, mix, lse, order, pair
            )
            if fast and pair == 2:
                large_got = swap(pair_grads[2][1], low)

        dprojs = [dprojs[pair] for pair in range(3)]
        if fast:
            large_x = swap(pair_grads[0][1], low)
            small_got = swap(after(pair_grads[1][1], pair_grads[0]), "y")
            up_sent, dprojs, down_got = after((up_sent, dprojs, down_got), pair_grads[0])
            down_sum = down_sum + down_got.astype(F32)
            down_got = swap(down_sum[1].astype(BF16), near[1])
            total = up_parts[0].astype(F32) + sum(g.astype(F32) for g in up_sent)
            up_sum, up_got = total[:2], swap(total[2:].astype(BF16), near[0])
        back_other = project(dprojs, weights, 1, 0, BF16)
        got = swap(back_other, "core")
        own = project(dprojs, weights, 0, 0, F32)
        if fast:
            small = pair_grads[1][0].astype(F32) + after(small_got, own).astype(F32)
            small_x = swap(small[half:].astype(BF16), low)
        input_grad, last_sums = by_rows(
            last_kernel, "last", [layer_input, own, got, hidden_grad], vectors, [F32], True
        )
        if not fast:
            own, other = (
                natural(jnp.concatenate(p, axis=1))
                for p in (
                    (jnp.concatenate(pair_grads[0]), pair_grads[1][0]),
                    (jnp.concatenate(pair_grads[2]), pair_grads[1][1]),
                )
            )
            attn_grad = scatter_rows(own, other, rows)

        def bias_row(large, small, at):
            row = 0.0
            for i, kind in enumerate((0, 2)):
                source = 2 * d * kind
                for piece, to in (
                    (large[:1, source : source + 2 * d], 0),
                    (small[:1, source + at : source + at + d], 2 * d),
                ):
                    to = i * side + to
                    row = row + jnp.pad(piece, ((0, 0), (to, width - to - piece.shape[1])))
            return row

        if fast:
            last_sums, large_x, large_y, small_x, up_got, down_got = after(
                (last_sums, large_x, large_y, small_x, up_got, down_got)
            )
            large_sent, small_sent = (large_x, large_y), small_x
        common = jnp.concatenate(
            [middle_sums[:4], branch_sums[:1], result_sums[:2], last_sums[:2]], axis=0
        )
        common = common + swap(common, "core")
        own = jnp.concatenate([common, bias_row(pair_sums[0], pair_sums[1], 0), up_sums[:1]], axis=0)
        other = jnp.concatenate([common, bias_row(pair_sums[2], pair_sums[1], d), up_sums_o[:1]], axis=0)
        sums = own + swap(other, "y")
        if fast:
            large = pair_grads[0][0].astype(F32) + sum(g.astype(F32) for g in large_sent)
            small = small[:half] + small_sent.astype(F32)
            both = jnp.concatenate([large, small], axis=1).reshape(-1, block, 12 * d)
            attn_near = send_near(both, near)
            total = up_sum + up_got.astype(F32)
            up_grad = total[0] + swap(total[1].astype(BF16), near[1]).astype(F32)
            down_grad = down_sum[0] + down_got.astype(F32)
        for axis in reversed(rows[1:]):
            sums = sums + swap(sums, axis)
        entries = float(tokens * 2 ** (len(rows) + 2) * width)
        *vecs, qkv_bias_grad, rms_values = small_sums(sums, swap(sums, rows[0]), side, entries)
        if fast:
            qkv_grad, output_grad = attention_sum(attn_near[0], attn_near[1].values())
        else:
            qkv_grad, output_grad = attention_sum(attn_grad, ())
        return (
            layer_output,
            input_grad,
            vecs[0],
            vecs[1],
            qkv_grad,
            qkv_bias_grad,
            output_grad,
            vecs[2],
            vecs[3],
            vecs[4],
            up_grad,
            vecs[5],
            down_grad,
            vecs[6],
            rms_values[:, 0],
        )

    return local


def solution(mesh):
    row_size, col_size = mesh.shape["row"], mesh.shape["col"]
    bits = row_size.bit_length() - 1
    rows = tuple(f"r{b}" for b in reversed(range(bits)))
    cube = Mesh(mesh.devices.reshape((2,) * bits + (col_size // 2, 2)), rows + ("y", "core"))
    col = ("y", "core")
    every = rows + col
    placed = (
        P(every, None),
        P(),
        P(),
        P(rows, None, col),
        P(None, col),
        P(rows, col),
        P(),
        P(),
        P(),
        P(rows, col),
        P(col),
        P(rows, col),
        P(),
        P(every, None),
    )
    return jax.shard_map(
        make_local(rows),
        mesh=cube,
        in_specs=placed,
        out_specs=(
            P(every, None),
            P(every, None),
            P(),
            P(),
            P(rows, None, col),
            P(None, col),
            P(rows, col),
            P(),
            P(),
            P(),
            P(rows, col),
            P(col),
            P(rows, col),
            P(),
            P(),
        ),
        check_vma=False,
    )
```

```python
import math
from functools import partial

import jax
import jax.numpy as jnp
from jax import lax
from jax.experimental import pallas as pl
from jax.experimental.pallas import tpu as pltpu
from jax.sharding import Mesh, PartitionSpec as P

HEAD_DIM = 64
EPSILON = 1e-06
SWAP = [(0, 1), (1, 0)]
LOG2E = math.log2(math.e)
BF16 = jnp.bfloat16
F32 = jnp.float32
VMEM_BYTES = 16 * 2**20


def call(kernel, **kwargs):
    params = pltpu.CompilerParams(vmem_limit_bytes=VMEM_BYTES)
    return pl.pallas_call(kernel, compiler_params=params, **kwargs)


def cost(flops, bytes_accessed, transcendentals):
    return pl.CostEstimate(flops=0, bytes_accessed=0, transcendentals=0)


def after(arrays, *others):
    return lax.optimization_barrier((arrays, others))[0]


def table_of(*vectors):
    row = lax.broadcasted_iota(jnp.int32, (8, vectors[0].shape[0]), 0)
    out = jnp.zeros(row.shape, F32)
    for i, v in enumerate(vectors):
        out = jnp.where(row == i, v[None, :], out)
    return out


def swap(array, axis):
    return lax.ppermute(array, axis, SWAP)


def dot_nn(left, right):
    return lax.dot_general(left, right, (((1,), (0,)), ((), ())), preferred_element_type=F32)


def dot_nt(left, right):
    return lax.dot_general(left, right, (((1,), (1,)), ((), ())), preferred_element_type=F32)


def dot_tn(left, right):
    return lax.dot_general(left, right, (((0,), (0,)), ((), ())), preferred_element_type=F32)


def xor_exchange(blocks_of, axes):
    got = {}
    count = len(axes)
    sizes = [2] * count
    for bits in range(1, 2**count):
        perm = [(i, i ^ bits) for i in range(math.prod(sizes))]
        got[bits] = lax.ppermute(blocks_of(bits), axes, perm)
    return got


def in_order(own, got, axes):
    parts = [own] + [got[bits] for bits in range(1, 2 ** len(axes))]
    for depth, axis in enumerate(reversed(axes)):
        bit = 2**depth
        flip = lax.axis_index(axis) == 1
        parts = [jnp.where(flip, parts[i ^ bit], parts[i]) for i in range(len(parts))]
    return jnp.stack(parts)


def pair_in_order(own, other, axis, dim):
    flip = lax.axis_index(axis) == 1
    return jnp.stack([jnp.where(flip, other, own), jnp.where(flip, own, other)], axis=dim)


def gather_rows(shard, rows):
    low, high = rows[-1], rows[:-1]
    n, c = shard.shape
    near = high[-2:]
    stack = in_order(shard, xor_exchange(lambda bits: shard, near), near)
    for axis in reversed(high[:-2]):
        other = swap(stack, axis)
        stack = pair_in_order(stack, other, axis, 0).reshape(-1, n, c)
    half = c // 2
    first, second = stack[:, :, :half], stack[:, :, half:]
    first_low, second_y = swap(first, low), swap(second, "y")
    first = pair_in_order(first, first_low, low, 1).reshape(-1, half)
    first_y = swap(first, "y")
    second_low = swap(jnp.stack([second, second_y]), low)
    second_own = pair_in_order(second, second_low[0], low, 1).reshape(-1, half)
    second_other = pair_in_order(second_y, second_low[1], low, 1).reshape(-1, half)
    return (
        jnp.concatenate([first, second_own], axis=1),
        jnp.concatenate([first_y, second_other], axis=1),
    )


def pick(array, axis, dim, other):
    zero = lax.index_in_dim(array, 0, dim, keepdims=False)
    one = lax.index_in_dim(array, 1, dim, keepdims=False)
    flip = lax.axis_index(axis) == (0 if other else 1)
    return jnp.where(flip, one, zero)


def scatter_rows(own, other, rows):
    low, high = rows[-1], rows[:-1]
    near = high[-2:]
    total = 2 ** len(rows)
    n, c = own.shape[0] // total, own.shape[1]
    half = c // 2
    own = own.reshape(total // 2, 2, n, c)
    other = other.reshape(total // 2, 2, n, c)
    a_own, a_other = own[..., :half], other[..., :half]
    b_own, b_other = own[..., half:], other[..., half:]
    a_got = swap(a_other, "y")
    b_send = jnp.stack([pick(b_own, low, 1, True), pick(b_other, low, 1, True)])
    b_got = swap(b_send, low)
    a_sum = a_own.astype(F32) + a_got.astype(F32)
    a_send = pick(a_sum, low, 1, True).astype(BF16)
    b_own = pick(b_own, low, 1, False).astype(F32) + b_got[0].astype(F32)
    b_other = (pick(b_other, low, 1, False).astype(F32) + b_got[1].astype(F32)).astype(BF16)
    a_got = swap(a_send, low)
    b_got = swap(b_other, "y")
    a_sum = pick(a_sum, low, 1, False) + a_got.astype(F32)
    b_sum = b_own + b_got.astype(F32)
    both = jnp.concatenate([a_sum, b_sum], axis=2)
    for axis in high[:-2]:
        both = both.reshape(2, -1, n, c)
        got = swap(pick(both, axis, 0, True).astype(BF16), axis)
        both = pick(both, axis, 0, False) + got.astype(F32)
    low_both = both.astype(BF16)
    place = lax.axis_index(near)
    take = lambda bits: lax.dynamic_index_in_dim(low_both, place ^ bits, 0, keepdims=False)
    got = xor_exchange(take, near)
    out = lax.dynamic_index_in_dim(both, place, 0, keepdims=False)
    for piece in got.values():
        out = out + piece.astype(F32)
    return out


BLOCKS = 8


def gather_near(shard, near):
    got = xor_exchange(lambda bits: shard, near)
    return [shard] + [got[bits] for bits in range(1, 2 ** len(near))]


def gather_far(stack, low):
    return stack, swap(stack, low), swap(stack, "y")


def gather_corners(far, low):
    stack, from_low, from_y = far
    half = stack.shape[0] // 2
    return (*far, swap(from_low[:half], "y"), swap(from_y[half:], low))


def gather_plain(shard, rows):
    pieces = []
    for side in gather_rows(shard, rows):
        width, c = side.shape
        blocks = side.reshape(BLOCKS // 2, 2, width // BLOCKS, c)
        pieces += [blocks[:, 0], blocks[:, 1]]
    half = BLOCKS // 4
    return (*pieces[:3], pieces[3][:half], pieces[3][half:])


def reduce_corners(parts, low):
    return swap(parts[3], "y"), swap(parts[4], low)


def reduce_far(parts, got, low):
    _, to_low, to_y, _, _ = parts
    half = to_low.shape[0] // 2
    add = lambda a, b: (a.astype(F32) + b.astype(F32)).astype(BF16)
    to_low = jnp.concatenate([add(to_low[:half], got[0]), to_low[half:]])
    to_y = jnp.concatenate([to_y[:half], add(to_y[half:], got[1])])
    return swap(to_low, low), swap(to_y, "y")


def send_near(stack, near):
    low = stack.astype(BF16)
    return stack[0], xor_exchange(lambda bits: low[bits], near)


def sum_near(own, got):
    for piece in got.values():
        own = own + piece.astype(F32)
    return own


def here(rows):
    if rows is None:
        return 0, 0
    return lax.axis_index(rows[:-1]), lax.axis_index(rows[-1])


def flip(at, by):
    return by if isinstance(at, int) else lax.bitwise_xor(at, by)


def slot_of(rows, block):
    z, x = here(rows)
    block_z, block_x = divmod(block, 2)
    return flip(x, block_x) * (BLOCKS // 2) + flip(z, block_z)


def whole(shape):
    return pl.BlockSpec(shape, lambda *_: (0,) * len(shape))


def side_pieces(raw, sides):
    return [p for side in sides for p in (raw[:2] if side == 0 else raw[2:])]


def put_together(rows, refs, out_ref, source=slice(None), target=slice(None)):
    z, x = here(rows)
    at = 0
    for ref, x_flip in zip(refs, (0, 1, 1)):
        for k in range(ref.shape[0]):
            n = ref.shape[1]
            slot = k + (at if x_flip else 0)
            row = (flip(z, slot) * 2 + flip(x, x_flip)) * n
            out_ref[pl.ds(pl.multiple_of(row, n), n), target] = ref[k, :, source]
        at += ref.shape[0] * x_flip


def turn_kernel(rows, a_ref, b_ref, out_ref):
    tokens, width = a_ref.shape
    n = width // BLOCKS
    for half, ref in enumerate((a_ref, b_ref)):
        turned = ref[...].T
        for block in range(BLOCKS):
            at = pl.multiple_of(slot_of(rows, block) * n, n)
            out_ref[pl.ds(at, n), half * tokens : (half + 1) * tokens] = turned[
                block * n : (block + 1) * n, :
            ]


def turn(a, b, rows):
    tokens, width = a.shape
    return call(
        partial(turn_kernel, rows),
        out_shape=jax.ShapeDtypeStruct((width, 2 * tokens), BF16),
        cost_estimate=cost(
            flops=0, bytes_accessed=8 * tokens * width, transcendentals=0
        ),
        name="turn",
    )(a, b)


GRAD_PARTS = {0: (2, 2), 1: (2, 4, 4)}


def store_parts(grads, refs):
    at = 0
    for ref in refs:
        ref[...] = grads[at : at + ref.shape[0]].astype(BF16)
        at += ref.shape[0]


def grad_shapes(width, c):
    return [jax.ShapeDtypeStruct((width // f, c), BF16) for side in (0, 1) for f in GRAD_PARTS[side]]


def pair_sources(pair):
    return {0: [(0, 0, 2)], 1: [(0, 2, 1), (1, 2, 1)], 2: [(1, 0, 2)]}[pair]


Q_BIAS, V_BIAS, UP_BIAS = range(3)


def attend_forward_kernel(rows, pair, *refs):
    *refs, q_ref, k_ref, v_ref, w_ref, mixed_ref, lse_ref, vt_ref = refs
    xa_ref, xb_ref, *raw, own_ref, other_ref = refs
    raw = {0: [raw], 1: [raw[:2], raw[2:]], 2: [raw]}[pair]
    d = HEAD_DIM
    two = 2 * d
    tokens = xa_ref.shape[0]
    step = pl.program_id(0)
    block = mixed_ref.shape[0]

    @pl.when(step == 0)
    def _():
        for kind in range(4):
            at = kind * two
            for pieces, (_, first, heads) in zip(raw, pair_sources(pair)):
                source = (kind * 3 + first) * d
                put_together(
                    rows,
                    pieces,
                    w_ref,
                    slice(source, source + heads * d),
                    slice(at, at + heads * d),
                )
                at += heads * d
        bias = []
        for row in (Q_BIAS, None, V_BIAS):
            for side, first, heads in pair_sources(pair):
                cols = slice(first * d, (first + heads) * d)
                if row is None:
                    bias.append(jnp.zeros((1, heads * d), F32))
                else:
                    bias.append((own_ref, other_ref)[side][row : row + 1, cols])
        bias = jnp.concatenate(bias, axis=1)
        for half, ref in enumerate((xa_ref, xb_ref)):
            at = slice(half * tokens, (half + 1) * tokens)
            proj = (dot_nn(ref[...], w_ref[:, : 3 * two]) + bias).astype(BF16)
            q_ref[at, :] = proj[:, :two]
            k_ref[at, :] = proj[:, two : 2 * two]
            v_ref[at, :] = proj[:, 2 * two :]
        turned = v_ref[...].T
        for head in range(2):
            vt_ref[head, :d, :] = turned[head * d : (head + 1) * d, :]
            vt_ref[head, d:, :] = jnp.ones((vt_ref.shape[1] - d, turned.shape[1]), BF16)

    query = q_ref[pl.ds(pl.multiple_of(step * block, block), block), :]
    lane = lax.broadcasted_iota(jnp.int32, query.shape, 1)
    outs = []
    for head in range(2):
        masked = jnp.where(lane // d == head, query, jnp.zeros_like(query)) * BF16(d**-0.5)
        scores = dot_nt(k_ref[...], masked)
        top = jnp.max(scores, axis=0, keepdims=True)
        weights = jnp.exp2((scores - top) * LOG2E).astype(BF16)
        out = dot_nn(vt_ref[head], weights)
        total = out[d : d + 1, :]
        outs.append(out[:d, :] * (1.0 / total))
        lse_ref[head : head + 1, :] = top + jnp.log(total)
    mixed_ref[...] = jnp.concatenate(outs, axis=0).T.astype(BF16)


def attend_forward(xa, xb, raw, own, other, rows, pair):
    tokens, width = xa.shape
    seq = 2 * tokens
    two = 2 * HEAD_DIM
    block = 512
    part = jax.ShapeDtypeStruct((seq, two), BF16)
    weight = jax.ShapeDtypeStruct((width, 4 * two), BF16)
    ins = [xa, xb, *side_pieces(raw, [side for side, *_ in pair_sources(pair)]), own, other]
    return call(
        partial(attend_forward_kernel, rows, pair),
        grid=(seq // block,),
        in_specs=[whole(a.shape) for a in ins],
        out_specs=[
            whole(part.shape),
            whole(part.shape),
            whole(part.shape),
            whole(weight.shape),
            pl.BlockSpec((block, two), lambda i: (i, 0)),
            pl.BlockSpec((8, block), lambda i: (0, i)),
        ],
        out_shape=[part, part, part, weight, part, jax.ShapeDtypeStruct((8, seq), F32)],
        scratch_shapes=[pltpu.VMEM((2, HEAD_DIM + 16, seq), BF16)],
        cost_estimate=cost(
            flops=24 * seq * seq * two, bytes_accessed=16 * seq * width, transcendentals=seq * seq
        ),
        name=f"attend_forward_{pair}",
    )(*ins)


def attend_backward_kernel(rows, pair, *refs):
    q_ref, k_ref, v_ref, w_ref, ga_ref, gb_ref, turned_ref, mixed_ref, lse_ref = refs[:9]
    kt_ref, dk_acc, dv_acc, gmix_ref, gall_ref, out_ref = refs[-6:]
    *grads_refs, dproj_ref, sum_ref = refs[9:-6]
    step = pl.program_id(0)
    d = HEAD_DIM
    two = 2 * d
    scale = d**-0.5
    tokens = ga_ref.shape[0]
    block = lse_ref.shape[1]

    @pl.when(step == 0)
    def _():
        kt_ref[...] = k_ref[...].T
        dk_acc[...] = jnp.zeros_like(dk_acc)
        dv_acc[...] = jnp.zeros_like(dv_acc)
        for half, ref in enumerate((ga_ref, gb_ref)):
            at = slice(half * tokens, (half + 1) * tokens)
            gall_ref[at, :] = ref[...]
            gmix_ref[at, :] = dot_nn(ref[...], w_ref[:, 3 * two :]).astype(BF16)

    here_rows = pl.ds(pl.multiple_of(step * block, block), block)
    query = q_ref[here_rows, :]
    grad = gmix_ref[here_rows, :]
    lane = lax.broadcasted_iota(jnp.int32, query.shape, 1)
    dots = (grad.astype(F32) * mixed_ref[here_rows, :].astype(F32)).T
    dqs = []
    for head in range(2):
        mine = lane // d == head
        query_h = jnp.where(mine, query, jnp.zeros_like(query))
        grad_h = jnp.where(mine, grad, jnp.zeros_like(grad))
        row_dots = jnp.sum(dots[head * d : (head + 1) * d, :], axis=0, keepdims=True)
        log_total = lse_ref[head : head + 1, :] * LOG2E
        scores = dot_nt(k_ref[...], query_h * BF16(scale))
        probs = jnp.exp2(scores * LOG2E - log_total)
        grad_probs = dot_nt(v_ref[...], grad_h)
        grad_scores = (probs * (grad_probs - row_dots)).astype(BF16)
        dv_acc[...] += dot_nn(probs.astype(BF16), grad_h)
        dk_acc[...] += dot_nn(grad_scores, query_h)
        dqs.append(dot_nn(kt_ref[head * d : (head + 1) * d, :], grad_scores) * scale)
    dproj_ref[here_rows, :two] = jnp.concatenate(dqs, axis=0).T.astype(BF16)

    @pl.when(step == pl.num_programs(0) - 1)
    def _():
        dproj_ref[:, two : 2 * two] = (dk_acc[...] * scale).astype(BF16)
        dproj_ref[:, 2 * two :] = dv_acc[...].astype(BF16)
        dproj = dproj_ref[...]
        sum_ref[0:1, :] = jnp.sum(dproj.astype(F32), axis=0, keepdims=True)
        out_ref[:, : 3 * two] = dot_nn(turned_ref[...], dproj).astype(BF16)
        grads = dot_nn(mixed_ref[...].T, gall_ref[...]).T.astype(BF16)
        n = grads.shape[0] // BLOCKS
        for at_block in range(BLOCKS):
            at = pl.multiple_of(slot_of(rows, at_block) * n, n)
            out_ref[pl.ds(at, n), 3 * two :] = grads[at_block * n : (at_block + 1) * n, :]
        if pair != 1:
            store_parts(out_ref[...], grads_refs)
        else:
            for kind in range(4):
                for side, ref in enumerate(grads_refs):
                    ref[:, kind * d : (kind + 1) * d] = out_ref[
                        :, kind * two + side * d : kind * two + (side + 1) * d
                    ]


def attend_backward(q, k, v, w, ga, gb, turned, mixed, lse, rows, pair):
    seq, two = q.shape
    width = ga.shape[1]
    block = 256
    grads = (width, 2 * two) if pair == 1 else (width // 2, 4 * two)
    outs = [jax.ShapeDtypeStruct(grads, BF16)] * 2 + [
        jax.ShapeDtypeStruct((seq, 3 * two), BF16),
        jax.ShapeDtypeStruct((8, 3 * two), F32),
    ]
    ins = [q, k, v, w, ga, gb, turned, mixed]
    *grads, dproj, sums = call(
        partial(attend_backward_kernel, rows, pair),
        grid=(seq // block,),
        in_specs=[whole(a.shape) for a in ins] + [pl.BlockSpec((8, block), lambda i: (0, i))],
        out_specs=[whole(o.shape) for o in outs],
        out_shape=outs,
        scratch_shapes=[
            pltpu.VMEM((two, seq), BF16),
            pltpu.VMEM((seq, two), F32),
            pltpu.VMEM((seq, two), F32),
            pltpu.VMEM((seq, two), BF16),
            pltpu.VMEM((seq, width), BF16),
            pltpu.VMEM((width, 4 * two), BF16),
        ],
        cost_estimate=cost(
            flops=50 * seq * seq * two, bytes_accessed=16 * seq * width, transcendentals=seq * seq
        ),
        name=f"attend_backward_{pair}",
    )(*ins, lse)
    return grads, dproj, sums


def project_kernel(first, cols, *refs):
    count = (len(refs) - 1) // 2
    total = 0.0
    for part, weight in zip(refs[:count], refs[count:-1]):
        total = total + dot_nt(part[...], weight[...])
    refs[-1][...] = total.astype(refs[-1].dtype)


def project(parts, weights, half, first, dtype):
    seq, cols = parts[0].shape
    width = weights[0].shape[0]
    tokens = seq // 2
    return call(
        partial(project_kernel, first, cols),
        grid=(1,),
        in_specs=[pl.BlockSpec((tokens, cols), lambda i: (half, 0)) for _ in parts]
        + [pl.BlockSpec((width, cols), lambda i: (0, first // cols)) for _ in weights],
        out_specs=whole((tokens, width)),
        out_shape=jax.ShapeDtypeStruct((tokens, width), dtype),
        cost_estimate=cost(
            flops=2 * tokens * width * cols * 3, bytes_accessed=0, transcendentals=0
        ),
        name="project",
    )(*parts, *weights)


def statistics(rows):
    mean = jnp.mean(rows, axis=1, keepdims=True)
    centered = rows - mean
    inverse = lax.rsqrt(jnp.mean(jnp.square(centered), axis=1, keepdims=True) + EPSILON)
    return centered * inverse, inverse


def add_rows(sum_ref, values):
    @pl.when(pl.program_id(0) == 0)
    def _():
        sum_ref[...] = jnp.zeros_like(sum_ref)

    for i, value in enumerate(values):
        sum_ref[i : i + 1, :] += jnp.sum(value, axis=0, keepdims=True)


ATTN_GAIN, ATTN_SHIFT, MLP_GAIN, MLP_SHIFT, OUTPUT_BIAS, DOWN_BIAS = range(6)


def vector(ref, at):
    return ref[at : at + 1, :]


def norm_kernel(x_ref, vec_ref, out_ref):
    hat, _ = statistics(x_ref[...].astype(F32))
    out_ref[...] = (hat * vector(vec_ref, ATTN_GAIN) + vector(vec_ref, ATTN_SHIFT)).astype(BF16)


def resid_kernel(x_ref, own_ref, got_ref, vec_ref, resid_ref, out_ref, sum_ref):
    branch = own_ref[...] + got_ref[...].astype(F32) + vector(vec_ref, OUTPUT_BIAS)
    resid = x_ref[...].astype(F32) + branch
    resid_ref[...] = resid
    hat, _ = statistics(resid)
    out_ref[...] = (hat * vector(vec_ref, MLP_GAIN) + vector(vec_ref, MLP_SHIFT)).astype(BF16)
    add_rows(sum_ref, [branch * branch])


def result_kernel(resid_ref, own_ref, got_ref, vec_ref, out_ref, sum_ref):
    branch = own_ref[...] + got_ref[...].astype(F32) + vector(vec_ref, DOWN_BIAS)
    result = resid_ref[...] + branch
    out_ref[...] = result.astype(BF16)
    add_rows(sum_ref, [result * result, branch * branch])


def norm_gradient(grad, rows, gain):
    hat, inverse = statistics(rows)
    grad_hat = grad * gain
    first = jnp.mean(grad_hat, axis=1, keepdims=True)
    second = jnp.mean(grad_hat * hat, axis=1, keepdims=True)
    return inverse * (grad_hat - first - hat * second), grad * hat


def middle_kernel(resid_ref, own_ref, got_ref, cot_ref, vec_ref, grad_ref, low_ref, sum_ref):
    grad = own_ref[...] + got_ref[...].astype(F32)
    back, gains = norm_gradient(grad, resid_ref[...], vector(vec_ref, MLP_GAIN))
    cot = cot_ref[...].astype(F32)
    hidden = cot + back
    grad_ref[...] = hidden
    low = hidden.astype(BF16)
    low_ref[...] = low
    add_rows(sum_ref, [gains, grad, low.astype(F32), cot])


def last_kernel(x_ref, own_ref, got_ref, hidden_ref, vec_ref, grad_ref, sum_ref):
    grad = own_ref[...] + got_ref[...].astype(F32)
    back, gains = norm_gradient(grad, x_ref[...].astype(F32), vector(vec_ref, ATTN_GAIN))
    grad_ref[...] = hidden_ref[...] + back
    add_rows(sum_ref, [gains, grad])


def attention_sum_kernel(own_ref, *refs):
    *got_refs, qkv_ref, out_ref = refs
    d = HEAD_DIM
    total = own_ref[...]
    for ref in got_refs:
        total = total + ref[...].astype(F32)
    for kind in range(4):
        large = total[:, 2 * d * kind : 2 * d * (kind + 1)]
        small = total[:, d * (8 + kind) : d * (9 + kind)]
        if kind < 3:
            qkv_ref[:, kind, : 2 * d] = large
            qkv_ref[:, kind, 2 * d :] = small
        else:
            out_ref[:, : 2 * d] = large
            out_ref[:, 2 * d :] = small


def attention_sum(own, got):
    n = own.shape[0]
    side = 3 * HEAD_DIM
    return call(
        attention_sum_kernel,
        out_shape=[
            jax.ShapeDtypeStruct((n, 3, side), F32),
            jax.ShapeDtypeStruct((n, side), F32),
        ],
        cost_estimate=cost(flops=0, bytes_accessed=0, transcendentals=0),
        name="attention_sum",
    )(own, *got)


def small_sums_kernel(entries, own_ref, got_ref, *outs):
    total = own_ref[...] + got_ref[...]
    *vector_refs, qkv_ref, rms_ref = outs
    for ref, row in zip(vector_refs, (7, 8, 2, 0, 1, 10, 3)):
        ref[...] = total[row]
    side = qkv_ref.shape[1]
    qkv_ref[0:1, :] = total[9:10, :side]
    qkv_ref[1:2, :] = total[9:10, side : 2 * side]
    means = jnp.sum(total[4:7, :], axis=1, keepdims=True) / entries
    means = jnp.broadcast_to(jnp.sqrt(means), (3, rms_ref.shape[1]))
    rms_ref[0:1, :] = means[1:2]
    rms_ref[1:2, :] = means[0:1]
    rms_ref[2:3, :] = means[2:3]


def small_sums(own, got, side, entries):
    width = own.shape[1]
    return call(
        partial(small_sums_kernel, entries),
        out_shape=[jax.ShapeDtypeStruct((width,), F32)] * 7
        + [jax.ShapeDtypeStruct((2, side), F32), jax.ShapeDtypeStruct((3, 128), F32)],
        cost_estimate=cost(flops=0, bytes_accessed=0, transcendentals=0),
        name="small_sums",
    )(own, got)


def by_rows(kernel, name, rows, vectors, outs, sums=False):
    tokens, width = rows[0].shape
    block = tokens // 2
    part = pl.BlockSpec((block, width), lambda i: (i, 0))
    out_shape = [jax.ShapeDtypeStruct((tokens, width), t) for t in outs]
    out_specs = [part] * len(outs)
    if sums:
        out_shape.append(jax.ShapeDtypeStruct((8, width), F32))
        out_specs.append(whole((8, width)))
    return call(
        kernel,
        grid=(tokens // block,),
        in_specs=[part] * len(rows) + [whole(vectors.shape)],
        out_specs=out_specs,
        out_shape=out_shape,
        cost_estimate=cost(flops=0, bytes_accessed=0, transcendentals=0),
        name=name,
    )(*rows, vectors)


def gelu_parts(u):
    c0 = math.sqrt(2.0 / math.pi)
    square = u * u
    t = jnp.tanh(u * (c0 + (c0 * 0.044715) * square))
    half = 0.5 * u
    act = half + half * t
    slope = 0.5 + 0.5 * t + half * (1.0 - t * t) * (c0 + (3.0 * c0 * 0.044715) * square)
    return act, slope


def up_kernel(rows, side, *refs):
    xa_ref, xb_ref, turned_ref, *raw, bias_ref, act_ref, slope_ref = refs[: -1 - len(GRAD_PARTS[side])]
    outs, w_ref = refs[-1 - len(GRAD_PARTS[side]) : -1], refs[-1]
    tokens = xa_ref.shape[0]
    put_together(rows, raw, w_ref)
    for half, ref in enumerate((xa_ref, xb_ref)):
        act, slope = gelu_parts(dot_nn(ref[...], w_ref[...]) + vector(bias_ref, UP_BIAS))
        act_ref[half * tokens : (half + 1) * tokens, :] = act.astype(BF16)
        slope_ref[half * tokens : (half + 1) * tokens, :] = slope.astype(BF16)
    store_parts(dot_nn(turned_ref[...], act_ref[...]), outs)


TILE = 256


def tiles(*dims):
    return pl.BlockSpec((*dims, TILE), lambda j: (0,) * len(dims) + (j,))


def raw_tiles(raw):
    return [tiles(*r.shape[:2]) for r in raw]


def up_and_down_grads(xa, xb, turned, raw, bias, rows, side):
    tokens, width = xa.shape
    c = bias.shape[1]
    hidden = jax.ShapeDtypeStruct((2 * tokens, c), BF16)
    grads = [jax.ShapeDtypeStruct((width // f, c), BF16) for f in GRAD_PARTS[side]]
    raw = side_pieces(raw, [side])
    act, slope, *grads = call(
        partial(up_kernel, rows, side),
        grid=(c // TILE,),
        in_specs=[whole(xa.shape), whole(xb.shape), whole(turned.shape)]
        + raw_tiles(raw)
        + [tiles(8)],
        out_specs=[tiles(2 * tokens)] * 2 + [tiles(g.shape[0]) for g in grads],
        out_shape=[hidden] * 2 + grads,
        scratch_shapes=[pltpu.VMEM((width, TILE), BF16)],
        cost_estimate=cost(
            flops=8 * tokens * width * c, bytes_accessed=0, transcendentals=2 * tokens * c
        ),
        name=f"up_and_down_grads_{side}",
    )(xa, xb, turned, *raw, bias)
    return act, slope, grads


def hidden_back_kernel(rows, side, *refs):
    ga_ref, gb_ref, *raw = refs[: 6 + 2 * side]
    down, up = raw[: len(raw) // 2], raw[len(raw) // 2 :]
    slope_ref, *before, pre_ref, sum_ref = refs[6 + 2 * side : 9 + 3 * side]
    *outs, acc_ref, w_ref, u_ref = refs[9 + 3 * side :]
    step = pl.program_id(0)
    tokens = ga_ref.shape[0]

    @pl.when(step == 0)
    def _():
        acc_ref[...] = before[0][...] if side else jnp.zeros_like(acc_ref)

    put_together(rows, down, w_ref)
    put_together(rows, up, u_ref)
    totals = 0.0
    for half, ref in enumerate((ga_ref, gb_ref)):
        at = slice(half * tokens, (half + 1) * tokens)
        back = dot_nn(ref[...], w_ref[...]) * slope_ref[at, :].astype(F32)
        pre = back.astype(BF16)
        pre_ref[at, :] = pre
        totals = totals + jnp.sum(pre.astype(F32), axis=0, keepdims=True)
        acc_ref[at, :] += dot_nt(pre, u_ref[...])
    sum_ref[0:1, :] = totals

    @pl.when(step == pl.num_programs(0) - 1)
    def _():
        if side:
            outs[0][...] = acc_ref[:tokens, :]
            outs[1][...] = acc_ref[tokens:, :].astype(BF16)
        else:
            outs[0][...] = acc_ref[...]


def hidden_back(ga, gb, down, up, slope, before, rows, side):
    tokens, width = ga.shape
    seq, c = slope.shape
    if side:
        backs = [jax.ShapeDtypeStruct(ga.shape, t) for t in (F32, BF16)]
    else:
        backs = [jax.ShapeDtypeStruct((seq, width), F32)]
    return call(
        partial(hidden_back_kernel, rows, side),
        grid=(c // TILE,),
        in_specs=[whole(ga.shape), whole(gb.shape)]
        + raw_tiles(down)
        + raw_tiles(up)
        + [tiles(seq)]
        + [whole(b.shape) for b in before],
        out_specs=[tiles(seq), tiles(8)] + [whole(b.shape) for b in backs],
        out_shape=[jax.ShapeDtypeStruct((seq, c), BF16), jax.ShapeDtypeStruct((8, c), F32)] + backs,
        scratch_shapes=[
            pltpu.VMEM((seq, width), F32),
            pltpu.VMEM((width, TILE), BF16),
            pltpu.VMEM((width, TILE), BF16),
        ],
        cost_estimate=cost(
            flops=8 * tokens * width * c, bytes_accessed=12 * tokens * c, transcendentals=0
        ),
        name=f"hidden_back_{side}",
    )(ga, gb, *down, *up, slope, *before)


def mlp_out_kernel(rows, *refs):
    act_ref, act_o_ref = refs[:2]
    down = refs[2:7]
    own_ref, other_ref, acc_ref, w_ref = refs[7:]
    step = pl.program_id(0)
    tokens = own_ref.shape[0]

    @pl.when(step == 0)
    def _():
        acc_ref[...] = jnp.zeros_like(acc_ref)

    put_together(rows, down[:2], w_ref.at[0])
    put_together(rows, down[2:], w_ref.at[1])
    acc_ref[...] += dot_nt(act_ref[...], w_ref[0]) + dot_nt(act_o_ref[...], w_ref[1])

    @pl.when(step == pl.num_programs(0) - 1)
    def _():
        own_ref[...] = acc_ref[:tokens, :]
        other_ref[...] = acc_ref[tokens:, :].astype(BF16)


def mlp_out(act, act_o, down, width, rows):
    seq, c = act.shape
    outs = [jax.ShapeDtypeStruct((seq // 2, width), t) for t in (F32, BF16)]
    return call(
        partial(mlp_out_kernel, rows),
        grid=(c // TILE,),
        in_specs=[tiles(seq)] * 2 + raw_tiles(down),
        out_specs=[whole(o.shape) for o in outs],
        out_shape=outs,
        scratch_shapes=[pltpu.VMEM((seq, width), F32), pltpu.VMEM((2, width, TILE), BF16)],
        cost_estimate=cost(
            flops=4 * seq * width * c, bytes_accessed=4 * seq * c, transcendentals=0
        ),
        name="mlp_out",
    )(act, act_o, *down)


def weight_grads_kernel(turned_ref, g_ref, go_ref, *outs):
    store_parts(dot_nn(turned_ref[...], g_ref[...]), outs[:2])
    store_parts(dot_nn(turned_ref[...], go_ref[...]), outs[2:])


def weight_grads(turned, grad, grad_o):
    width, seq = turned.shape
    c = grad.shape[1]
    return call(
        weight_grads_kernel,
        grid=(c // TILE,),
        in_specs=[whole(turned.shape), tiles(seq), tiles(seq)],
        out_specs=[tiles(s.shape[0]) for s in grad_shapes(width, c)],
        out_shape=grad_shapes(width, c),
        cost_estimate=cost(
            flops=4 * seq * width * c, bytes_accessed=6 * seq * c, transcendentals=0
        ),
        name="weight_grads",
    )(turned, grad, grad_o)


def make_local(rows):
    low, near = rows[-1], rows[:-1]
    fast = 2 ** len(rows) == BLOCKS
    order = rows if fast else None

    def to_blocks(parts):
        width, c = parts[0].shape[0] * 2, parts[0].shape[1]
        return [p.reshape(-1, width // BLOCKS, c) for p in parts]

    def reduce_plain(parts):
        blocks = to_blocks(parts)
        own = jnp.stack(blocks[:2], axis=1)
        other = jnp.stack([blocks[2], jnp.concatenate(blocks[3:])], axis=1)
        width, c = parts[0].shape[0] * 2, parts[0].shape[1]
        return scatter_rows(own.reshape(width, c), other.reshape(width, c), rows)

    def natural(grads):
        width, c = grads.shape
        blocks = grads.reshape(2, BLOCKS // 2, width // BLOCKS, c)
        return jnp.swapaxes(blocks, 0, 1).reshape(width, c)

    def local(
        layer_input,
        attn_gain,
        attn_shift,
        qkv_weight,
        qkv_bias,
        output_weight,
        output_bias,
        mlp_gain,
        mlp_shift,
        up_weight,
        up_bias,
        down_weight,
        down_bias,
        cotangent,
    ):
        tokens, width = layer_input.shape
        n, _, side = qkv_weight.shape
        hidden = up_weight.shape[1]
        d = HEAD_DIM

        attn_shard = jnp.concatenate([qkv_weight.reshape(n, -1), output_weight], axis=1)
        vectors = table_of(attn_gain, attn_shift, mlp_gain, mlp_shift, output_bias, down_bias)
        (attn_in,) = by_rows(norm_kernel, "norm", [layer_input], vectors, [BF16])
        attn_in_other = swap(attn_in, "core")
        cot_other = swap(cotangent, "core")
        bias_own = jnp.pad(qkv_bias, ((0, 6), (0, hidden - side)))
        bias_own = bias_own + jnp.pad(up_bias[None, :], ((UP_BIAS, 7 - UP_BIAS), (0, 0)))
        bias_other = swap(bias_own, "y")
        if fast:
            attn_near = gather_near(attn_shard, near)
            attn_near = after(attn_near, cot_other, bias_other)
            attn_stack = jnp.stack(attn_near)
            mlp_near = gather_near(jnp.stack([up_weight, down_weight]), near)
            attn_far = gather_far(attn_stack, low)
            attn_raw = gather_corners(attn_far, low)
        else:
            attn_raw, up_raw, down_raw = (
                gather_plain(w, rows) for w in (attn_shard, up_weight, down_weight)
            )
        halves = (attn_in, attn_in_other, cotangent, cot_other)
        if fast:
            halves = after(halves, attn_stack)
        attn_turned = turn(*halves[:2], order)
        cot_turned = turn(*halves[2:], order)
        attended = []
        for pair in range(3):
            bias = bias_own
            if fast and pair == 0:
                bias = after(bias, attn_far, attn_turned, cot_turned)
            if pair:
                bias = after(bias, attended[pair - 1][4])
            if fast and pair == 1:
                mlp_near = after(mlp_near, attended[0][4], attn_raw)
                up_far = gather_far(jnp.stack([m[0] for m in mlp_near]), low)
                down_stack = jnp.stack([m[1] for m in mlp_near])
                bias = after(bias, up_far[0], down_stack)
            attended.append(
                attend_forward(attn_in, attn_in_other, attn_raw, bias, bias_other, order, pair)
            )
        mixed = [a[4] for a in attended]
        weights = [a[3] for a in attended]
        if fast:
            mixed, up_far = after((mixed, up_far))
            up_raw = gather_corners(up_far, low)
        got = swap(project(mixed, weights, 1, 6 * d, BF16), "core")
        own = project(mixed, weights, 0, 6 * d, F32)
        hidden_resid, mlp_in, branch_sums = by_rows(
            resid_kernel,
            "resid",
            [layer_input, own, got],
            vectors,
            [F32, BF16],
            True,
        )
        mlp_in_other = swap(mlp_in, "core")
        if fast:
            down_far = gather_far(after(down_stack, mlp_in_other), low)
        ins = (mlp_in, mlp_in_other, cot_turned)
        grads = (cotangent, cot_other)
        act, slope, down_own = up_and_down_grads(*ins, up_raw, bias_own, order, 0)
        if fast:
            down_raw = gather_corners(after(down_far, act), low)
        pre, up_sums, back = hidden_back(*grads, down_raw[:2], up_raw[:2], slope, (), order, 0)
        bias_other = after(bias_other, pre)
        act_o, slope_o, down_other = up_and_down_grads(*ins, up_raw, bias_other, order, 1)
        down_parts = down_own + down_other
        if fast:
            down_parts = to_blocks(down_parts)
            down_got = reduce_corners(down_parts, low)
        else:
            down_grad = reduce_plain(down_parts)
        pre_o, up_sums_o, back, back_other = hidden_back(
            *grads, down_raw[2:], up_raw[2:], slope_o, (back,), order, 1
        )
        back_got = swap(back_other, "core")
        mlp_turned = turn(*after((mlp_in, mlp_in_other), pre_o), order)
        up_parts = weight_grads(mlp_turned, pre, pre_o)
        if fast:
            up_parts = to_blocks(up_parts)
            up_got = reduce_corners(up_parts, low)
        else:
            up_grad = reduce_plain(up_parts)
        hidden_grad, grad_attn, middle_sums = by_rows(
            middle_kernel,
            "middle",
            [hidden_resid, after(back, up_parts), back_got, cotangent],
            vectors,
            [F32, BF16],
            True,
        )
        grad_attn_other = swap(grad_attn, "core")
        if fast:
            down_sent = reduce_far(down_parts, after(down_got, grad_attn), low)

        half, block = width // 2, width // BLOCKS
        pair_grads, pair_sums, dprojs = {}, {}, {}
        for pair in (2, 1, 0):
            q, k, v, w, mix, lse = attended[pair]
            if pair != 2:
                lse = after(lse, pair_grads[pair + 1])
            if fast and pair == 1:
                lse, down_sent = after((lse, down_sent))
                total = down_parts[0].astype(F32) + sum(g.astype(F32) for g in down_sent)
                down_sum, down_got = total[:2], swap(total[2:].astype(BF16), near[0])
            if fast and pair == 0:
                lse, large_got, up_got = after((lse, large_got, up_got))
                up_sent = reduce_far(up_parts, up_got, low)
                large_y = (pair_grads[2][0].astype(F32) + large_got.astype(F32)).astype(BF16)
                large_y = swap(large_y, "y")
            pair_grads[pair], dprojs[pair], pair_sums[pair] = attend_backward(
                q, k, v, w, grad_attn, grad_attn_other, attn_turned, mix, lse, order, pair
            )
            if fast and pair == 2:
                large_got = swap(pair_grads[2][1], low)

        dprojs = [dprojs[pair] for pair in range(3)]
        if fast:
            large_x = swap(pair_grads[0][1], low)
            small_got = swap(pair_grads[1][1], "y")
            up_sent, dprojs, down_got = after((up_sent, dprojs, down_got), pair_grads[0])
            down_sum = down_sum + down_got.astype(F32)
            down_got = swap(down_sum[1].astype(BF16), near[1])
            total = up_parts[0].astype(F32) + sum(g.astype(F32) for g in up_sent)
            up_sum, up_got = total[:2], swap(total[2:].astype(BF16), near[0])
        act, act_o = after((act, act_o), pair_grads[0])
        branch, branch_other = mlp_out(act, act_o, down_raw, width, order)
        branch_got = swap(branch_other, "core")
        back_other = project(after(dprojs, branch), weights, 1, 0, BF16)
        got = swap(back_other, "core")
        own = project(after(dprojs, back_other), weights, 0, 0, F32)
        layer_output, result_sums = by_rows(
            result_kernel,
            "result",
            [hidden_resid, after(branch, own), branch_got],
            vectors,
            [BF16],
            True,
        )
        if fast:
            small = pair_grads[1][0].astype(F32) + after(small_got, own).astype(F32)
            small_x = swap(small[half:].astype(BF16), low)
            large_sent, small_sent = (large_x, large_y), small_x
            own, large_sent, small_sent, down_got, got = after(
                (own, large_sent, small_sent, down_got, got), layer_output
            )
        input_grad, last_sums = by_rows(
            last_kernel, "last", [layer_input, own, got, hidden_grad], vectors, [F32], True
        )
        if fast:
            up_got, last_sums = after((up_got, last_sums))
        if not fast:
            own, other = (
                natural(jnp.concatenate(p, axis=1))
                for p in (
                    (jnp.concatenate(pair_grads[0]), pair_grads[1][0]),
                    (jnp.concatenate(pair_grads[2]), pair_grads[1][1]),
                )
            )
            attn_grad = scatter_rows(own, other, rows)

        def bias_row(large, small, at):
            row = 0.0
            for i, kind in enumerate((0, 2)):
                source = 2 * d * kind
                for piece, to in (
                    (large[:1, source : source + 2 * d], 0),
                    (small[:1, source + at : source + at + d], 2 * d),
                ):
                    to = i * side + to
                    row = row + jnp.pad(piece, ((0, 0), (to, width - to - piece.shape[1])))
            return row
        common = jnp.concatenate(
            [middle_sums[:4], branch_sums[:1], result_sums[:2], last_sums[:2]], axis=0
        )
        common = common + swap(common, "core")
        own = jnp.concatenate([common, bias_row(pair_sums[0], pair_sums[1], 0), up_sums[:1]], axis=0)
        other = jnp.concatenate([common, bias_row(pair_sums[2], pair_sums[1], d), up_sums_o[:1]], axis=0)
        sums = own + swap(other, "y")
        if fast:
            large = pair_grads[0][0].astype(F32) + sum(g.astype(F32) for g in large_sent)
            small = small[:half] + small_sent.astype(F32)
            both = jnp.concatenate([large, small], axis=1).reshape(-1, block, 12 * d)
            attn_near = send_near(both, near)
            total = up_sum + up_got.astype(F32)
            up_grad = total[0] + swap(total[1].astype(BF16), near[1]).astype(F32)
            down_grad = down_sum[0] + down_got.astype(F32)
        for axis in reversed(rows[1:]):
            sums = sums + swap(sums, axis)
        entries = float(tokens * 2 ** (len(rows) + 2) * width)
        *vecs, qkv_bias_grad, rms_values = small_sums(sums, swap(sums, rows[0]), side, entries)
        if fast:
            qkv_grad, output_grad = attention_sum(attn_near[0], attn_near[1].values())
        else:
            qkv_grad, output_grad = attention_sum(attn_grad, ())
        return (
            layer_output,
            input_grad,
            vecs[0],
            vecs[1],
            qkv_grad,
            qkv_bias_grad,
            output_grad,
            vecs[2],
            vecs[3],
            vecs[4],
            up_grad,
            vecs[5],
            down_grad,
            vecs[6],
            rms_values[:, 0],
        )

    return local


def solution(mesh):
    row_size, col_size = mesh.shape["row"], mesh.shape["col"]
    bits = row_size.bit_length() - 1
    rows = tuple(f"r{b}" for b in reversed(range(bits)))
    cube = Mesh(mesh.devices.reshape((2,) * bits + (col_size // 2, 2)), rows + ("y", "core"))
    col = ("y", "core")
    every = rows + col
    placed = (
        P(every, None),
        P(),
        P(),
        P(rows, None, col),
        P(None, col),
        P(rows, col),
        P(),
        P(),
        P(),
        P(rows, col),
        P(col),
        P(rows, col),
        P(),
        P(every, None),
    )
    return jax.shard_map(
        make_local(rows),
        mesh=cube,
        in_specs=placed,
        out_specs=(
            P(every, None),
            P(every, None),
            P(),
            P(),
            P(rows, None, col),
            P(None, col),
            P(rows, col),
            P(),
            P(),
            P(),
            P(rows, col),
            P(col),
            P(rows, col),
            P(),
            P(),
        ),
        check_vma=False,
    )
```

```python
import math
from functools import partial

import jax
import jax.numpy as jnp
from jax import lax
from jax.experimental import pallas as pl
from jax.experimental.pallas import tpu as pltpu
from jax.sharding import Mesh, PartitionSpec as P

HEAD_DIM = 64
EPSILON = 1e-06
SWAP = [(0, 1), (1, 0)]
LOG2E = math.log2(math.e)
BF16 = jnp.bfloat16
F32 = jnp.float32
VMEM_BYTES = 16 * 2**20


def call(kernel, **kwargs):
    params = pltpu.CompilerParams(vmem_limit_bytes=VMEM_BYTES)
    return pl.pallas_call(kernel, compiler_params=params, **kwargs)


def cost(flops, bytes_accessed, transcendentals):
    return pl.CostEstimate(flops=0, bytes_accessed=0, transcendentals=0)


def after(arrays, *others):
    return lax.optimization_barrier((arrays, others))[0]


def table_of(*vectors):
    row = lax.broadcasted_iota(jnp.int32, (8, vectors[0].shape[0]), 0)
    out = jnp.zeros(row.shape, F32)
    for i, v in enumerate(vectors):
        out = jnp.where(row == i, v[None, :], out)
    return out


def swap(array, axis):
    return lax.ppermute(array, axis, SWAP)


def dot_nn(left, right):
    return lax.dot_general(left, right, (((1,), (0,)), ((), ())), preferred_element_type=F32)


def dot_nt(left, right):
    return lax.dot_general(left, right, (((1,), (1,)), ((), ())), preferred_element_type=F32)


def dot_tn(left, right):
    return lax.dot_general(left, right, (((0,), (0,)), ((), ())), preferred_element_type=F32)


def xor_exchange(blocks_of, axes):
    got = {}
    count = len(axes)
    sizes = [2] * count
    for bits in range(1, 2**count):
        perm = [(i, i ^ bits) for i in range(math.prod(sizes))]
        got[bits] = lax.ppermute(blocks_of(bits), axes, perm)
    return got


def in_order(own, got, axes):
    parts = [own] + [got[bits] for bits in range(1, 2 ** len(axes))]
    for depth, axis in enumerate(reversed(axes)):
        bit = 2**depth
        flip = lax.axis_index(axis) == 1
        parts = [jnp.where(flip, parts[i ^ bit], parts[i]) for i in range(len(parts))]
    return jnp.stack(parts)


def pair_in_order(own, other, axis, dim):
    flip = lax.axis_index(axis) == 1
    return jnp.stack([jnp.where(flip, other, own), jnp.where(flip, own, other)], axis=dim)


def gather_rows(shard, rows):
    low, high = rows[-1], rows[:-1]
    n, c = shard.shape
    near = high[-2:]
    stack = in_order(shard, xor_exchange(lambda bits: shard, near), near)
    for axis in reversed(high[:-2]):
        other = swap(stack, axis)
        stack = pair_in_order(stack, other, axis, 0).reshape(-1, n, c)
    half = c // 2
    first, second = stack[:, :, :half], stack[:, :, half:]
    first_low, second_y = swap(first, low), swap(second, "y")
    first = pair_in_order(first, first_low, low, 1).reshape(-1, half)
    first_y = swap(first, "y")
    second_low = swap(jnp.stack([second, second_y]), low)
    second_own = pair_in_order(second, second_low[0], low, 1).reshape(-1, half)
    second_other = pair_in_order(second_y, second_low[1], low, 1).reshape(-1, half)
    return (
        jnp.concatenate([first, second_own], axis=1),
        jnp.concatenate([first_y, second_other], axis=1),
    )


def pick(array, axis, dim, other):
    zero = lax.index_in_dim(array, 0, dim, keepdims=False)
    one = lax.index_in_dim(array, 1, dim, keepdims=False)
    flip = lax.axis_index(axis) == (0 if other else 1)
    return jnp.where(flip, one, zero)


def scatter_rows(own, other, rows):
    low, high = rows[-1], rows[:-1]
    near = high[-2:]
    total = 2 ** len(rows)
    n, c = own.shape[0] // total, own.shape[1]
    half = c // 2
    own = own.reshape(total // 2, 2, n, c)
    other = other.reshape(total // 2, 2, n, c)
    a_own, a_other = own[..., :half], other[..., :half]
    b_own, b_other = own[..., half:], other[..., half:]
    a_got = swap(a_other, "y")
    b_send = jnp.stack([pick(b_own, low, 1, True), pick(b_other, low, 1, True)])
    b_got = swap(b_send, low)
    a_sum = a_own.astype(F32) + a_got.astype(F32)
    a_send = pick(a_sum, low, 1, True).astype(BF16)
    b_own = pick(b_own, low, 1, False).astype(F32) + b_got[0].astype(F32)
    b_other = (pick(b_other, low, 1, False).astype(F32) + b_got[1].astype(F32)).astype(BF16)
    a_got = swap(a_send, low)
    b_got = swap(b_other, "y")
    a_sum = pick(a_sum, low, 1, False) + a_got.astype(F32)
    b_sum = b_own + b_got.astype(F32)
    both = jnp.concatenate([a_sum, b_sum], axis=2)
    for axis in high[:-2]:
        both = both.reshape(2, -1, n, c)
        got = swap(pick(both, axis, 0, True).astype(BF16), axis)
        both = pick(both, axis, 0, False) + got.astype(F32)
    low_both = both.astype(BF16)
    place = lax.axis_index(near)
    take = lambda bits: lax.dynamic_index_in_dim(low_both, place ^ bits, 0, keepdims=False)
    got = xor_exchange(take, near)
    out = lax.dynamic_index_in_dim(both, place, 0, keepdims=False)
    for piece in got.values():
        out = out + piece.astype(F32)
    return out


BLOCKS = 8


def gather_near(shard, near):
    got = xor_exchange(lambda bits: shard, near)
    return [shard] + [got[bits] for bits in range(1, 2 ** len(near))]


def gather_far(stack, low):
    return stack, swap(stack, low), swap(stack, "y")


def gather_corners(far, low):
    stack, from_low, from_y = far
    half = stack.shape[0] // 2
    return (*far, swap(from_low[:half], "y"), swap(from_y[half:], low))


def gather_plain(shard, rows):
    pieces = []
    for side in gather_rows(shard, rows):
        width, c = side.shape
        blocks = side.reshape(BLOCKS // 2, 2, width // BLOCKS, c)
        pieces += [blocks[:, 0], blocks[:, 1]]
    half = BLOCKS // 4
    return (*pieces[:3], pieces[3][:half], pieces[3][half:])


def reduce_corners(parts, low):
    return swap(parts[3], "y"), swap(parts[4], low)


def far_sums(parts, got):
    _, to_low, to_y, _, _ = parts
    half = to_low.shape[0] // 2
    add = lambda a, b: (a.astype(F32) + b.astype(F32)).astype(BF16)
    to_low = jnp.concatenate([add(to_low[:half], got[0]), to_low[half:]])
    to_y = jnp.concatenate([to_y[:half], add(to_y[half:], got[1])])
    return to_low, to_y


def reduce_far(parts, got, low):
    to_low, to_y = far_sums(parts, got)
    return swap(to_low, low), swap(to_y, "y")


def send_near(stack, near):
    low = stack.astype(BF16)
    return stack[0], xor_exchange(lambda bits: low[bits], near)


def sum_near(own, got):
    for piece in got.values():
        own = own + piece.astype(F32)
    return own


def here(rows):
    if rows is None:
        return 0, 0
    return lax.axis_index(rows[:-1]), lax.axis_index(rows[-1])


def flip(at, by):
    return by if isinstance(at, int) else lax.bitwise_xor(at, by)


def slot_of(rows, block):
    z, x = here(rows)
    block_z, block_x = divmod(block, 2)
    return flip(x, block_x) * (BLOCKS // 2) + flip(z, block_z)


def whole(shape):
    return pl.BlockSpec(shape, lambda *_: (0,) * len(shape))


def side_pieces(raw, sides):
    return [p for side in sides for p in (raw[:2] if side == 0 else raw[2:])]


def put_together(rows, refs, out_ref, source=slice(None), target=slice(None)):
    z, x = here(rows)
    at = 0
    for ref, x_flip in zip(refs, (0, 1, 1)):
        for k in range(ref.shape[0]):
            n = ref.shape[1]
            slot = k + (at if x_flip else 0)
            row = (flip(z, slot) * 2 + flip(x, x_flip)) * n
            out_ref[pl.ds(pl.multiple_of(row, n), n), target] = ref[k, :, source]
        at += ref.shape[0] * x_flip


def turn_kernel(rows, a_ref, b_ref, out_ref):
    tokens, width = a_ref.shape
    n = width // BLOCKS
    for half, ref in enumerate((a_ref, b_ref)):
        turned = ref[...].T
        for block in range(BLOCKS):
            at = pl.multiple_of(slot_of(rows, block) * n, n)
            out_ref[pl.ds(at, n), half * tokens : (half + 1) * tokens] = turned[
                block * n : (block + 1) * n, :
            ]


def turn(a, b, rows):
    tokens, width = a.shape
    return call(
        partial(turn_kernel, rows),
        out_shape=jax.ShapeDtypeStruct((width, 2 * tokens), BF16),
        cost_estimate=cost(
            flops=0, bytes_accessed=8 * tokens * width, transcendentals=0
        ),
        name="turn",
    )(a, b)


GRAD_PARTS = {0: (2, 2), 1: (2, 4, 4)}


def store_parts(grads, refs):
    at = 0
    for ref in refs:
        ref[...] = grads[at : at + ref.shape[0]].astype(BF16)
        at += ref.shape[0]


def grad_shapes(width, c):
    return [jax.ShapeDtypeStruct((width // f, c), BF16) for side in (0, 1) for f in GRAD_PARTS[side]]


def pair_sources(pair):
    return {0: [(0, 0, 2)], 1: [(0, 2, 1), (1, 2, 1)], 2: [(1, 0, 2)]}[pair]


Q_BIAS, V_BIAS, UP_BIAS = range(3)


def attend_forward_kernel(rows, pair, *refs):
    *refs, q_ref, k_ref, v_ref, w_ref, mixed_ref, lse_ref, vt_ref = refs
    xa_ref, xb_ref, *raw, own_ref, other_ref = refs
    raw = {0: [raw], 1: [raw[:2], raw[2:]], 2: [raw]}[pair]
    d = HEAD_DIM
    two = 2 * d
    tokens = xa_ref.shape[0]
    step = pl.program_id(0)
    block = mixed_ref.shape[0]

    @pl.when(step == 0)
    def _():
        for kind in range(4):
            at = kind * two
            for pieces, (_, first, heads) in zip(raw, pair_sources(pair)):
                source = (kind * 3 + first) * d
                put_together(
                    rows,
                    pieces,
                    w_ref,
                    slice(source, source + heads * d),
                    slice(at, at + heads * d),
                )
                at += heads * d
        bias = []
        for row in (Q_BIAS, None, V_BIAS):
            for side, first, heads in pair_sources(pair):
                cols = slice(first * d, (first + heads) * d)
                if row is None:
                    bias.append(jnp.zeros((1, heads * d), F32))
                else:
                    bias.append((own_ref, other_ref)[side][row : row + 1, cols])
        bias = jnp.concatenate(bias, axis=1)
        for half, ref in enumerate((xa_ref, xb_ref)):
            at = slice(half * tokens, (half + 1) * tokens)
            proj = (dot_nn(ref[...], w_ref[:, : 3 * two]) + bias).astype(BF16)
            q_ref[at, :] = proj[:, :two]
            k_ref[at, :] = proj[:, two : 2 * two]
            v_ref[at, :] = proj[:, 2 * two :]
        turned = v_ref[...].T
        for head in range(2):
            vt_ref[head, :d, :] = turned[head * d : (head + 1) * d, :]
            vt_ref[head, d:, :] = jnp.ones((vt_ref.shape[1] - d, turned.shape[1]), BF16)

    query = q_ref[pl.ds(pl.multiple_of(step * block, block), block), :]
    lane = lax.broadcasted_iota(jnp.int32, query.shape, 1)
    outs = []
    for head in range(2):
        masked = jnp.where(lane // d == head, query, jnp.zeros_like(query)) * BF16(d**-0.5)
        scores = dot_nt(k_ref[...], masked)
        top = jnp.max(scores, axis=0, keepdims=True)
        weights = jnp.exp2((scores - top) * LOG2E).astype(BF16)
        out = dot_nn(vt_ref[head], weights)
        total = out[d : d + 1, :]
        outs.append(out[:d, :] * (1.0 / total))
        lse_ref[head : head + 1, :] = top + jnp.log(total)
    mixed_ref[...] = jnp.concatenate(outs, axis=0).T.astype(BF16)


def attend_forward(xa, xb, raw, own, other, rows, pair):
    tokens, width = xa.shape
    seq = 2 * tokens
    two = 2 * HEAD_DIM
    block = 512
    part = jax.ShapeDtypeStruct((seq, two), BF16)
    weight = jax.ShapeDtypeStruct((width, 4 * two), BF16)
    ins = [xa, xb, *side_pieces(raw, [side for side, *_ in pair_sources(pair)]), own, other]
    return call(
        partial(attend_forward_kernel, rows, pair),
        grid=(seq // block,),
        in_specs=[whole(a.shape) for a in ins],
        out_specs=[
            whole(part.shape),
            whole(part.shape),
            whole(part.shape),
            whole(weight.shape),
            pl.BlockSpec((block, two), lambda i: (i, 0)),
            pl.BlockSpec((8, block), lambda i: (0, i)),
        ],
        out_shape=[part, part, part, weight, part, jax.ShapeDtypeStruct((8, seq), F32)],
        scratch_shapes=[pltpu.VMEM((2, HEAD_DIM + 16, seq), BF16)],
        cost_estimate=cost(
            flops=24 * seq * seq * two, bytes_accessed=16 * seq * width, transcendentals=seq * seq
        ),
        name=f"attend_forward_{pair}",
    )(*ins)


def attend_backward_kernel(rows, pair, *refs):
    q_ref, k_ref, v_ref, w_ref, ga_ref, gb_ref, turned_ref, mixed_ref, lse_ref = refs[:9]
    kt_ref, dk_acc, dv_acc, gmix_ref, gall_ref, out_ref = refs[-6:]
    *grads_refs, dproj_ref, sum_ref = refs[9:-6]
    step = pl.program_id(0)
    d = HEAD_DIM
    two = 2 * d
    scale = d**-0.5
    tokens = ga_ref.shape[0]
    block = lse_ref.shape[1]

    @pl.when(step == 0)
    def _():
        kt_ref[...] = k_ref[...].T
        dk_acc[...] = jnp.zeros_like(dk_acc)
        dv_acc[...] = jnp.zeros_like(dv_acc)
        for half, ref in enumerate((ga_ref, gb_ref)):
            at = slice(half * tokens, (half + 1) * tokens)
            gall_ref[at, :] = ref[...]
            gmix_ref[at, :] = dot_nn(ref[...], w_ref[:, 3 * two :]).astype(BF16)

    here_rows = pl.ds(pl.multiple_of(step * block, block), block)
    query = q_ref[here_rows, :]
    grad = gmix_ref[here_rows, :]
    lane = lax.broadcasted_iota(jnp.int32, query.shape, 1)
    dots = (grad.astype(F32) * mixed_ref[here_rows, :].astype(F32)).T
    dqs = []
    for head in range(2):
        mine = lane // d == head
        query_h = jnp.where(mine, query, jnp.zeros_like(query))
        grad_h = jnp.where(mine, grad, jnp.zeros_like(grad))
        row_dots = jnp.sum(dots[head * d : (head + 1) * d, :], axis=0, keepdims=True)
        log_total = lse_ref[head : head + 1, :] * LOG2E
        scores = dot_nt(k_ref[...], query_h * BF16(scale))
        probs = jnp.exp2(scores * LOG2E - log_total)
        grad_probs = dot_nt(v_ref[...], grad_h)
        grad_scores = (probs * (grad_probs - row_dots)).astype(BF16)
        dv_acc[...] += dot_nn(probs.astype(BF16), grad_h)
        dk_acc[...] += dot_nn(grad_scores, query_h)
        dqs.append(dot_nn(kt_ref[head * d : (head + 1) * d, :], grad_scores) * scale)
    dproj_ref[here_rows, :two] = jnp.concatenate(dqs, axis=0).T.astype(BF16)

    @pl.when(step == pl.num_programs(0) - 1)
    def _():
        dproj_ref[:, two : 2 * two] = (dk_acc[...] * scale).astype(BF16)
        dproj_ref[:, 2 * two :] = dv_acc[...].astype(BF16)
        dproj = dproj_ref[...]
        sum_ref[0:1, :] = jnp.sum(dproj.astype(F32), axis=0, keepdims=True)
        out_ref[:, : 3 * two] = dot_nn(turned_ref[...], dproj).astype(BF16)
        grads = dot_nn(mixed_ref[...].T, gall_ref[...]).T.astype(BF16)
        n = grads.shape[0] // BLOCKS
        for at_block in range(BLOCKS):
            at = pl.multiple_of(slot_of(rows, at_block) * n, n)
            out_ref[pl.ds(at, n), 3 * two :] = grads[at_block * n : (at_block + 1) * n, :]
        if pair != 1:
            store_parts(out_ref[...], grads_refs)
        else:
            for kind in range(4):
                for side, ref in enumerate(grads_refs):
                    ref[:, kind * d : (kind + 1) * d] = out_ref[
                        :, kind * two + side * d : kind * two + (side + 1) * d
                    ]


def attend_backward(q, k, v, w, ga, gb, turned, mixed, lse, rows, pair):
    seq, two = q.shape
    width = ga.shape[1]
    block = 256
    grads = (width, 2 * two) if pair == 1 else (width // 2, 4 * two)
    outs = [jax.ShapeDtypeStruct(grads, BF16)] * 2 + [
        jax.ShapeDtypeStruct((seq, 3 * two), BF16),
        jax.ShapeDtypeStruct((8, 3 * two), F32),
    ]
    ins = [q, k, v, w, ga, gb, turned, mixed]
    *grads, dproj, sums = call(
        partial(attend_backward_kernel, rows, pair),
        grid=(seq // block,),
        in_specs=[whole(a.shape) for a in ins] + [pl.BlockSpec((8, block), lambda i: (0, i))],
        out_specs=[whole(o.shape) for o in outs],
        out_shape=outs,
        scratch_shapes=[
            pltpu.VMEM((two, seq), BF16),
            pltpu.VMEM((seq, two), F32),
            pltpu.VMEM((seq, two), F32),
            pltpu.VMEM((seq, two), BF16),
            pltpu.VMEM((seq, width), BF16),
            pltpu.VMEM((width, 4 * two), BF16),
        ],
        cost_estimate=cost(
            flops=50 * seq * seq * two, bytes_accessed=16 * seq * width, transcendentals=seq * seq
        ),
        name=f"attend_backward_{pair}",
    )(*ins, lse)
    return grads, dproj, sums


def project_kernel(first, cols, *refs):
    count = (len(refs) - 1) // 2
    total = 0.0
    for part, weight in zip(refs[:count], refs[count:-1]):
        total = total + dot_nt(part[...], weight[...])
    refs[-1][...] = total.astype(refs[-1].dtype)


def project(parts, weights, half, first, dtype):
    seq, cols = parts[0].shape
    width = weights[0].shape[0]
    tokens = seq // 2
    return call(
        partial(project_kernel, first, cols),
        grid=(1,),
        in_specs=[pl.BlockSpec((tokens, cols), lambda i: (half, 0)) for _ in parts]
        + [pl.BlockSpec((width, cols), lambda i: (0, first // cols)) for _ in weights],
        out_specs=whole((tokens, width)),
        out_shape=jax.ShapeDtypeStruct((tokens, width), dtype),
        cost_estimate=cost(
            flops=2 * tokens * width * cols * 3, bytes_accessed=0, transcendentals=0
        ),
        name="project",
    )(*parts, *weights)


def statistics(rows):
    mean = jnp.mean(rows, axis=1, keepdims=True)
    centered = rows - mean
    inverse = lax.rsqrt(jnp.mean(jnp.square(centered), axis=1, keepdims=True) + EPSILON)
    return centered * inverse, inverse


def add_rows(sum_ref, values):
    @pl.when(pl.program_id(0) == 0)
    def _():
        sum_ref[...] = jnp.zeros_like(sum_ref)

    for i, value in enumerate(values):
        sum_ref[i : i + 1, :] += jnp.sum(value, axis=0, keepdims=True)


ATTN_GAIN, ATTN_SHIFT, MLP_GAIN, MLP_SHIFT, OUTPUT_BIAS, DOWN_BIAS = range(6)


def vector(ref, at):
    return ref[at : at + 1, :]


def norm_kernel(x_ref, vec_ref, out_ref):
    hat, _ = statistics(x_ref[...].astype(F32))
    out_ref[...] = (hat * vector(vec_ref, ATTN_GAIN) + vector(vec_ref, ATTN_SHIFT)).astype(BF16)


def resid_kernel(x_ref, own_ref, got_ref, vec_ref, resid_ref, out_ref, sum_ref):
    branch = own_ref[...] + got_ref[...].astype(F32) + vector(vec_ref, OUTPUT_BIAS)
    resid = x_ref[...].astype(F32) + branch
    resid_ref[...] = resid
    hat, _ = statistics(resid)
    out_ref[...] = (hat * vector(vec_ref, MLP_GAIN) + vector(vec_ref, MLP_SHIFT)).astype(BF16)
    add_rows(sum_ref, [branch * branch])


def result_kernel(resid_ref, own_ref, got_ref, vec_ref, out_ref, sum_ref):
    branch = own_ref[...] + got_ref[...].astype(F32) + vector(vec_ref, DOWN_BIAS)
    result = resid_ref[...] + branch
    out_ref[...] = result.astype(BF16)
    add_rows(sum_ref, [result * result, branch * branch])


def norm_gradient(grad, rows, gain):
    hat, inverse = statistics(rows)
    grad_hat = grad * gain
    first = jnp.mean(grad_hat, axis=1, keepdims=True)
    second = jnp.mean(grad_hat * hat, axis=1, keepdims=True)
    return inverse * (grad_hat - first - hat * second), grad * hat


def middle_kernel(resid_ref, own_ref, got_ref, cot_ref, vec_ref, grad_ref, low_ref, sum_ref):
    grad = own_ref[...] + got_ref[...].astype(F32)
    back, gains = norm_gradient(grad, resid_ref[...], vector(vec_ref, MLP_GAIN))
    cot = cot_ref[...].astype(F32)
    hidden = cot + back
    grad_ref[...] = hidden
    low = hidden.astype(BF16)
    low_ref[...] = low
    add_rows(sum_ref, [gains, grad, low.astype(F32), cot])


def last_kernel(x_ref, own_ref, got_ref, hidden_ref, vec_ref, grad_ref, sum_ref):
    grad = own_ref[...] + got_ref[...].astype(F32)
    back, gains = norm_gradient(grad, x_ref[...].astype(F32), vector(vec_ref, ATTN_GAIN))
    grad_ref[...] = hidden_ref[...] + back
    add_rows(sum_ref, [gains, grad])


def attention_sum_kernel(own_ref, *refs):
    *got_refs, qkv_ref, out_ref = refs
    d = HEAD_DIM
    total = own_ref[...]
    for ref in got_refs:
        total = total + ref[...].astype(F32)
    for kind in range(4):
        large = total[:, 2 * d * kind : 2 * d * (kind + 1)]
        small = total[:, d * (8 + kind) : d * (9 + kind)]
        if kind < 3:
            qkv_ref[:, kind, : 2 * d] = large
            qkv_ref[:, kind, 2 * d :] = small
        else:
            out_ref[:, : 2 * d] = large
            out_ref[:, 2 * d :] = small


def attention_sum(own, got):
    n = own.shape[0]
    side = 3 * HEAD_DIM
    return call(
        attention_sum_kernel,
        out_shape=[
            jax.ShapeDtypeStruct((n, 3, side), F32),
            jax.ShapeDtypeStruct((n, side), F32),
        ],
        cost_estimate=cost(flops=0, bytes_accessed=0, transcendentals=0),
        name="attention_sum",
    )(own, *got)


def small_sums_kernel(entries, own_ref, got_ref, *outs):
    total = own_ref[...] + got_ref[...]
    *vector_refs, qkv_ref, rms_ref = outs
    for ref, row in zip(vector_refs, (7, 8, 2, 0, 1, 10, 3)):
        ref[...] = total[row]
    side = qkv_ref.shape[1]
    qkv_ref[0:1, :] = total[9:10, :side]
    qkv_ref[1:2, :] = total[9:10, side : 2 * side]
    means = jnp.sum(total[4:7, :], axis=1, keepdims=True) / entries
    means = jnp.broadcast_to(jnp.sqrt(means), (3, rms_ref.shape[1]))
    rms_ref[0:1, :] = means[1:2]
    rms_ref[1:2, :] = means[0:1]
    rms_ref[2:3, :] = means[2:3]


def small_sums(own, got, side, entries):
    width = own.shape[1]
    return call(
        partial(small_sums_kernel, entries),
        out_shape=[jax.ShapeDtypeStruct((width,), F32)] * 7
        + [jax.ShapeDtypeStruct((2, side), F32), jax.ShapeDtypeStruct((3, 128), F32)],
        cost_estimate=cost(flops=0, bytes_accessed=0, transcendentals=0),
        name="small_sums",
    )(own, got)


def by_rows(kernel, name, rows, vectors, outs, sums=False):
    tokens, width = rows[0].shape
    block = tokens // 2
    part = pl.BlockSpec((block, width), lambda i: (i, 0))
    out_shape = [jax.ShapeDtypeStruct((tokens, width), t) for t in outs]
    out_specs = [part] * len(outs)
    if sums:
        out_shape.append(jax.ShapeDtypeStruct((8, width), F32))
        out_specs.append(whole((8, width)))
    return call(
        kernel,
        grid=(tokens // block,),
        in_specs=[part] * len(rows) + [whole(vectors.shape)],
        out_specs=out_specs,
        out_shape=out_shape,
        cost_estimate=cost(flops=0, bytes_accessed=0, transcendentals=0),
        name=name,
    )(*rows, vectors)


def gelu_parts(u):
    c0 = math.sqrt(2.0 / math.pi)
    square = u * u
    t = jnp.tanh(u * (c0 + (c0 * 0.044715) * square))
    half = 0.5 * u
    act = half + half * t
    slope = 0.5 + 0.5 * t + half * (1.0 - t * t) * (c0 + (3.0 * c0 * 0.044715) * square)
    return act, slope


def up_kernel(rows, side, *refs):
    xa_ref, xb_ref, turned_ref, *raw, bias_ref, act_ref, slope_ref = refs[: -1 - len(GRAD_PARTS[side])]
    outs, w_ref = refs[-1 - len(GRAD_PARTS[side]) : -1], refs[-1]
    tokens = xa_ref.shape[0]
    put_together(rows, raw, w_ref)
    for half, ref in enumerate((xa_ref, xb_ref)):
        act, slope = gelu_parts(dot_nn(ref[...], w_ref[...]) + vector(bias_ref, UP_BIAS))
        act_ref[half * tokens : (half + 1) * tokens, :] = act.astype(BF16)
        slope_ref[half * tokens : (half + 1) * tokens, :] = slope.astype(BF16)
    store_parts(dot_nn(turned_ref[...], act_ref[...]), outs)


TILE = 256


def tiles(*dims):
    return pl.BlockSpec((*dims, TILE), lambda j: (0,) * len(dims) + (j,))


def raw_tiles(raw):
    return [tiles(*r.shape[:2]) for r in raw]


def up_and_down_grads(xa, xb, turned, raw, bias, rows, side):
    tokens, width = xa.shape
    c = bias.shape[1]
    hidden = jax.ShapeDtypeStruct((2 * tokens, c), BF16)
    grads = [jax.ShapeDtypeStruct((width // f, c), BF16) for f in GRAD_PARTS[side]]
    raw = side_pieces(raw, [side])
    act, slope, *grads = call(
        partial(up_kernel, rows, side),
        grid=(c // TILE,),
        in_specs=[whole(xa.shape), whole(xb.shape), whole(turned.shape)]
        + raw_tiles(raw)
        + [tiles(8)],
        out_specs=[tiles(2 * tokens)] * 2 + [tiles(g.shape[0]) for g in grads],
        out_shape=[hidden] * 2 + grads,
        scratch_shapes=[pltpu.VMEM((width, TILE), BF16)],
        cost_estimate=cost(
            flops=8 * tokens * width * c, bytes_accessed=0, transcendentals=2 * tokens * c
        ),
        name=f"up_and_down_grads_{side}",
    )(xa, xb, turned, *raw, bias)
    return act, slope, grads


def hidden_back_kernel(rows, side, *refs):
    ga_ref, gb_ref, *raw = refs[: 6 + 2 * side]
    down, up = raw[: len(raw) // 2], raw[len(raw) // 2 :]
    slope_ref, *before, pre_ref, sum_ref = refs[6 + 2 * side : 9 + 3 * side]
    *outs, acc_ref, w_ref, u_ref = refs[9 + 3 * side :]
    step = pl.program_id(0)
    tokens = ga_ref.shape[0]

    @pl.when(step == 0)
    def _():
        acc_ref[...] = before[0][...] if side else jnp.zeros_like(acc_ref)

    put_together(rows, down, w_ref)
    put_together(rows, up, u_ref)
    totals = 0.0
    for half, ref in enumerate((ga_ref, gb_ref)):
        at = slice(half * tokens, (half + 1) * tokens)
        back = dot_nn(ref[...], w_ref[...]) * slope_ref[at, :].astype(F32)
        pre = back.astype(BF16)
        pre_ref[at, :] = pre
        totals = totals + jnp.sum(pre.astype(F32), axis=0, keepdims=True)
        acc_ref[at, :] += dot_nt(pre, u_ref[...])
    sum_ref[0:1, :] = totals

    @pl.when(step == pl.num_programs(0) - 1)
    def _():
        if side:
            outs[0][...] = acc_ref[:tokens, :]
            outs[1][...] = acc_ref[tokens:, :].astype(BF16)
        else:
            outs[0][...] = acc_ref[...]


def hidden_back(ga, gb, down, up, slope, before, rows, side):
    tokens, width = ga.shape
    seq, c = slope.shape
    if side:
        backs = [jax.ShapeDtypeStruct(ga.shape, t) for t in (F32, BF16)]
    else:
        backs = [jax.ShapeDtypeStruct((seq, width), F32)]
    return call(
        partial(hidden_back_kernel, rows, side),
        grid=(c // TILE,),
        in_specs=[whole(ga.shape), whole(gb.shape)]
        + raw_tiles(down)
        + raw_tiles(up)
        + [tiles(seq)]
        + [whole(b.shape) for b in before],
        out_specs=[tiles(seq), tiles(8)] + [whole(b.shape) for b in backs],
        out_shape=[jax.ShapeDtypeStruct((seq, c), BF16), jax.ShapeDtypeStruct((8, c), F32)] + backs,
        scratch_shapes=[
            pltpu.VMEM((seq, width), F32),
            pltpu.VMEM((width, TILE), BF16),
            pltpu.VMEM((width, TILE), BF16),
        ],
        cost_estimate=cost(
            flops=8 * tokens * width * c, bytes_accessed=12 * tokens * c, transcendentals=0
        ),
        name=f"hidden_back_{side}",
    )(ga, gb, *down, *up, slope, *before)


def mlp_out_kernel(rows, *refs):
    act_ref, act_o_ref = refs[:2]
    down = refs[2:7]
    own_ref, other_ref, acc_ref, w_ref = refs[7:]
    step = pl.program_id(0)
    tokens = own_ref.shape[0]

    @pl.when(step == 0)
    def _():
        acc_ref[...] = jnp.zeros_like(acc_ref)

    put_together(rows, down[:2], w_ref.at[0])
    put_together(rows, down[2:], w_ref.at[1])
    acc_ref[...] += dot_nt(act_ref[...], w_ref[0]) + dot_nt(act_o_ref[...], w_ref[1])

    @pl.when(step == pl.num_programs(0) - 1)
    def _():
        own_ref[...] = acc_ref[:tokens, :]
        other_ref[...] = acc_ref[tokens:, :].astype(BF16)


def mlp_out(act, act_o, down, width, rows):
    seq, c = act.shape
    outs = [jax.ShapeDtypeStruct((seq // 2, width), t) for t in (F32, BF16)]
    return call(
        partial(mlp_out_kernel, rows),
        grid=(c // TILE,),
        in_specs=[tiles(seq)] * 2 + raw_tiles(down),
        out_specs=[whole(o.shape) for o in outs],
        out_shape=outs,
        scratch_shapes=[pltpu.VMEM((seq, width), F32), pltpu.VMEM((2, width, TILE), BF16)],
        cost_estimate=cost(
            flops=4 * seq * width * c, bytes_accessed=4 * seq * c, transcendentals=0
        ),
        name="mlp_out",
    )(act, act_o, *down)


def weight_grads_kernel(turned_ref, g_ref, go_ref, *outs):
    store_parts(dot_nn(turned_ref[...], g_ref[...]), outs[:2])
    store_parts(dot_nn(turned_ref[...], go_ref[...]), outs[2:])


def weight_grads(turned, grad, grad_o):
    width, seq = turned.shape
    c = grad.shape[1]
    return call(
        weight_grads_kernel,
        grid=(c // TILE,),
        in_specs=[whole(turned.shape), tiles(seq), tiles(seq)],
        out_specs=[tiles(s.shape[0]) for s in grad_shapes(width, c)],
        out_shape=grad_shapes(width, c),
        cost_estimate=cost(
            flops=4 * seq * width * c, bytes_accessed=6 * seq * c, transcendentals=0
        ),
        name="weight_grads",
    )(turned, grad, grad_o)


def make_local(rows):
    low, near = rows[-1], rows[:-1]
    fast = 2 ** len(rows) == BLOCKS
    order = rows if fast else None

    def to_blocks(parts):
        width, c = parts[0].shape[0] * 2, parts[0].shape[1]
        return [p.reshape(-1, width // BLOCKS, c) for p in parts]

    def reduce_plain(parts):
        blocks = to_blocks(parts)
        own = jnp.stack(blocks[:2], axis=1)
        other = jnp.stack([blocks[2], jnp.concatenate(blocks[3:])], axis=1)
        width, c = parts[0].shape[0] * 2, parts[0].shape[1]
        return scatter_rows(own.reshape(width, c), other.reshape(width, c), rows)

    def natural(grads):
        width, c = grads.shape
        blocks = grads.reshape(2, BLOCKS // 2, width // BLOCKS, c)
        return jnp.swapaxes(blocks, 0, 1).reshape(width, c)

    def local(
        layer_input,
        attn_gain,
        attn_shift,
        qkv_weight,
        qkv_bias,
        output_weight,
        output_bias,
        mlp_gain,
        mlp_shift,
        up_weight,
        up_bias,
        down_weight,
        down_bias,
        cotangent,
    ):
        tokens, width = layer_input.shape
        n, _, side = qkv_weight.shape
        hidden = up_weight.shape[1]
        d = HEAD_DIM

        attn_shard = jnp.concatenate([qkv_weight.reshape(n, -1), output_weight], axis=1)
        vectors = table_of(attn_gain, attn_shift, mlp_gain, mlp_shift, output_bias, down_bias)
        (attn_in,) = by_rows(norm_kernel, "norm", [layer_input], vectors, [BF16])
        attn_in_other = swap(attn_in, "core")
        cot_other = swap(cotangent, "core")
        bias_own = jnp.pad(qkv_bias, ((0, 6), (0, hidden - side)))
        bias_own = bias_own + jnp.pad(up_bias[None, :], ((UP_BIAS, 7 - UP_BIAS), (0, 0)))
        bias_other = swap(bias_own, "y")
        if fast:
            attn_near = gather_near(attn_shard, near)
            attn_near = after(attn_near, cot_other, bias_other)
            attn_stack = jnp.stack(attn_near)
            mlp_near = gather_near(jnp.stack([up_weight, down_weight]), near)
            attn_far = gather_far(attn_stack, low)
            attn_raw = gather_corners(attn_far, low)
        else:
            attn_raw, up_raw, down_raw = (
                gather_plain(w, rows) for w in (attn_shard, up_weight, down_weight)
            )
        halves = (attn_in, attn_in_other, cotangent, cot_other)
        if fast:
            halves = after(halves, attn_stack)
        attn_turned = turn(*halves[:2], order)
        cot_turned = turn(*halves[2:], order)
        attended = []
        for pair in range(3):
            bias = bias_own
            if fast and pair == 0:
                bias = after(bias, attn_far, attn_turned, cot_turned)
            if pair:
                bias = after(bias, attended[pair - 1][4])
            if fast and pair == 1:
                mlp_near = after(mlp_near, attended[0][4], attn_raw)
                up_far = gather_far(jnp.stack([m[0] for m in mlp_near]), low)
                down_stack = jnp.stack([m[1] for m in mlp_near])
                bias = after(bias, up_far[0], down_stack)
            attended.append(
                attend_forward(attn_in, attn_in_other, attn_raw, bias, bias_other, order, pair)
            )
        mixed = [a[4] for a in attended]
        weights = [a[3] for a in attended]
        if fast:
            mixed, up_far = after((mixed, up_far))
            up_raw = gather_corners(up_far, low)
        got = swap(project(mixed, weights, 1, 6 * d, BF16), "core")
        own = project(mixed, weights, 0, 6 * d, F32)
        hidden_resid, mlp_in, branch_sums = by_rows(
            resid_kernel,
            "resid",
            [layer_input, own, got],
            vectors,
            [F32, BF16],
            True,
        )
        mlp_in_other = swap(mlp_in, "core")
        if fast:
            down_far = gather_far(after(down_stack, mlp_in_other), low)
        ins = (mlp_in, mlp_in_other, cot_turned)
        grads = (cotangent, cot_other)
        act, slope, down_own = up_and_down_grads(*ins, up_raw, bias_own, order, 0)
        if fast:
            down_raw = gather_corners(after(down_far, act), low)
        pre, up_sums, back = hidden_back(*grads, down_raw[:2], up_raw[:2], slope, (), order, 0)
        bias_other = after(bias_other, pre)
        act_o, slope_o, down_other = up_and_down_grads(*ins, up_raw, bias_other, order, 1)
        down_parts = down_own + down_other
        if fast:
            down_parts = to_blocks(down_parts)
            down_got = reduce_corners(down_parts, low)
        else:
            down_grad = reduce_plain(down_parts)
        pre_o, up_sums_o, back, back_other = hidden_back(
            *grads, down_raw[2:], up_raw[2:], slope_o, (back,), order, 1
        )
        back_got = swap(back_other, "core")
        mlp_turned = turn(*after((mlp_in, mlp_in_other), pre_o), order)
        up_parts = weight_grads(mlp_turned, pre, pre_o)
        if fast:
            up_parts = to_blocks(up_parts)
            up_got = reduce_corners(up_parts, low)
        else:
            up_grad = reduce_plain(up_parts)
        hidden_grad, grad_attn, middle_sums = by_rows(
            middle_kernel,
            "middle",
            [hidden_resid, after(back, up_parts), back_got, cotangent],
            vectors,
            [F32, BF16],
            True,
        )
        grad_attn_other = swap(grad_attn, "core")
        if fast:
            down_sent = reduce_far(down_parts, after(down_got, grad_attn), low)

        half, block = width // 2, width // BLOCKS
        pair_grads, pair_sums, dprojs = {}, {}, {}
        for pair in (2, 1, 0):
            q, k, v, w, mix, lse = attended[pair]
            if pair != 2:
                lse = after(lse, pair_grads[pair + 1])
            if fast and pair == 1:
                lse, down_sent = after((lse, down_sent))
                total = down_parts[0].astype(F32) + sum(g.astype(F32) for g in down_sent)
                down_sum, down_got = total[:2], swap(total[2:].astype(BF16), near[0])
            if fast and pair == 0:
                to_low, to_y = far_sums(up_parts, after(up_got, pair_grads[1]))
                up_sent = (swap(to_low, low), swap(to_y, "y"))
                lse, large_got = after((lse, large_got), to_low, to_y)
                large_y = (pair_grads[2][0].astype(F32) + large_got.astype(F32)).astype(BF16)
                large_y = swap(large_y, "y")
            pair_grads[pair], dprojs[pair], pair_sums[pair] = attend_backward(
                q, k, v, w, grad_attn, grad_attn_other, attn_turned, mix, lse, order, pair
            )
            if fast and pair == 2:
                large_got = swap(pair_grads[2][1], low)

        dprojs = [dprojs[pair] for pair in range(3)]
        if fast:
            large_x = swap(pair_grads[0][1], low)
            small_got = swap(pair_grads[1][1], "y")
            up_sent, dprojs, down_got = after((up_sent, dprojs, down_got), pair_grads[0])
            down_sum = down_sum + down_got.astype(F32)
            total = up_parts[0].astype(F32) + sum(g.astype(F32) for g in up_sent)
            up_sum, up_got = total[:2], swap(total[2:].astype(BF16), near[0])
        act, act_o = after((act, act_o), pair_grads[0])
        branch, branch_other = mlp_out(act, act_o, down_raw, width, order)
        branch_got = swap(branch_other, "core")
        back_other = project(after(dprojs, branch), weights, 1, 0, BF16)
        got = swap(back_other, "core")
        dprojs = after(dprojs, back_other)
        if fast:
            dprojs, large_x = after((dprojs, large_x))
        own = project(dprojs, weights, 0, 0, F32)
        layer_output, result_sums = by_rows(
            result_kernel,
            "result",
            [hidden_resid, after(branch, own), branch_got],
            vectors,
            [BF16],
            True,
        )
        if fast:
            small = pair_grads[1][0].astype(F32) + after(small_got, own).astype(F32)
            small_x = swap(small[half:].astype(BF16), low)
            large_sent, small_sent = (large_x, large_y), small_x
            own, large_sent, small_sent, got = after(
                (own, large_sent, small_sent, got), layer_output
            )
        input_grad, last_sums = by_rows(
            last_kernel, "last", [layer_input, own, got, hidden_grad], vectors, [F32], True
        )
        if fast:
            up_got, last_sums = after((up_got, last_sums))
            down_sum = after(down_sum, last_sums)
            down_got = swap(down_sum[1].astype(BF16), near[1])
        if not fast:
            own, other = (
                natural(jnp.concatenate(p, axis=1))
                for p in (
                    (jnp.concatenate(pair_grads[0]), pair_grads[1][0]),
                    (jnp.concatenate(pair_grads[2]), pair_grads[1][1]),
                )
            )
            attn_grad = scatter_rows(own, other, rows)

        def bias_row(large, small, at):
            row = 0.0
            for i, kind in enumerate((0, 2)):
                source = 2 * d * kind
                for piece, to in (
                    (large[:1, source : source + 2 * d], 0),
                    (small[:1, source + at : source + at + d], 2 * d),
                ):
                    to = i * side + to
                    row = row + jnp.pad(piece, ((0, 0), (to, width - to - piece.shape[1])))
            return row
        common = jnp.concatenate(
            [middle_sums[:4], branch_sums[:1], result_sums[:2], last_sums[:2]], axis=0
        )
        common = common + swap(common, "core")
        own = jnp.concatenate([common, bias_row(pair_sums[0], pair_sums[1], 0), up_sums[:1]], axis=0)
        other = jnp.concatenate([common, bias_row(pair_sums[2], pair_sums[1], d), up_sums_o[:1]], axis=0)
        sums = own + swap(other, "y")
        if fast:
            large = pair_grads[0][0].astype(F32) + sum(g.astype(F32) for g in large_sent)
            small = small[:half] + small_sent.astype(F32)
            both = jnp.concatenate([large, small], axis=1).reshape(-1, block, 12 * d)
            attn_near = send_near(both, near)
            total = up_sum + up_got.astype(F32)
            up_grad = total[0] + swap(total[1].astype(BF16), near[1]).astype(F32)
            down_grad = down_sum[0] + down_got.astype(F32)
        for axis in reversed(rows[1:]):
            sums = sums + swap(sums, axis)
        entries = float(tokens * 2 ** (len(rows) + 2) * width)
        *vecs, qkv_bias_grad, rms_values = small_sums(sums, swap(sums, rows[0]), side, entries)
        if fast:
            qkv_grad, output_grad = attention_sum(attn_near[0], attn_near[1].values())
        else:
            qkv_grad, output_grad = attention_sum(attn_grad, ())
        return (
            layer_output,
            input_grad,
            vecs[0],
            vecs[1],
            qkv_grad,
            qkv_bias_grad,
            output_grad,
            vecs[2],
            vecs[3],
            vecs[4],
            up_grad,
            vecs[5],
            down_grad,
            vecs[6],
            rms_values[:, 0],
        )

    return local


def solution(mesh):
    row_size, col_size = mesh.shape["row"], mesh.shape["col"]
    bits = row_size.bit_length() - 1
    rows = tuple(f"r{b}" for b in reversed(range(bits)))
    cube = Mesh(mesh.devices.reshape((2,) * bits + (col_size // 2, 2)), rows + ("y", "core"))
    col = ("y", "core")
    every = rows + col
    placed = (
        P(every, None),
        P(),
        P(),
        P(rows, None, col),
        P(None, col),
        P(rows, col),
        P(),
        P(),
        P(),
        P(rows, col),
        P(col),
        P(rows, col),
        P(),
        P(every, None),
    )
    return jax.shard_map(
        make_local(rows),
        mesh=cube,
        in_specs=placed,
        out_specs=(
            P(every, None),
            P(every, None),
            P(),
            P(),
            P(rows, None, col),
            P(None, col),
            P(rows, col),
            P(),
            P(),
            P(),
            P(rows, col),
            P(col),
            P(rows, col),
            P(),
            P(),
        ),
        check_vma=False,
    )
```

```python
import math
from functools import partial

import jax
import jax.numpy as jnp
from jax import lax
from jax.experimental import pallas as pl
from jax.experimental.pallas import tpu as pltpu
from jax.sharding import Mesh, PartitionSpec as P

HEAD_DIM = 64
EPSILON = 1e-06
SWAP = [(0, 1), (1, 0)]
LOG2E = math.log2(math.e)
BF16 = jnp.bfloat16
F32 = jnp.float32
VMEM_BYTES = 16 * 2**20


def call(kernel, **kwargs):
    params = pltpu.CompilerParams(vmem_limit_bytes=VMEM_BYTES)
    return pl.pallas_call(kernel, compiler_params=params, **kwargs)


def cost(flops, bytes_accessed, transcendentals):
    return pl.CostEstimate(flops=0, bytes_accessed=0, transcendentals=0)


def after(arrays, *others):
    return lax.optimization_barrier((arrays, others))[0]


def table_of(*vectors):
    row = lax.broadcasted_iota(jnp.int32, (8, vectors[0].shape[0]), 0)
    out = jnp.zeros(row.shape, F32)
    for i, v in enumerate(vectors):
        out = jnp.where(row == i, v[None, :], out)
    return out


def swap(array, axis):
    return lax.ppermute(array, axis, SWAP)


def dot_nn(left, right):
    return lax.dot_general(left, right, (((1,), (0,)), ((), ())), preferred_element_type=F32)


def dot_nt(left, right):
    return lax.dot_general(left, right, (((1,), (1,)), ((), ())), preferred_element_type=F32)


def dot_tn(left, right):
    return lax.dot_general(left, right, (((0,), (0,)), ((), ())), preferred_element_type=F32)


def xor_exchange(blocks_of, axes):
    got = {}
    count = len(axes)
    sizes = [2] * count
    for bits in range(1, 2**count):
        perm = [(i, i ^ bits) for i in range(math.prod(sizes))]
        got[bits] = lax.ppermute(blocks_of(bits), axes, perm)
    return got


def in_order(own, got, axes):
    parts = [own] + [got[bits] for bits in range(1, 2 ** len(axes))]
    for depth, axis in enumerate(reversed(axes)):
        bit = 2**depth
        flip = lax.axis_index(axis) == 1
        parts = [jnp.where(flip, parts[i ^ bit], parts[i]) for i in range(len(parts))]
    return jnp.stack(parts)


def pair_in_order(own, other, axis, dim):
    flip = lax.axis_index(axis) == 1
    return jnp.stack([jnp.where(flip, other, own), jnp.where(flip, own, other)], axis=dim)


def gather_rows(shard, rows):
    low, high = rows[-1], rows[:-1]
    n, c = shard.shape
    near = high[-2:]
    stack = in_order(shard, xor_exchange(lambda bits: shard, near), near)
    for axis in reversed(high[:-2]):
        other = swap(stack, axis)
        stack = pair_in_order(stack, other, axis, 0).reshape(-1, n, c)
    half = c // 2
    first, second = stack[:, :, :half], stack[:, :, half:]
    first_low, second_y = swap(first, low), swap(second, "y")
    first = pair_in_order(first, first_low, low, 1).reshape(-1, half)
    first_y = swap(first, "y")
    second_low = swap(jnp.stack([second, second_y]), low)
    second_own = pair_in_order(second, second_low[0], low, 1).reshape(-1, half)
    second_other = pair_in_order(second_y, second_low[1], low, 1).reshape(-1, half)
    return (
        jnp.concatenate([first, second_own], axis=1),
        jnp.concatenate([first_y, second_other], axis=1),
    )


def pick(array, axis, dim, other):
    zero = lax.index_in_dim(array, 0, dim, keepdims=False)
    one = lax.index_in_dim(array, 1, dim, keepdims=False)
    flip = lax.axis_index(axis) == (0 if other else 1)
    return jnp.where(flip, one, zero)


def scatter_rows(own, other, rows):
    low, high = rows[-1], rows[:-1]
    near = high[-2:]
    total = 2 ** len(rows)
    n, c = own.shape[0] // total, own.shape[1]
    half = c // 2
    own = own.reshape(total // 2, 2, n, c)
    other = other.reshape(total // 2, 2, n, c)
    a_own, a_other = own[..., :half], other[..., :half]
    b_own, b_other = own[..., half:], other[..., half:]
    a_got = swap(a_other, "y")
    b_send = jnp.stack([pick(b_own, low, 1, True), pick(b_other, low, 1, True)])
    b_got = swap(b_send, low)
    a_sum = a_own.astype(F32) + a_got.astype(F32)
    a_send = pick(a_sum, low, 1, True).astype(BF16)
    b_own = pick(b_own, low, 1, False).astype(F32) + b_got[0].astype(F32)
    b_other = (pick(b_other, low, 1, False).astype(F32) + b_got[1].astype(F32)).astype(BF16)
    a_got = swap(a_send, low)
    b_got = swap(b_other, "y")
    a_sum = pick(a_sum, low, 1, False) + a_got.astype(F32)
    b_sum = b_own + b_got.astype(F32)
    both = jnp.concatenate([a_sum, b_sum], axis=2)
    for axis in high[:-2]:
        both = both.reshape(2, -1, n, c)
        got = swap(pick(both, axis, 0, True).astype(BF16), axis)
        both = pick(both, axis, 0, False) + got.astype(F32)
    low_both = both.astype(BF16)
    place = lax.axis_index(near)
    take = lambda bits: lax.dynamic_index_in_dim(low_both, place ^ bits, 0, keepdims=False)
    got = xor_exchange(take, near)
    out = lax.dynamic_index_in_dim(both, place, 0, keepdims=False)
    for piece in got.values():
        out = out + piece.astype(F32)
    return out


BLOCKS = 8


def gather_near(shard, near):
    got = xor_exchange(lambda bits: shard, near)
    return [shard] + [got[bits] for bits in range(1, 2 ** len(near))]


def gather_far(stack, low):
    return stack, swap(stack, low), swap(stack, "y")


def gather_corners(far, low):
    stack, from_low, from_y = far
    half = stack.shape[0] // 2
    return (*far, swap(from_low[:half], "y"), swap(from_y[half:], low))


def gather_plain(shard, rows):
    pieces = []
    for side in gather_rows(shard, rows):
        width, c = side.shape
        blocks = side.reshape(BLOCKS // 2, 2, width // BLOCKS, c)
        pieces += [blocks[:, 0], blocks[:, 1]]
    half = BLOCKS // 4
    return (*pieces[:3], pieces[3][:half], pieces[3][half:])


def reduce_corners(parts, low):
    return swap(parts[3], "y"), swap(parts[4], low)


def far_sums(parts, got):
    _, to_low, to_y, _, _ = parts
    half = to_low.shape[0] // 2
    add = lambda a, b: (a.astype(F32) + b.astype(F32)).astype(BF16)
    to_low = jnp.concatenate([add(to_low[:half], got[0]), to_low[half:]])
    to_y = jnp.concatenate([to_y[:half], add(to_y[half:], got[1])])
    return to_low, to_y


def reduce_far(parts, got, low):
    to_low, to_y = far_sums(parts, got)
    return swap(to_low, low), swap(to_y, "y")


def send_near(stack, near):
    low = stack.astype(BF16)
    return stack[0], xor_exchange(lambda bits: low[bits], near)


def sum_near(own, got):
    for piece in got.values():
        own = own + piece.astype(F32)
    return own


def here(rows):
    if rows is None:
        return 0, 0
    return lax.axis_index(rows[:-1]), lax.axis_index(rows[-1])


def flip(at, by):
    return by if isinstance(at, int) else lax.bitwise_xor(at, by)


def slot_of(rows, block):
    z, x = here(rows)
    block_z, block_x = divmod(block, 2)
    return flip(x, block_x) * (BLOCKS // 2) + flip(z, block_z)


def whole(shape):
    return pl.BlockSpec(shape, lambda *_: (0,) * len(shape))


def side_pieces(raw, sides):
    return [p for side in sides for p in (raw[:2] if side == 0 else raw[2:])]


def put_together(rows, refs, out_ref, source=slice(None), target=slice(None)):
    z, x = here(rows)
    at = 0
    for ref, x_flip in zip(refs, (0, 1, 1)):
        for k in range(ref.shape[0]):
            n = ref.shape[1]
            slot = k + (at if x_flip else 0)
            row = (flip(z, slot) * 2 + flip(x, x_flip)) * n
            out_ref[pl.ds(pl.multiple_of(row, n), n), target] = ref[k, :, source]
        at += ref.shape[0] * x_flip


def turn_kernel(rows, a_ref, b_ref, out_ref):
    tokens, width = a_ref.shape
    n = width // BLOCKS
    for half, ref in enumerate((a_ref, b_ref)):
        turned = ref[...].T
        for block in range(BLOCKS):
            at = pl.multiple_of(slot_of(rows, block) * n, n)
            out_ref[pl.ds(at, n), half * tokens : (half + 1) * tokens] = turned[
                block * n : (block + 1) * n, :
            ]


def turn(a, b, rows):
    tokens, width = a.shape
    return call(
        partial(turn_kernel, rows),
        out_shape=jax.ShapeDtypeStruct((width, 2 * tokens), BF16),
        cost_estimate=cost(
            flops=0, bytes_accessed=8 * tokens * width, transcendentals=0
        ),
        name="turn",
    )(a, b)


GRAD_PARTS = {0: (2, 2), 1: (2, 4, 4)}


def store_parts(grads, refs):
    at = 0
    for ref in refs:
        ref[...] = grads[at : at + ref.shape[0]].astype(BF16)
        at += ref.shape[0]


def grad_shapes(width, c):
    return [jax.ShapeDtypeStruct((width // f, c), BF16) for side in (0, 1) for f in GRAD_PARTS[side]]


def pair_sources(pair):
    return {0: [(0, 0, 2)], 1: [(0, 2, 1), (1, 2, 1)], 2: [(1, 0, 2)]}[pair]


Q_BIAS, V_BIAS, UP_BIAS = range(3)


def attend_forward_kernel(rows, pair, *refs):
    *refs, q_ref, k_ref, v_ref, w_ref, mixed_ref, lse_ref, vt_ref = refs
    xa_ref, xb_ref, *raw, own_ref, other_ref = refs
    raw = {0: [raw], 1: [raw[:2], raw[2:]], 2: [raw]}[pair]
    d = HEAD_DIM
    two = 2 * d
    tokens = xa_ref.shape[0]
    step = pl.program_id(0)
    block = mixed_ref.shape[0]

    @pl.when(step == 0)
    def _():
        for kind in range(4):
            at = kind * two
            for pieces, (_, first, heads) in zip(raw, pair_sources(pair)):
                source = (kind * 3 + first) * d
                put_together(
                    rows,
                    pieces,
                    w_ref,
                    slice(source, source + heads * d),
                    slice(at, at + heads * d),
                )
                at += heads * d
        bias = []
        for row in (Q_BIAS, None, V_BIAS):
            for side, first, heads in pair_sources(pair):
                cols = slice(first * d, (first + heads) * d)
                if row is None:
                    bias.append(jnp.zeros((1, heads * d), F32))
                else:
                    bias.append((own_ref, other_ref)[side][row : row + 1, cols])
        bias = jnp.concatenate(bias, axis=1)
        for half, ref in enumerate((xa_ref, xb_ref)):
            at = slice(half * tokens, (half + 1) * tokens)
            proj = (dot_nn(ref[...], w_ref[:, : 3 * two]) + bias).astype(BF16)
            q_ref[at, :] = proj[:, :two]
            k_ref[at, :] = proj[:, two : 2 * two]
            v_ref[at, :] = proj[:, 2 * two :]
        turned = v_ref[...].T
        for head in range(2):
            vt_ref[head, :d, :] = turned[head * d : (head + 1) * d, :]
            vt_ref[head, d:, :] = jnp.ones((vt_ref.shape[1] - d, turned.shape[1]), BF16)

    query = q_ref[pl.ds(pl.multiple_of(step * block, block), block), :]
    lane = lax.broadcasted_iota(jnp.int32, query.shape, 1)
    outs = []
    for head in range(2):
        masked = jnp.where(lane // d == head, query, jnp.zeros_like(query)) * BF16(d**-0.5)
        scores = dot_nt(k_ref[...], masked)
        top = jnp.max(scores, axis=0, keepdims=True)
        weights = jnp.exp2((scores - top) * LOG2E).astype(BF16)
        out = dot_nn(vt_ref[head], weights)
        total = out[d : d + 1, :]
        outs.append(out[:d, :] * (1.0 / total))
        lse_ref[head : head + 1, :] = top + jnp.log(total)
    mixed_ref[...] = jnp.concatenate(outs, axis=0).T.astype(BF16)


def attend_forward(xa, xb, raw, own, other, rows, pair):
    tokens, width = xa.shape
    seq = 2 * tokens
    two = 2 * HEAD_DIM
    block = 512
    part = jax.ShapeDtypeStruct((seq, two), BF16)
    weight = jax.ShapeDtypeStruct((width, 4 * two), BF16)
    ins = [xa, xb, *side_pieces(raw, [side for side, *_ in pair_sources(pair)]), own, other]
    return call(
        partial(attend_forward_kernel, rows, pair),
        grid=(seq // block,),
        in_specs=[whole(a.shape) for a in ins],
        out_specs=[
            whole(part.shape),
            whole(part.shape),
            whole(part.shape),
            whole(weight.shape),
            pl.BlockSpec((block, two), lambda i: (i, 0)),
            pl.BlockSpec((8, block), lambda i: (0, i)),
        ],
        out_shape=[part, part, part, weight, part, jax.ShapeDtypeStruct((8, seq), F32)],
        scratch_shapes=[pltpu.VMEM((2, HEAD_DIM + 16, seq), BF16)],
        cost_estimate=cost(
            flops=24 * seq * seq * two, bytes_accessed=16 * seq * width, transcendentals=seq * seq
        ),
        name=f"attend_forward_{pair}",
    )(*ins)


def attend_backward_kernel(rows, pair, *refs):
    q_ref, k_ref, v_ref, w_ref, ga_ref, gb_ref, turned_ref, mixed_ref, lse_ref = refs[:9]
    kt_ref, dk_acc, dv_acc, gmix_ref, gall_ref, out_ref = refs[-6:]
    *grads_refs, dproj_ref, sum_ref = refs[9:-6]
    step = pl.program_id(0)
    d = HEAD_DIM
    two = 2 * d
    scale = d**-0.5
    tokens = ga_ref.shape[0]
    block = lse_ref.shape[1]

    @pl.when(step == 0)
    def _():
        kt_ref[...] = k_ref[...].T
        dk_acc[...] = jnp.zeros_like(dk_acc)
        dv_acc[...] = jnp.zeros_like(dv_acc)
        for half, ref in enumerate((ga_ref, gb_ref)):
            at = slice(half * tokens, (half + 1) * tokens)
            gall_ref[at, :] = ref[...]
            gmix_ref[at, :] = dot_nn(ref[...], w_ref[:, 3 * two :]).astype(BF16)

    here_rows = pl.ds(pl.multiple_of(step * block, block), block)
    query = q_ref[here_rows, :]
    grad = gmix_ref[here_rows, :]
    lane = lax.broadcasted_iota(jnp.int32, query.shape, 1)
    dots = (grad.astype(F32) * mixed_ref[here_rows, :].astype(F32)).T
    dqs = []
    for head in range(2):
        mine = lane // d == head
        query_h = jnp.where(mine, query, jnp.zeros_like(query))
        grad_h = jnp.where(mine, grad, jnp.zeros_like(grad))
        row_dots = jnp.sum(dots[head * d : (head + 1) * d, :], axis=0, keepdims=True)
        log_total = lse_ref[head : head + 1, :] * LOG2E
        scores = dot_nt(k_ref[...], query_h * BF16(scale))
        probs = jnp.exp2(scores * LOG2E - log_total)
        grad_probs = dot_nt(v_ref[...], grad_h)
        grad_scores = (probs * (grad_probs - row_dots)).astype(BF16)
        dv_acc[...] += dot_nn(probs.astype(BF16), grad_h)
        dk_acc[...] += dot_nn(grad_scores, query_h)
        dqs.append(dot_nn(kt_ref[head * d : (head + 1) * d, :], grad_scores) * scale)
    dproj_ref[here_rows, :two] = jnp.concatenate(dqs, axis=0).T.astype(BF16)

    @pl.when(step == pl.num_programs(0) - 1)
    def _():
        dproj_ref[:, two : 2 * two] = (dk_acc[...] * scale).astype(BF16)
        dproj_ref[:, 2 * two :] = dv_acc[...].astype(BF16)
        dproj = dproj_ref[...]
        sum_ref[0:1, :] = jnp.sum(dproj.astype(F32), axis=0, keepdims=True)
        out_ref[:, : 3 * two] = dot_nn(turned_ref[...], dproj).astype(BF16)
        grads = dot_nn(mixed_ref[...].T, gall_ref[...]).T.astype(BF16)
        n = grads.shape[0] // BLOCKS
        for at_block in range(BLOCKS):
            at = pl.multiple_of(slot_of(rows, at_block) * n, n)
            out_ref[pl.ds(at, n), 3 * two :] = grads[at_block * n : (at_block + 1) * n, :]
        if pair != 1:
            store_parts(out_ref[...], grads_refs)
        else:
            for kind in range(4):
                for side, ref in enumerate(grads_refs):
                    ref[:, kind * d : (kind + 1) * d] = out_ref[
                        :, kind * two + side * d : kind * two + (side + 1) * d
                    ]


def attend_backward(q, k, v, w, ga, gb, turned, mixed, lse, rows, pair):
    seq, two = q.shape
    width = ga.shape[1]
    block = 512
    grads = (width, 2 * two) if pair == 1 else (width // 2, 4 * two)
    outs = [jax.ShapeDtypeStruct(grads, BF16)] * 2 + [
        jax.ShapeDtypeStruct((seq, 3 * two), BF16),
        jax.ShapeDtypeStruct((8, 3 * two), F32),
    ]
    ins = [q, k, v, w, ga, gb, turned, mixed]
    *grads, dproj, sums = call(
        partial(attend_backward_kernel, rows, pair),
        grid=(seq // block,),
        in_specs=[whole(a.shape) for a in ins] + [pl.BlockSpec((8, block), lambda i: (0, i))],
        out_specs=[whole(o.shape) for o in outs],
        out_shape=outs,
        scratch_shapes=[
            pltpu.VMEM((two, seq), BF16),
            pltpu.VMEM((seq, two), F32),
            pltpu.VMEM((seq, two), F32),
            pltpu.VMEM((seq, two), BF16),
            pltpu.VMEM((seq, width), BF16),
            pltpu.VMEM((width, 4 * two), BF16),
        ],
        cost_estimate=cost(
            flops=50 * seq * seq * two, bytes_accessed=16 * seq * width, transcendentals=seq * seq
        ),
        name=f"attend_backward_{pair}",
    )(*ins, lse)
    return grads, dproj, sums


def project_kernel(first, cols, *refs):
    count = (len(refs) - 1) // 2
    total = 0.0
    for part, weight in zip(refs[:count], refs[count:-1]):
        total = total + dot_nt(part[...], weight[...])
    refs[-1][...] = total.astype(refs[-1].dtype)


def project(parts, weights, half, first, dtype):
    seq, cols = parts[0].shape
    width = weights[0].shape[0]
    tokens = seq // 2
    return call(
        partial(project_kernel, first, cols),
        grid=(1,),
        in_specs=[pl.BlockSpec((tokens, cols), lambda i: (half, 0)) for _ in parts]
        + [pl.BlockSpec((width, cols), lambda i: (0, first // cols)) for _ in weights],
        out_specs=whole((tokens, width)),
        out_shape=jax.ShapeDtypeStruct((tokens, width), dtype),
        cost_estimate=cost(
            flops=2 * tokens * width * cols * 3, bytes_accessed=0, transcendentals=0
        ),
        name="project",
    )(*parts, *weights)


def statistics(rows):
    mean = jnp.mean(rows, axis=1, keepdims=True)
    centered = rows - mean
    inverse = lax.rsqrt(jnp.mean(jnp.square(centered), axis=1, keepdims=True) + EPSILON)
    return centered * inverse, inverse


def add_rows(sum_ref, values):
    @pl.when(pl.program_id(0) == 0)
    def _():
        sum_ref[...] = jnp.zeros_like(sum_ref)

    for i, value in enumerate(values):
        sum_ref[i : i + 1, :] += jnp.sum(value, axis=0, keepdims=True)


ATTN_GAIN, ATTN_SHIFT, MLP_GAIN, MLP_SHIFT, OUTPUT_BIAS, DOWN_BIAS = range(6)


def vector(ref, at):
    return ref[at : at + 1, :]


def norm_kernel(x_ref, vec_ref, out_ref):
    hat, _ = statistics(x_ref[...].astype(F32))
    out_ref[...] = (hat * vector(vec_ref, ATTN_GAIN) + vector(vec_ref, ATTN_SHIFT)).astype(BF16)


def resid_kernel(x_ref, own_ref, got_ref, vec_ref, resid_ref, out_ref, sum_ref):
    branch = own_ref[...] + got_ref[...].astype(F32) + vector(vec_ref, OUTPUT_BIAS)
    resid = x_ref[...].astype(F32) + branch
    resid_ref[...] = resid
    hat, _ = statistics(resid)
    out_ref[...] = (hat * vector(vec_ref, MLP_GAIN) + vector(vec_ref, MLP_SHIFT)).astype(BF16)
    add_rows(sum_ref, [branch * branch])


def result_kernel(resid_ref, own_ref, got_ref, vec_ref, out_ref, sum_ref):
    branch = own_ref[...] + got_ref[...].astype(F32) + vector(vec_ref, DOWN_BIAS)
    result = resid_ref[...] + branch
    out_ref[...] = result.astype(BF16)
    add_rows(sum_ref, [result * result, branch * branch])


def norm_gradient(grad, rows, gain):
    hat, inverse = statistics(rows)
    grad_hat = grad * gain
    first = jnp.mean(grad_hat, axis=1, keepdims=True)
    second = jnp.mean(grad_hat * hat, axis=1, keepdims=True)
    return inverse * (grad_hat - first - hat * second), grad * hat


def middle_kernel(resid_ref, own_ref, got_ref, cot_ref, vec_ref, grad_ref, low_ref, sum_ref):
    grad = own_ref[...] + got_ref[...].astype(F32)
    back, gains = norm_gradient(grad, resid_ref[...], vector(vec_ref, MLP_GAIN))
    cot = cot_ref[...].astype(F32)
    hidden = cot + back
    grad_ref[...] = hidden
    low = hidden.astype(BF16)
    low_ref[...] = low
    add_rows(sum_ref, [gains, grad, low.astype(F32), cot])


def last_kernel(x_ref, own_ref, got_ref, hidden_ref, vec_ref, grad_ref, sum_ref):
    grad = own_ref[...] + got_ref[...].astype(F32)
    back, gains = norm_gradient(grad, x_ref[...].astype(F32), vector(vec_ref, ATTN_GAIN))
    grad_ref[...] = hidden_ref[...] + back
    add_rows(sum_ref, [gains, grad])


def attention_sum_kernel(own_ref, *refs):
    *got_refs, qkv_ref, out_ref = refs
    d = HEAD_DIM
    total = own_ref[...]
    for ref in got_refs:
        total = total + ref[...].astype(F32)
    for kind in range(4):
        large = total[:, 2 * d * kind : 2 * d * (kind + 1)]
        small = total[:, d * (8 + kind) : d * (9 + kind)]
        if kind < 3:
            qkv_ref[:, kind, : 2 * d] = large
            qkv_ref[:, kind, 2 * d :] = small
        else:
            out_ref[:, : 2 * d] = large
            out_ref[:, 2 * d :] = small


def attention_sum(own, got):
    n = own.shape[0]
    side = 3 * HEAD_DIM
    return call(
        attention_sum_kernel,
        out_shape=[
            jax.ShapeDtypeStruct((n, 3, side), F32),
            jax.ShapeDtypeStruct((n, side), F32),
        ],
        cost_estimate=cost(flops=0, bytes_accessed=0, transcendentals=0),
        name="attention_sum",
    )(own, *got)


def small_sums_kernel(entries, own_ref, got_ref, *outs):
    total = own_ref[...] + got_ref[...]
    *vector_refs, qkv_ref, rms_ref = outs
    for ref, row in zip(vector_refs, (7, 8, 2, 0, 1, 10, 3)):
        ref[...] = total[row]
    side = qkv_ref.shape[1]
    qkv_ref[0:1, :] = total[9:10, :side]
    qkv_ref[1:2, :] = total[9:10, side : 2 * side]
    means = jnp.sum(total[4:7, :], axis=1, keepdims=True) / entries
    means = jnp.broadcast_to(jnp.sqrt(means), (3, rms_ref.shape[1]))
    rms_ref[0:1, :] = means[1:2]
    rms_ref[1:2, :] = means[0:1]
    rms_ref[2:3, :] = means[2:3]


def small_sums(own, got, side, entries):
    width = own.shape[1]
    return call(
        partial(small_sums_kernel, entries),
        out_shape=[jax.ShapeDtypeStruct((width,), F32)] * 7
        + [jax.ShapeDtypeStruct((2, side), F32), jax.ShapeDtypeStruct((3, 128), F32)],
        cost_estimate=cost(flops=0, bytes_accessed=0, transcendentals=0),
        name="small_sums",
    )(own, got)


def by_rows(kernel, name, rows, vectors, outs, sums=False):
    tokens, width = rows[0].shape
    block = tokens // 2
    part = pl.BlockSpec((block, width), lambda i: (i, 0))
    out_shape = [jax.ShapeDtypeStruct((tokens, width), t) for t in outs]
    out_specs = [part] * len(outs)
    if sums:
        out_shape.append(jax.ShapeDtypeStruct((8, width), F32))
        out_specs.append(whole((8, width)))
    return call(
        kernel,
        grid=(tokens // block,),
        in_specs=[part] * len(rows) + [whole(vectors.shape)],
        out_specs=out_specs,
        out_shape=out_shape,
        cost_estimate=cost(flops=0, bytes_accessed=0, transcendentals=0),
        name=name,
    )(*rows, vectors)


def gelu_parts(u):
    c0 = math.sqrt(2.0 / math.pi)
    square = u * u
    t = jnp.tanh(u * (c0 + (c0 * 0.044715) * square))
    half = 0.5 * u
    act = half + half * t
    slope = 0.5 + 0.5 * t + half * (1.0 - t * t) * (c0 + (3.0 * c0 * 0.044715) * square)
    return act, slope


def up_kernel(rows, side, *refs):
    xa_ref, xb_ref, turned_ref, *raw, bias_ref, act_ref, slope_ref = refs[: -1 - len(GRAD_PARTS[side])]
    outs, w_ref = refs[-1 - len(GRAD_PARTS[side]) : -1], refs[-1]
    tokens = xa_ref.shape[0]
    put_together(rows, raw, w_ref)
    for half, ref in enumerate((xa_ref, xb_ref)):
        act, slope = gelu_parts(dot_nn(ref[...], w_ref[...]) + vector(bias_ref, UP_BIAS))
        act_ref[half * tokens : (half + 1) * tokens, :] = act.astype(BF16)
        slope_ref[half * tokens : (half + 1) * tokens, :] = slope.astype(BF16)
    store_parts(dot_nn(turned_ref[...], act_ref[...]), outs)


TILE = 256


def tiles(*dims):
    return pl.BlockSpec((*dims, TILE), lambda j: (0,) * len(dims) + (j,))


def raw_tiles(raw):
    return [tiles(*r.shape[:2]) for r in raw]


def up_and_down_grads(xa, xb, turned, raw, bias, rows, side):
    tokens, width = xa.shape
    c = bias.shape[1]
    hidden = jax.ShapeDtypeStruct((2 * tokens, c), BF16)
    grads = [jax.ShapeDtypeStruct((width // f, c), BF16) for f in GRAD_PARTS[side]]
    raw = side_pieces(raw, [side])
    act, slope, *grads = call(
        partial(up_kernel, rows, side),
        grid=(c // TILE,),
        in_specs=[whole(xa.shape), whole(xb.shape), whole(turned.shape)]
        + raw_tiles(raw)
        + [tiles(8)],
        out_specs=[tiles(2 * tokens)] * 2 + [tiles(g.shape[0]) for g in grads],
        out_shape=[hidden] * 2 + grads,
        scratch_shapes=[pltpu.VMEM((width, TILE), BF16)],
        cost_estimate=cost(
            flops=8 * tokens * width * c, bytes_accessed=0, transcendentals=2 * tokens * c
        ),
        name=f"up_and_down_grads_{side}",
    )(xa, xb, turned, *raw, bias)
    return act, slope, grads


def hidden_back_kernel(rows, side, *refs):
    ga_ref, gb_ref, *raw = refs[: 6 + 2 * side]
    down, up = raw[: len(raw) // 2], raw[len(raw) // 2 :]
    slope_ref, *before, pre_ref, sum_ref = refs[6 + 2 * side : 9 + 3 * side]
    *outs, acc_ref, w_ref, u_ref = refs[9 + 3 * side :]
    step = pl.program_id(0)
    tokens = ga_ref.shape[0]

    @pl.when(step == 0)
    def _():
        acc_ref[...] = before[0][...] if side else jnp.zeros_like(acc_ref)

    put_together(rows, down, w_ref)
    put_together(rows, up, u_ref)
    totals = 0.0
    for half, ref in enumerate((ga_ref, gb_ref)):
        at = slice(half * tokens, (half + 1) * tokens)
        back = dot_nn(ref[...], w_ref[...]) * slope_ref[at, :].astype(F32)
        pre = back.astype(BF16)
        pre_ref[at, :] = pre
        totals = totals + jnp.sum(pre.astype(F32), axis=0, keepdims=True)
        acc_ref[at, :] += dot_nt(pre, u_ref[...])
    sum_ref[0:1, :] = totals

    @pl.when(step == pl.num_programs(0) - 1)
    def _():
        if side:
            outs[0][...] = acc_ref[:tokens, :]
            outs[1][...] = acc_ref[tokens:, :].astype(BF16)
        else:
            outs[0][...] = acc_ref[...]


def hidden_back(ga, gb, down, up, slope, before, rows, side):
    tokens, width = ga.shape
    seq, c = slope.shape
    if side:
        backs = [jax.ShapeDtypeStruct(ga.shape, t) for t in (F32, BF16)]
    else:
        backs = [jax.ShapeDtypeStruct((seq, width), F32)]
    return call(
        partial(hidden_back_kernel, rows, side),
        grid=(c // TILE,),
        in_specs=[whole(ga.shape), whole(gb.shape)]
        + raw_tiles(down)
        + raw_tiles(up)
        + [tiles(seq)]
        + [whole(b.shape) for b in before],
        out_specs=[tiles(seq), tiles(8)] + [whole(b.shape) for b in backs],
        out_shape=[jax.ShapeDtypeStruct((seq, c), BF16), jax.ShapeDtypeStruct((8, c), F32)] + backs,
        scratch_shapes=[
            pltpu.VMEM((seq, width), F32),
            pltpu.VMEM((width, TILE), BF16),
            pltpu.VMEM((width, TILE), BF16),
        ],
        cost_estimate=cost(
            flops=8 * tokens * width * c, bytes_accessed=12 * tokens * c, transcendentals=0
        ),
        name=f"hidden_back_{side}",
    )(ga, gb, *down, *up, slope, *before)


def mlp_out_kernel(rows, *refs):
    act_ref, act_o_ref = refs[:2]
    down = refs[2:7]
    own_ref, other_ref, acc_ref, w_ref = refs[7:]
    step = pl.program_id(0)
    tokens = own_ref.shape[0]

    @pl.when(step == 0)
    def _():
        acc_ref[...] = jnp.zeros_like(acc_ref)

    put_together(rows, down[:2], w_ref.at[0])
    put_together(rows, down[2:], w_ref.at[1])
    acc_ref[...] += dot_nt(act_ref[...], w_ref[0]) + dot_nt(act_o_ref[...], w_ref[1])

    @pl.when(step == pl.num_programs(0) - 1)
    def _():
        own_ref[...] = acc_ref[:tokens, :]
        other_ref[...] = acc_ref[tokens:, :].astype(BF16)


def mlp_out(act, act_o, down, width, rows):
    seq, c = act.shape
    outs = [jax.ShapeDtypeStruct((seq // 2, width), t) for t in (F32, BF16)]
    return call(
        partial(mlp_out_kernel, rows),
        grid=(c // TILE,),
        in_specs=[tiles(seq)] * 2 + raw_tiles(down),
        out_specs=[whole(o.shape) for o in outs],
        out_shape=outs,
        scratch_shapes=[pltpu.VMEM((seq, width), F32), pltpu.VMEM((2, width, TILE), BF16)],
        cost_estimate=cost(
            flops=4 * seq * width * c, bytes_accessed=4 * seq * c, transcendentals=0
        ),
        name="mlp_out",
    )(act, act_o, *down)


def weight_grads_kernel(turned_ref, g_ref, go_ref, *outs):
    store_parts(dot_nn(turned_ref[...], g_ref[...]), outs[:2])
    store_parts(dot_nn(turned_ref[...], go_ref[...]), outs[2:])


def weight_grads(turned, grad, grad_o):
    width, seq = turned.shape
    c = grad.shape[1]
    return call(
        weight_grads_kernel,
        grid=(c // TILE,),
        in_specs=[whole(turned.shape), tiles(seq), tiles(seq)],
        out_specs=[tiles(s.shape[0]) for s in grad_shapes(width, c)],
        out_shape=grad_shapes(width, c),
        cost_estimate=cost(
            flops=4 * seq * width * c, bytes_accessed=6 * seq * c, transcendentals=0
        ),
        name="weight_grads",
    )(turned, grad, grad_o)


def make_local(rows):
    low, near = rows[-1], rows[:-1]
    fast = 2 ** len(rows) == BLOCKS
    order = rows if fast else None

    def to_blocks(parts):
        width, c = parts[0].shape[0] * 2, parts[0].shape[1]
        return [p.reshape(-1, width // BLOCKS, c) for p in parts]

    def reduce_plain(parts):
        blocks = to_blocks(parts)
        own = jnp.stack(blocks[:2], axis=1)
        other = jnp.stack([blocks[2], jnp.concatenate(blocks[3:])], axis=1)
        width, c = parts[0].shape[0] * 2, parts[0].shape[1]
        return scatter_rows(own.reshape(width, c), other.reshape(width, c), rows)

    def natural(grads):
        width, c = grads.shape
        blocks = grads.reshape(2, BLOCKS // 2, width // BLOCKS, c)
        return jnp.swapaxes(blocks, 0, 1).reshape(width, c)

    def local(
        layer_input,
        attn_gain,
        attn_shift,
        qkv_weight,
        qkv_bias,
        output_weight,
        output_bias,
        mlp_gain,
        mlp_shift,
        up_weight,
        up_bias,
        down_weight,
        down_bias,
        cotangent,
    ):
        tokens, width = layer_input.shape
        n, _, side = qkv_weight.shape
        hidden = up_weight.shape[1]
        d = HEAD_DIM

        attn_shard = jnp.concatenate([qkv_weight.reshape(n, -1), output_weight], axis=1)
        vectors = table_of(attn_gain, attn_shift, mlp_gain, mlp_shift, output_bias, down_bias)
        (attn_in,) = by_rows(norm_kernel, "norm", [layer_input], vectors, [BF16])
        attn_in_other = swap(attn_in, "core")
        cot_other = swap(cotangent, "core")
        bias_own = jnp.pad(qkv_bias, ((0, 6), (0, hidden - side)))
        bias_own = bias_own + jnp.pad(up_bias[None, :], ((UP_BIAS, 7 - UP_BIAS), (0, 0)))
        bias_other = swap(bias_own, "y")
        if fast:
            attn_near = gather_near(attn_shard, near)
            attn_near = after(attn_near, cot_other, bias_other)
            attn_stack = jnp.stack(attn_near)
            mlp_near = gather_near(jnp.stack([up_weight, down_weight]), near)
            attn_far = gather_far(attn_stack, low)
            attn_raw = gather_corners(attn_far, low)
        else:
            attn_raw, up_raw, down_raw = (
                gather_plain(w, rows) for w in (attn_shard, up_weight, down_weight)
            )
        halves = (attn_in, attn_in_other, cotangent, cot_other)
        if fast:
            halves = after(halves, attn_stack)
        attn_turned = turn(*halves[:2], order)
        cot_turned = turn(*halves[2:], order)
        attended = []
        for pair in range(3):
            bias = bias_own
            if fast and pair == 0:
                bias = after(bias, attn_far, attn_turned, cot_turned)
            if pair:
                bias = after(bias, attended[pair - 1][4])
            if fast and pair == 1:
                mlp_near = after(mlp_near, attended[0][4], attn_raw)
                up_far = gather_far(jnp.stack([m[0] for m in mlp_near]), low)
                down_stack = jnp.stack([m[1] for m in mlp_near])
                bias = after(bias, up_far[0], down_stack)
            attended.append(
                attend_forward(attn_in, attn_in_other, attn_raw, bias, bias_other, order, pair)
            )
        mixed = [a[4] for a in attended]
        weights = [a[3] for a in attended]
        if fast:
            mixed, up_far = after((mixed, up_far))
            up_raw = gather_corners(up_far, low)
        got = swap(project(mixed, weights, 1, 6 * d, BF16), "core")
        own = project(mixed, weights, 0, 6 * d, F32)
        hidden_resid, mlp_in, branch_sums = by_rows(
            resid_kernel,
            "resid",
            [layer_input, own, got],
            vectors,
            [F32, BF16],
            True,
        )
        mlp_in_other = swap(mlp_in, "core")
        if fast:
            down_far = gather_far(after(down_stack, mlp_in_other), low)
        ins = (mlp_in, mlp_in_other, cot_turned)
        grads = (cotangent, cot_other)
        act, slope, down_own = up_and_down_grads(*ins, up_raw, bias_own, order, 0)
        if fast:
            down_raw = gather_corners(after(down_far, act), low)
        pre, up_sums, back = hidden_back(*grads, down_raw[:2], up_raw[:2], slope, (), order, 0)
        bias_other = after(bias_other, pre)
        act_o, slope_o, down_other = up_and_down_grads(*ins, up_raw, bias_other, order, 1)
        down_parts = down_own + down_other
        if fast:
            down_parts = to_blocks(down_parts)
            down_got = reduce_corners(down_parts, low)
        else:
            down_grad = reduce_plain(down_parts)
        pre_o, up_sums_o, back, back_other = hidden_back(
            *grads, down_raw[2:], up_raw[2:], slope_o, (back,), order, 1
        )
        back_got = swap(back_other, "core")
        mlp_turned = turn(*after((mlp_in, mlp_in_other), pre_o), order)
        up_parts = weight_grads(mlp_turned, pre, pre_o)
        if fast:
            up_parts = to_blocks(up_parts)
            up_got = reduce_corners(up_parts, low)
        else:
            up_grad = reduce_plain(up_parts)
        hidden_grad, grad_attn, middle_sums = by_rows(
            middle_kernel,
            "middle",
            [hidden_resid, after(back, up_parts), back_got, cotangent],
            vectors,
            [F32, BF16],
            True,
        )
        grad_attn_other = swap(grad_attn, "core")
        if fast:
            down_sent = reduce_far(down_parts, after(down_got, grad_attn), low)

        half, block = width // 2, width // BLOCKS
        pair_grads, pair_sums, dprojs = {}, {}, {}
        for pair in (2, 1, 0):
            q, k, v, w, mix, lse = attended[pair]
            if pair != 2:
                lse = after(lse, pair_grads[pair + 1])
            if fast and pair == 1:
                lse, down_sent = after((lse, down_sent))
                total = down_parts[0].astype(F32) + sum(g.astype(F32) for g in down_sent)
                down_sum, down_got = total[:2], swap(total[2:].astype(BF16), near[0])
            if fast and pair == 0:
                to_low, to_y = far_sums(up_parts, after(up_got, pair_grads[1]))
                up_sent = (swap(to_low, low), swap(to_y, "y"))
                lse, large_got = after((lse, large_got), to_low, to_y)
                large_y = (pair_grads[2][0].astype(F32) + large_got.astype(F32)).astype(BF16)
                large_y = swap(large_y, "y")
            pair_grads[pair], dprojs[pair], pair_sums[pair] = attend_backward(
                q, k, v, w, grad_attn, grad_attn_other, attn_turned, mix, lse, order, pair
            )
            if fast and pair == 2:
                large_got = swap(pair_grads[2][1], low)

        dprojs = [dprojs[pair] for pair in range(3)]
        if fast:
            large_x = swap(pair_grads[0][1], low)
            small_got = swap(pair_grads[1][1], "y")
            up_sent, dprojs, down_got = after((up_sent, dprojs, down_got), pair_grads[0])
            down_sum = down_sum + down_got.astype(F32)
            total = up_parts[0].astype(F32) + sum(g.astype(F32) for g in up_sent)
            up_sum, up_got = total[:2], swap(total[2:].astype(BF16), near[0])
        act, act_o = after((act, act_o), pair_grads[0])
        branch, branch_other = mlp_out(act, act_o, down_raw, width, order)
        branch_got = swap(branch_other, "core")
        back_other = project(after(dprojs, branch), weights, 1, 0, BF16)
        got = swap(back_other, "core")
        dprojs = after(dprojs, back_other)
        if fast:
            dprojs, large_x = after((dprojs, large_x))
        own = project(dprojs, weights, 0, 0, F32)
        layer_output, result_sums = by_rows(
            result_kernel,
            "result",
            [hidden_resid, after(branch, own), branch_got],
            vectors,
            [BF16],
            True,
        )
        if fast:
            small = pair_grads[1][0].astype(F32) + after(small_got, own).astype(F32)
            small_x = swap(small[half:].astype(BF16), low)
            large_sent, small_sent = (large_x, large_y), small_x
            own, large_sent, small_sent, got = after(
                (own, large_sent, small_sent, got), layer_output
            )
        input_grad, last_sums = by_rows(
            last_kernel, "last", [layer_input, own, got, hidden_grad], vectors, [F32], True
        )
        if fast:
            up_got, last_sums = after((up_got, last_sums))
            down_sum = after(down_sum, last_sums)
            down_got = swap(down_sum[1].astype(BF16), near[1])
        if not fast:
            own, other = (
                natural(jnp.concatenate(p, axis=1))
                for p in (
                    (jnp.concatenate(pair_grads[0]), pair_grads[1][0]),
                    (jnp.concatenate(pair_grads[2]), pair_grads[1][1]),
                )
            )
            attn_grad = scatter_rows(own, other, rows)

        def bias_row(large, small, at):
            row = 0.0
            for i, kind in enumerate((0, 2)):
                source = 2 * d * kind
                for piece, to in (
                    (large[:1, source : source + 2 * d], 0),
                    (small[:1, source + at : source + at + d], 2 * d),
                ):
                    to = i * side + to
                    row = row + jnp.pad(piece, ((0, 0), (to, width - to - piece.shape[1])))
            return row
        common = jnp.concatenate(
            [middle_sums[:4], branch_sums[:1], result_sums[:2], last_sums[:2]], axis=0
        )
        common = common + swap(common, "core")
        own = jnp.concatenate([common, bias_row(pair_sums[0], pair_sums[1], 0), up_sums[:1]], axis=0)
        other = jnp.concatenate([common, bias_row(pair_sums[2], pair_sums[1], d), up_sums_o[:1]], axis=0)
        sums = own + swap(other, "y")
        if fast:
            large = pair_grads[0][0].astype(F32) + sum(g.astype(F32) for g in large_sent)
            small = small[:half] + small_sent.astype(F32)
            both = jnp.concatenate([large, small], axis=1).reshape(-1, block, 12 * d)
            attn_near = send_near(both, near)
            total = up_sum + up_got.astype(F32)
            up_grad = total[0] + swap(total[1].astype(BF16), near[1]).astype(F32)
            down_grad = down_sum[0] + down_got.astype(F32)
        for axis in reversed(rows[1:]):
            sums = sums + swap(sums, axis)
        entries = float(tokens * 2 ** (len(rows) + 2) * width)
        *vecs, qkv_bias_grad, rms_values = small_sums(sums, swap(sums, rows[0]), side, entries)
        if fast:
            qkv_grad, output_grad = attention_sum(attn_near[0], attn_near[1].values())
        else:
            qkv_grad, output_grad = attention_sum(attn_grad, ())
        return (
            layer_output,
            input_grad,
            vecs[0],
            vecs[1],
            qkv_grad,
            qkv_bias_grad,
            output_grad,
            vecs[2],
            vecs[3],
            vecs[4],
            up_grad,
            vecs[5],
            down_grad,
            vecs[6],
            rms_values[:, 0],
        )

    return local


def solution(mesh):
    row_size, col_size = mesh.shape["row"], mesh.shape["col"]
    bits = row_size.bit_length() - 1
    rows = tuple(f"r{b}" for b in reversed(range(bits)))
    cube = Mesh(mesh.devices.reshape((2,) * bits + (col_size // 2, 2)), rows + ("y", "core"))
    col = ("y", "core")
    every = rows + col
    placed = (
        P(every, None),
        P(),
        P(),
        P(rows, None, col),
        P(None, col),
        P(rows, col),
        P(),
        P(),
        P(),
        P(rows, col),
        P(col),
        P(rows, col),
        P(),
        P(every, None),
    )
    return jax.shard_map(
        make_local(rows),
        mesh=cube,
        in_specs=placed,
        out_specs=(
            P(every, None),
            P(every, None),
            P(),
            P(),
            P(rows, None, col),
            P(None, col),
            P(rows, col),
            P(),
            P(),
            P(),
            P(rows, col),
            P(col),
            P(rows, col),
            P(),
            P(),
        ),
        check_vma=False,
    )
```
